32 devices in a mesh: fsdp: 4 (over z), ctx: 4 (over x, core), tp: 2 (over y).
Axes of the slice: x: 2, y: 2, z: 4, core: 2. Of those that a mesh axis runs over, the one named last changes fastest.
Arguments:
- tokens: bfloat16 [4, 2048, 1536], P('fsdp', 'ctx'), may hold values from -25 to 25
- lengths: int32 [4], P('fsdp'), may hold values from 512 to 2048, as said below
- routes: int32 [4, 2048, 8], P('fsdp', 'ctx'), may hold values from 0 to 15, all different within a row
- visit_order: int32 [4, 4, 4096], P('fsdp', 'ctx'), may hold values from 0 to 4095, each once within a row
- cotangent: bfloat16 [4, 2048, 1536], P('fsdp', 'ctx'), may hold values from -6 to 6
- first_gain: bfloat16 [1536], P('fsdp'), may hold values from 0.099609375 to 1.8984375
- query_weight: bfloat16 [1536, 1536], P('fsdp', 'tp'), may hold values from -0.15625 to 0.15625
- key_matrix: bfloat16 [1536, 512], P('fsdp', 'tp'), may hold values from -0.15625 to 0.15625
- value_matrix: bfloat16 [1536, 512], P('fsdp', 'tp'), may hold values from -0.15625 to 0.15625
- output_weight: bfloat16 [1536, 1536], P('tp', 'fsdp'), may hold values from -3.5 to 3.5
- second_gain: bfloat16 [1536], P('fsdp'), may hold values from 0.099609375 to 1.8984375
- router_weight: bfloat16 [1536, 16], P('fsdp'), may hold values from -0.078125 to 0.078125
- gate_weight: bfloat16 [16, 1536, 512], P('fsdp', None, 'tp'), may hold values from -0.15625 to 0.15625
- up_weight: bfloat16 [16, 1536, 512], P('fsdp', None, 'tp'), may hold values from -0.15625 to 0.15625
- down_weight: bfloat16 [16, 512, 1536], P('fsdp', 'tp'), may hold values from -0.75 to 0.75
Outputs:
- layer_out: bfloat16 [4, 2048, 1536], P('fsdp', 'ctx')
- grad_tokens: float32 [4, 2048, 1536], P('fsdp', 'ctx')
- grad_first_gain: float32 [1536], P('fsdp')
- grad_query_weight: float32 [1536, 1536], P('fsdp', 'tp')
- grad_key_weight: float32 [1536, 512], P('fsdp', 'tp')
- grad_value_weight: float32 [1536, 512], P('fsdp', 'tp')
- grad_output_weight: float32 [1536, 1536], P('tp', 'fsdp')
- grad_second_gain: float32 [1536], P('fsdp')
- grad_router_weight: float32 [1536, 16], P('fsdp')
- grad_gate_weight: float32 [16, 1536, 512], P('fsdp', None, 'tp')
- grad_up_weight: float32 [16, 1536, 512], P('fsdp', None, 'tp')
- grad_down_weight: float32 [16, 512, 1536], P('fsdp', 'tp')
The draws below stay inside these ranges and needn't reach their ends.
Inputs may be any that keep to these rules, and one draw needn't show every extreme that they name: `lengths`: in every draw some sequence has length 2048. `routes`: the 8 experts of a token are different. `visit_order`: for each sequence and block, the entries are a permutation of the block's pair numbers.
All inputs are finite; a program needn't handle non-finite values.
Results may differ from the reference program's by a relative error of at most 0.028.
Values may be sent and summed in bfloat16 or wider, within the bound.
No kernel may reach another device: no remote copies, remote signals or barrier semaphores. Data moves between devices by JAX's collectives and lax.ppermute only.
A program may use at most 256 MiB of HBM per device.

```python
import math
import jax
import jax.numpy as jnp
from jax import lax

MODEL_WIDTH = 1536
QUERY_HEADS = 24
KEY_VALUE_HEADS = 8
HEAD_SIZE = 64
F = 512
TOPK = 8
E = 16
SCORE_BLOCK = 512
SEQ_DEV = 512
PADDED_LENGTH = 2048
SEQS = 4
CAP = 256
N_CTX = 4
N_TP = 2


def draw_tokens(key, part):
    first_key = jax.random.fold_in(key, 21)
    second_key = jax.random.fold_in(key, 22)
    third_key = jax.random.fold_in(key, 23)
    base_values = jnp.clip(jax.random.normal(first_key, (SEQS, PADDED_LENGTH, MODEL_WIDTH), jnp.float32), -4.0, 4.0)
    row_scale = jnp.exp(jax.random.uniform(second_key, (SEQS, PADDED_LENGTH, 1), jnp.float32, -0.9, 0.9))
    column_scale = jnp.exp(jax.random.uniform(third_key, (MODEL_WIDTH,), jnp.float32, -0.9, 0.9))
    return (base_values * row_scale * column_scale).astype(jnp.bfloat16)


def draw_lengths(key, part):
    spread = jax.random.randint(jax.random.fold_in(key, 11), (SEQS,), PADDED_LENGTH // 4, PADDED_LENGTH + 1)
    chosen = jax.random.randint(jax.random.fold_in(key, 12), (), 0, SEQS)
    return jnp.where(jnp.arange(SEQS) == chosen, PADDED_LENGTH, spread).astype(jnp.int32)


def block_levels(key, shape, split, smallest, top_value):
    level, own = 1.0, jax.random.fold_in(key, 6)
    for position, parts in split:
        draws = jnp.exp(jax.random.uniform(jax.random.fold_in(own, position), (parts,), jnp.float32, smallest / len(split), top_value / len(split)))
        level = level * jnp.repeat(draws, shape[position] // parts).reshape([-1 if axis == position else 1 for axis in range(len(shape))])
    return level


def distinct(stream_key, rows, number_of, top, lift):
    sequence = jax.random.permutation(jax.random.fold_in(stream_key, 1), number_of)
    boost = sequence
    for power in range(3):
        boost = boost * boost // number_of
    boost = boost * lift // number_of
    tickets = jax.random.randint(jax.random.fold_in(stream_key, 2), (rows, number_of), 0, 4096) + boost
    fixed_rows = jax.random.permutation(jax.random.fold_in(stream_key, 3), rows)[jnp.arange(number_of) % rows]
    tickets = jnp.where(jnp.arange(rows)[:, None] == fixed_rows[None, :], 1 << 14, tickets)
    score = tickets * number_of + jnp.arange(number_of)
    return lax.top_k(score.astype(jnp.int32), top)[1].astype(jnp.int32)


def noise(key, dims, scale, bound, pieces=(), held_as=jnp.bfloat16):
    entries = jax.random.normal(key, dims, jnp.float32) * scale
    if len(pieces) > 0:
        entries = block_levels(key, dims, pieces, -0.22, 0.18) * entries
    return jnp.clip(entries, min=-bound, max=bound).astype(held_as)


def setup_inputs(seed: int = 0) -> dict:
    splits = jax.random.split(jax.random.key(seed), 16)
    tokens = draw_tokens(jax.random.fold_in(splits[15], 71), 0)
    lengths = draw_lengths(jax.random.fold_in(splits[15], 71), 0)
    routes = distinct(splits[2], SEQS * PADDED_LENGTH, E, TOPK, 4096).reshape((SEQS, PADDED_LENGTH, TOPK))
    visit_order = jax.vmap(lambda own: jax.random.permutation(own, SEQ_DEV * TOPK))(jax.random.split(splits[3], SEQS * N_CTX)).reshape((SEQS, N_CTX, SEQ_DEV * TOPK)).astype(jnp.int32)
    cotangent = noise(splits[4], (SEQS, PADDED_LENGTH, MODEL_WIDTH), 1.0, 6.0, ((0, 4), (1, 4)))
    first_gain = jnp.clip(1.0 + 0.18 * jax.random.normal(splits[5], (MODEL_WIDTH,), jnp.float32), 0.099609375, 1.8984375).astype(jnp.bfloat16)
    query_weight = noise(splits[6], (MODEL_WIDTH, QUERY_HEADS * HEAD_SIZE), MODEL_WIDTH ** -0.5, 0.15625, ((0, 4), (1, 2)))
    key_matrix = noise(splits[7], (MODEL_WIDTH, KEY_VALUE_HEADS * HEAD_SIZE), MODEL_WIDTH ** -0.5, 0.15625, ((0, 4), (1, 2)))
    value_matrix = noise(splits[8], (MODEL_WIDTH, KEY_VALUE_HEADS * HEAD_SIZE), MODEL_WIDTH ** -0.5, 0.15625, ((0, 4), (1, 2)))
    output_weight = noise(splits[9], (QUERY_HEADS * HEAD_SIZE, MODEL_WIDTH), (max(QUERY_HEADS * HEAD_SIZE // 512, 1)) ** -0.5, 3.5, ((0, 2), (1, 4)))
    second_gain = jnp.clip(1.0 + 0.18 * jax.random.normal(splits[10], (MODEL_WIDTH,), jnp.float32), 0.099609375, 1.8984375).astype(jnp.bfloat16)
    router_weight = noise(splits[11], (MODEL_WIDTH, E), (4 * MODEL_WIDTH) ** -0.5, 0.078125, ((0, 4),))
    gate_weight = noise(splits[12], (E, MODEL_WIDTH, F), MODEL_WIDTH ** -0.5, 0.15625, ((0, 4), (2, 2)))
    up_weight = noise(splits[13], (E, MODEL_WIDTH, F), MODEL_WIDTH ** -0.5, 0.15625, ((0, 4), (2, 2)))
    down_weight = noise(splits[14], (E, F, MODEL_WIDTH), (max(F // 8, 1)) ** -0.5, 0.75, ((0, 4), (1, 2)))
    return dict(tokens=tokens, lengths=lengths, routes=routes, visit_order=visit_order, cotangent=cotangent, first_gain=first_gain, query_weight=query_weight, key_matrix=key_matrix, value_matrix=value_matrix, output_weight=output_weight, second_gain=second_gain, router_weight=router_weight, gate_weight=gate_weight, up_weight=up_weight, down_weight=down_weight)


EPSILON = 1e-06
PRECISE = lax.Precision.HIGHEST

@jax.custom_vjp
def low(v):
    return lax.optimization_barrier(v.astype(jnp.bfloat16)).astype(jnp.float32)

@jax.custom_vjp
def low_back(v):
    return v

def low_keep(v):
    return (low(v), None)

def low_pass(kept, grad):
    return (grad,)

def back_keep(v):
    return (v, None)

def back_low(kept, grad):
    return (low(grad),)
low.defvjp(low_keep, low_pass)
low_back.defvjp(back_keep, back_low)

def matmul(left, right):
    return jnp.dot(left, right, precision=PRECISE, preferred_element_type=jnp.float32)

def rms_normed(values):
    return values * lax.rsqrt(lax.optimization_barrier(jnp.mean(values * values, axis=-1, keepdims=True)) + EPSILON)

def rotation_tables(positions):
    half_dim = HEAD_SIZE // 2
    frequency = jnp.exp(jnp.arange(half_dim, dtype=jnp.float32) * (-2.0 * math.log(10000.0) / HEAD_SIZE))
    angles = positions.astype(jnp.float32)[:, None] * frequency[None, :]
    return (jnp.cos(angles)[:, None, :], jnp.sin(angles)[:, None, :])

def rotate(values, cosine_table, sine_table):
    row_count = values.shape[0]
    head_count = values.shape[1] // HEAD_SIZE
    shaped = values.reshape(row_count, head_count, HEAD_SIZE)
    first_half = shaped[:, :, :HEAD_SIZE // 2]
    second_half = shaped[:, :, HEAD_SIZE // 2:]
    joined = jnp.concatenate([first_half * cosine_table - second_half * sine_table, second_half * cosine_table + first_half * sine_table], axis=-1)
    return joined.reshape(row_count, head_count * HEAD_SIZE)

def plan_block(route_rows, ranked, live_rows):
    pair_count = route_rows.shape[0] * route_rows.shape[1]
    pair_expert = route_rows.reshape(-1)
    pair_live = jnp.repeat(live_rows, route_rows.shape[1])
    ranked_expert = pair_expert[ranked]
    ranked_live = pair_live[ranked]
    expert_hits = ((ranked_expert[:, None] == jnp.arange(E, dtype=jnp.int32)[None, :]) & ranked_live[:, None]).astype(jnp.int32)
    earlier = jnp.cumsum(expert_hits, axis=0) - expert_hits
    slot_place = lax.optimization_barrier(jnp.sum(earlier * expert_hits, axis=1))
    is_kept = ranked_live & (slot_place < CAP)
    slot_index = jnp.where(is_kept, ranked_expert * CAP + slot_place, E * CAP).astype(jnp.int32)
    slot_pair = jnp.full((E * CAP + 1,), pair_count, jnp.int32).at[slot_index].set(ranked.astype(jnp.int32))[:E * CAP]
    pair_slot = jnp.full((pair_count,), E * CAP, jnp.int32).at[ranked].set(slot_index)
    return (slot_pair, pair_slot)

def take_rows(table, index_rows):
    return table[index_rows]

def sequence_layer(weights, inputs, length, route_rows, slot_pair, pair_slot):
    first_gain, query_weight, key_matrix, value_matrix, output_weight, second_gain, router_weight, gate_weight, up_weight, down_weight = weights
    positions = jnp.arange(PADDED_LENGTH, dtype=jnp.int32)
    valid = (positions < length).astype(jnp.float32)[:, None]
    cosine_table, sine_table = rotation_tables(positions)
    hidden_one = low(rms_normed(inputs) * first_gain)
    query_rows = low(rotate(low_back(matmul(hidden_one, query_weight)), cosine_table, sine_table))
    rotated_keys = low(rotate(low_back(matmul(hidden_one, key_matrix)), cosine_table, sine_table))
    every_value = low(low_back(matmul(hidden_one, value_matrix)))
    heads_per_group = QUERY_HEADS // KEY_VALUE_HEADS
    query_block_list = query_rows.reshape(PADDED_LENGTH // SCORE_BLOCK, SCORE_BLOCK, KEY_VALUE_HEADS, heads_per_group, HEAD_SIZE)
    key_head_rows = rotated_keys.reshape(PADDED_LENGTH, KEY_VALUE_HEADS, HEAD_SIZE)
    value_head_rows = every_value.reshape(PADDED_LENGTH, KEY_VALUE_HEADS, HEAD_SIZE)
    score_scale = HEAD_SIZE ** (-0.5)

    def attend_block(item):
        block_index, query_block = item
        query_pos = block_index * SCORE_BLOCK + jnp.arange(SCORE_BLOCK, dtype=jnp.int32)
        scores = low_back(jnp.einsum('qhgd,khd->hgqk', query_block, key_head_rows, precision=PRECISE, preferred_element_type=jnp.float32) * score_scale)
        allowed = (positions[None, :] <= query_pos[:, None]) & (positions[None, :] < length)
        probs = jax.nn.softmax(jnp.where(allowed, scores, -jnp.inf), axis=-1)
        return jnp.einsum('hgqk,khd->qhgd', low(probs), value_head_rows, precision=PRECISE, preferred_element_type=jnp.float32)
    attended = lax.map(jax.checkpoint(attend_block), (jnp.arange(PADDED_LENGTH // SCORE_BLOCK, dtype=jnp.int32), query_block_list))
    attended = low(low_back(attended.reshape(PADDED_LENGTH, QUERY_HEADS * HEAD_SIZE)))
    residual = inputs + low_back(matmul(attended, output_weight))
    hidden_two = low(rms_normed(residual) * second_gain)
    logits = low_back(matmul(hidden_two, router_weight))
    route_onehot = (route_rows[:, :, None] == jnp.arange(E, dtype=jnp.int32)[None, None, :]).astype(jnp.float32)
    gate_weights = jax.nn.softmax(lax.optimization_barrier(jnp.sum(route_onehot * logits[:, None, :], axis=-1)), axis=-1)
    slot_token = slot_pair // TOPK
    hidden_blocks = hidden_two.reshape(N_CTX, SEQ_DEV, MODEL_WIDTH)
    hidden_pad = jnp.concatenate([hidden_blocks, jnp.zeros((N_CTX, 1, MODEL_WIDTH), jnp.float32)], axis=1)
    dispatched = jax.vmap(take_rows)(hidden_pad, slot_token).reshape(N_CTX, E, CAP, MODEL_WIDTH)
    group_width = F // N_TP
    mixture = jnp.zeros((PADDED_LENGTH, MODEL_WIDTH), jnp.float32)
    for group_index in range(N_TP):
        low_col = group_index * group_width
        expert_in = low_back(dispatched)
        gate_pre = low_back(jnp.einsum('becd,edf->becf', expert_in, gate_weight[:, :, low_col:low_col + group_width], precision=PRECISE, preferred_element_type=jnp.float32))
        up_pre = low_back(jnp.einsum('becd,edf->becf', expert_in, up_weight[:, :, low_col:low_col + group_width], precision=PRECISE, preferred_element_type=jnp.float32))
        hidden_mid = low(jax.nn.silu(gate_pre) * up_pre)
        produced = low(low_back(jnp.einsum('becf,efd->becd', hidden_mid, down_weight[:, low_col:low_col + group_width, :], precision=PRECISE, preferred_element_type=jnp.float32)))
        produced_pad = jnp.concatenate([produced.reshape(N_CTX, E * CAP, MODEL_WIDTH), jnp.zeros((N_CTX, 1, MODEL_WIDTH), jnp.float32)], axis=1)
        pair_out = jax.vmap(take_rows)(produced_pad, pair_slot).reshape(PADDED_LENGTH, TOPK, MODEL_WIDTH)
        mixture = mixture + lax.optimization_barrier(jnp.sum(gate_weights[:, :, None] * pair_out, axis=1))
    return valid * (residual + mixture)

def reference(tokens, lengths, routes, visit_order, cotangent, first_gain, query_weight, key_matrix, value_matrix, output_weight, second_gain, router_weight, gate_weight, up_weight, down_weight):
    live_all = jnp.arange(PADDED_LENGTH, dtype=jnp.int32)[None, :] < lengths[:, None]
    route_blocks = routes.reshape(SEQS, N_CTX, SEQ_DEV, TOPK)
    live_blocks = live_all.reshape(SEQS, N_CTX, SEQ_DEV)
    slot_pair, pair_slot = jax.vmap(jax.vmap(plan_block))(route_blocks, visit_order, live_blocks)
    weights = (first_gain.astype(jnp.float32), query_weight.astype(jnp.float32), key_matrix.astype(jnp.float32), value_matrix.astype(jnp.float32), output_weight.astype(jnp.float32), second_gain.astype(jnp.float32), router_weight.astype(jnp.float32), gate_weight.astype(jnp.float32), up_weight.astype(jnp.float32), down_weight.astype(jnp.float32))

    def forward(all_inputs, weight_set):

        def one_sequence(item):
            inputs, length, route_rows, slot_rows, pair_rows = item
            return sequence_layer(weight_set, inputs, length, route_rows, slot_rows, pair_rows)
        return lax.map(jax.checkpoint(one_sequence), (all_inputs, lengths, routes, slot_pair, pair_slot))
    layer_out, pullback = jax.vjp(forward, tokens.astype(jnp.float32), weights)
    grad_inputs, grad_weights = pullback(cotangent.astype(jnp.float32))
    return (layer_out.astype(jnp.bfloat16), grad_inputs, grad_weights[0], grad_weights[1], grad_weights[2], grad_weights[3], grad_weights[4], grad_weights[5], grad_weights[6], grad_weights[7], grad_weights[8], grad_weights[9])
```

```python
import functools
import math

import jax
import jax.numpy as jnp
from jax import lax
from jax.experimental import pallas as pl
from jax.experimental.pallas import tpu as pltpu
from jax.sharding import Mesh
from jax.sharding import PartitionSpec as P

HEAD = 64
TOPK = 8
E = 16
CAP = 256
EPSILON = 1e-06
BF = jnp.bfloat16
F32 = jnp.float32
NEG = -1e30
FAR = 1e6


def dot(a, b, ca, cb):
    return lax.dot_general(a, b, (((ca,), (cb,)), ((), ())), preferred_element_type=F32)


def shift(v, axis, n, by=1):
    return lax.ppermute(v, axis, [(i, (i + by) % n) for i in range(n)])


def swap(v, axis):
    return lax.ppermute(v, axis, [(0, 1), (1, 0)])


def pick(v, index, parts, dim):
    size = v.shape[dim] // parts
    return lax.dynamic_slice_in_dim(v, index * size, size, dim)


def put(buffer, v, start, dim):
    return lax.dynamic_update_slice_in_dim(buffer, v, start, dim)


def ring_reduce(part, axis, n):
    me = lax.axis_index(axis)
    moving = part((me + n - 1) % n).astype(BF)
    for s in range(2, n):
        moving = (shift(moving, axis, n).astype(F32) + part((me + n - s) % n)).astype(BF)
    return shift(moving, axis, n).astype(F32) + part(me)


def core_halves(v, dim):
    core = lax.axis_index("core")
    mine = pick(v, core, 2, dim)
    theirs = pick(v, 1 - core, 2, dim)
    return mine.astype(F32) + swap(theirs.astype(BF), "core").astype(F32)


def core_join(v, dim):
    other = swap(v, "core")
    first = lax.axis_index("core") == 0
    return jnp.concatenate([jnp.where(first, v, other), jnp.where(first, other, v)], axis=dim)


def ring_gather(v, axis, n, dim):
    me = lax.axis_index(axis)
    size = v.shape[dim]
    shape = list(v.shape)
    shape[dim] = size * n
    out = put(jnp.zeros(shape, v.dtype), v, me * size, dim)
    moving = v
    for s in range(1, n):
        moving = shift(moving, axis, n)
        out = put(out, moving, ((me + n - s) % n) * size, dim)
    return out


def ctx_total(v, n_cx):
    half = core_halves(v, 0).astype(BF)
    part = ring_reduce(lambda j: pick(half, j, n_cx, 0).astype(F32), "cx", n_cx).astype(BF)
    return core_join(ring_gather(part, "cx", n_cx, 0), 0)


def normalize(values):
    inverse = lax.rsqrt(jnp.mean(values * values, axis=-1, keepdims=True) + EPSILON)
    return inverse, values * inverse


def norm_backward(grad, gain, inverse, normed):
    scaled = grad * gain
    return inverse * (scaled - normed * jnp.mean(scaled * normed, axis=-1, keepdims=True))


def rotate(v, cos, sin, inverse):
    rows = v.shape[1]
    shaped = v.reshape(-1, 2, HEAD // 2, rows)
    a, b = shaped[:, 0], shaped[:, 1]
    if inverse:
        out = jnp.stack([a * cos + b * sin, b * cos - a * sin], axis=1)
    else:
        out = jnp.stack([a * cos - b * sin, b * cos + a * sin], axis=1)
    return out.reshape(-1, rows)


def keep_plan(routes, order, live):
    rows = routes.shape[0]
    pairs = rows * TOPK
    token, choice = order // TOPK, order % TOPK
    rank = jnp.arange(pairs, dtype=jnp.int32)
    at_token = (jnp.arange(rows, dtype=jnp.int32)[:, None] == token[None, :]).astype(BF)
    at_choice = jnp.arange(TOPK, dtype=jnp.int32)[:, None] == choice[None, :]
    high = jnp.where(at_choice, (rank // 64)[None, :], 0).astype(BF)
    low = jnp.where(at_choice, (rank % 64)[None, :], 0).astype(BF)
    place = dot(jnp.concatenate([high, low], axis=0), at_token, 1, 1)
    place = place[:TOPK] * 64.0 + place[TOPK:]
    routes_t = routes.T
    hits = routes_t[:, None, :] == jnp.arange(E, dtype=jnp.int32)[None, :, None]
    routed = jnp.any(hits, axis=0)
    place_e = jnp.sum(jnp.where(hits, place[:, None, :], 0.0), axis=0)
    place_e = jnp.where(routed & live[None, :], place_e, FAR)
    earlier = jnp.sum(
        (place_e.T[:, :, None] < place_e[None, :, :]).astype(F32), axis=0
    )
    kept = routed & live[None, :] & (earlier < CAP)
    return routed, kept


def softmax_block(q, k, last, base, first_row, length):
    s = lax.dot_general(k, q, (((0,), (0,)), ((), ())), preferred_element_type=F32)
    if last:
        key = base + lax.broadcasted_iota(jnp.int32, s.shape, 0)
        query = first_row + lax.broadcasted_iota(jnp.int32, s.shape, 1)
        s = jnp.where((key <= query) & (key < length), s, NEG)
    return s


def attend_kernel(group, info_ref, q_ref, kv_ref, o_ref, lse_ref):
    count, first_row, length = info_ref[0], info_ref[1], info_ref[2]
    rows = q_ref.shape[1]
    keys = kv_ref.shape[3]
    for h in range(group):
        q = q_ref[h * HEAD : (h + 1) * HEAD, :]

        def step(j, carry, last):
            top, total, acc = carry
            k = kv_ref[j, 0]
            v = kv_ref[j, 1]
            s = softmax_block(q, k, last, j * keys, first_row, length)
            new_top = jnp.maximum(top, jnp.max(s, axis=0, keepdims=True))
            p = jnp.exp(s - new_top)
            fade = jnp.exp(top - new_top)
            total = total * fade + jnp.sum(p, axis=0, keepdims=True)
            acc = acc * fade + jnp.dot(v, p.astype(BF), preferred_element_type=F32)
            return new_top, total, acc

        carry = (
            jnp.full((1, rows), NEG, F32),
            jnp.zeros((1, rows), F32),
            jnp.zeros((HEAD, rows), F32),
        )
        carry = lax.fori_loop(0, count - 1, functools.partial(step, last=False), carry)
        top, total, acc = step(count - 1, carry, True)
        o_ref[h * HEAD : (h + 1) * HEAD, :] = (acc / total).astype(BF)
        lse_ref[0, h : h + 1, :] = top + jnp.log(total)


def attend(q, kv, info, group):
    rows = q.shape[1]
    n_ctx, _, depth, keys = kv.shape
    heads = depth // HEAD
    return pl.pallas_call(
        functools.partial(attend_kernel, group),
        name="attend",
        grid_spec=pltpu.PrefetchScalarGridSpec(
            num_scalar_prefetch=1,
            grid=(heads,),
            in_specs=[
                pl.BlockSpec((group * HEAD, rows), lambda g, i: (g, 0)),
                pl.BlockSpec((n_ctx, 2, HEAD, keys), lambda g, i: (0, 0, g, 0)),
            ],
            out_specs=[
                pl.BlockSpec((group * HEAD, rows), lambda g, i: (g, 0)),
                pl.BlockSpec((1, 8, rows), lambda g, i: (g, 0, 0)),
            ],
        ),
        out_shape=[
            jax.ShapeDtypeStruct(q.shape, BF),
            jax.ShapeDtypeStruct((heads, 8, rows), F32),
        ],
        compiler_params=pltpu.CompilerParams(vmem_limit_bytes=48 << 20),
        cost_estimate=pl.CostEstimate(
            flops=4 * q.shape[0] * rows * n_ctx * keys,
            transcendentals=q.shape[0] // HEAD * rows * n_ctx * keys,
            bytes_accessed=4 * q.size + 2 * kv.size,
        ),
    )(info, q, kv)


def attend_back_kernel(group, info_ref, q_ref, kv_ref, o_ref, do_ref, lse_ref, dq_ref, dkv_ref):
    count, first_row, length = info_ref[0], info_ref[1], info_ref[2]
    n_ctx = kv_ref.shape[0]
    keys = kv_ref.shape[3]
    delta = []
    for h in range(group):
        part = slice(h * HEAD, (h + 1) * HEAD)
        delta.append(
            jnp.sum(do_ref[part, :].astype(F32) * o_ref[part, :].astype(F32), axis=0, keepdims=True)
        )
    dq_ref[...] = jnp.zeros_like(dq_ref)

    def step(j, last):
        k = kv_ref[j, 0]
        v = kv_ref[j, 1]
        dk = jnp.zeros((keys, HEAD), F32)
        dv = jnp.zeros((keys, HEAD), F32)
        for h in range(group):
            part = slice(h * HEAD, (h + 1) * HEAD)
            q = q_ref[part, :]
            do = do_ref[part, :]
            s = softmax_block(q, k, last, j * keys, first_row, length)
            p = jnp.exp(s - lse_ref[0, h : h + 1, :])
            dp = lax.dot_general(v, do, (((0,), (0,)), ((), ())), preferred_element_type=F32)
            ds = (p * (dp - delta[h])).astype(BF)
            pb = p.astype(BF)
            dv += lax.dot_general(pb, do, (((1,), (1,)), ((), ())), preferred_element_type=F32)
            dk += lax.dot_general(ds, q, (((1,), (1,)), ((), ())), preferred_element_type=F32)
            dq_ref[part, :] += jnp.dot(k, ds, preferred_element_type=F32)
        dkv_ref[j, 0] = dk.T.astype(BF)
        dkv_ref[j, 1] = dv.T.astype(BF)

    @pl.loop(0, count - 1)
    def _(j):
        step(j, False)

    step(count - 1, True)

    @pl.loop(count, n_ctx)
    def _(j):
        dkv_ref[j] = jnp.zeros(dkv_ref.shape[1:], BF)


def attend_back(q, kv, o, do, lse, info, group):
    rows = q.shape[1]
    n_ctx, _, depth, keys = kv.shape
    heads = depth // HEAD
    wide = pl.BlockSpec((group * HEAD, rows), lambda g, i: (g, 0))
    blocks = pl.BlockSpec((n_ctx, 2, HEAD, keys), lambda g, i: (0, 0, g, 0))
    return pl.pallas_call(
        functools.partial(attend_back_kernel, group),
        name="attend_back",
        grid_spec=pltpu.PrefetchScalarGridSpec(
            num_scalar_prefetch=1,
            grid=(heads,),
            in_specs=[
                wide,
                blocks,
                wide,
                wide,
                pl.BlockSpec((1, 8, rows), lambda g, i: (g, 0, 0)),
            ],
            out_specs=[wide, blocks],
        ),
        out_shape=[
            jax.ShapeDtypeStruct(q.shape, F32),
            jax.ShapeDtypeStruct(kv.shape, BF),
        ],
        compiler_params=pltpu.CompilerParams(vmem_limit_bytes=48 << 20),
        cost_estimate=pl.CostEstimate(
            flops=10 * q.shape[0] * rows * n_ctx * keys,
            transcendentals=q.shape[0] // HEAD * rows * n_ctx * keys,
            bytes_accessed=10 * q.size + 4 * kv.size,
        ),
    )(info, q, kv, o, do, lse)


def local(
    sizes,
    tokens,
    lengths,
    routes,
    visit_order,
    cotangent,
    first_gain,
    query_weight,
    key_matrix,
    value_matrix,
    output_weight,
    second_gain,
    router_weight,
    gate_weight,
    up_weight,
    down_weight,
):
    n_z, n_cx = sizes
    n_ctx = 2 * n_cx
    z = lax.axis_index("fsdp")
    cx = lax.axis_index("cx")
    core = lax.axis_index("core")
    tp = lax.axis_index("tp")
    ctx = cx * 2 + core
    rows, width = tokens.shape[1:]
    half = rows // 2
    shard = query_weight.shape[0]
    q_width = query_weight.shape[1]
    kv_width = key_matrix.shape[1]
    group = q_width // kv_width
    held = gate_weight.shape[0]
    hidden = gate_weight.shape[2]
    first_row = ctx * rows
    length = lengths[0]
    positions = first_row + jnp.arange(rows, dtype=jnp.int32)
    live = positions < length
    valid = live.astype(F32)[:, None]

    small = jnp.concatenate(
        [first_gain[None], second_gain[None], router_weight.T], axis=0
    )
    small_full = put(jnp.zeros((2 + E, width), BF), small, z * shard, 1)
    for s in range(1, n_z):
        small_full = put(small_full, shift(small, "fsdp", n_z, s), ((z + n_z - s) % n_z) * shard, 1)
    gain_first = small_full[0:1].astype(F32)
    gain_second = small_full[1:2].astype(F32)
    router = small_full[2:]

    w_mine = jnp.concatenate([query_weight, key_matrix, value_matrix], axis=1)
    w_full = put(jnp.zeros((width, w_mine.shape[1]), BF), w_mine, z * shard, 0)
    moving = pick(w_mine, core, 2, 0)
    piece = shard // 2
    for s in range(1, n_z):
        moving = shift(moving, "fsdp", n_z)
        start = ((z + n_z - s) % n_z) * shard
        w_full = put(w_full, moving, start + core * piece, 0)
        w_full = put(w_full, swap(moving, "core"), start + (1 - core) * piece, 0)

    grad_out = (cotangent[0].astype(F32) * valid).astype(BF)
    grad_half = pick(grad_out, tp, 2, 0)
    grad_chunks = []
    moving = grad_half
    for s in range(n_z):
        if s:
            moving = shift(moving, "fsdp", n_z)
        grad_chunks.append(jnp.concatenate([moving, swap(moving, "tp")], axis=0))

    o_full = put(jnp.zeros((q_width, width), BF), output_weight, z * shard, 1)
    moving = pick(output_weight, core, 2, 0)
    o_piece = q_width // 2
    for s in range(1, n_z):
        moving = shift(moving, "fsdp", n_z)
        start = ((z + n_z - s) % n_z) * shard
        both = lax.dynamic_update_slice(o_full, moving, (core * o_piece, start))
        o_full = lax.dynamic_update_slice(both, swap(moving, "core"), ((1 - core) * o_piece, start))

    routed, kept = keep_plan(routes[0], visit_order[0, 0], live)

    inputs = tokens[0].astype(F32)
    inverse_one, normed_one = normalize(inputs)
    hidden_one = (normed_one * gain_first).astype(BF)
    frequency = jnp.exp(
        jnp.arange(HEAD // 2, dtype=F32) * (-2.0 * math.log(10000.0) / HEAD)
    )
    angles = frequency[:, None] * positions.astype(F32)[None, :]
    cos, sin = jnp.cos(angles), jnp.sin(angles)
    projected = dot(w_full, hidden_one, 0, 1)
    scale = HEAD**-0.5
    query = (rotate(projected[:q_width], cos, sin, False).astype(BF) * scale).astype(BF)
    key = rotate(projected[q_width : q_width + kv_width], cos, sin, False).astype(BF)
    value = projected[q_width + kv_width :].astype(BF)
    kv_mine = jnp.stack([key, value])[None]
    kv = jnp.zeros((n_ctx,) + kv_mine.shape[1:], BF)
    moving = kv_mine
    for s in range(n_cx):
        if s:
            moving = shift(moving, "cx", n_cx)
        source = ((cx + n_cx - s) % n_cx) * 2
        kv = put(kv, moving, source + core, 0)
        kv = put(kv, swap(moving, "core"), source + 1 - core, 0)
    count = jnp.minimum(ctx + 1, (length + rows - 1) // rows)
    info = jnp.stack([count, first_row, length])
    attended, lse = attend(query, kv, info, group)

    far = dot(pick(attended, 1 - tp, 2, 1), o_full, 0, 0).astype(BF)
    near = dot(pick(attended, tp, 2, 1), o_full, 0, 0)
    residual = pick(tokens[0], tp, 2, 0).astype(F32) + near + swap(far, "tp").astype(F32)
    inverse_two, normed_two = normalize(residual)
    hidden_two = (normed_two * gain_second).astype(BF)
    logits = dot(router, hidden_two, 1, 1)
    routed_half = pick(routed, tp, 2, 1)
    kept_half = pick(kept, tp, 2, 1).astype(F32)
    masked = jnp.where(routed_half, logits, NEG)
    raised = jnp.where(
        routed_half, jnp.exp(masked - jnp.max(masked, axis=0, keepdims=True)), 0.0
    )
    gates = raised / jnp.sum(raised, axis=0, keepdims=True)
    weights = gates * kept_half

    gate_up = jnp.concatenate(
        [gate_weight[e] for e in range(held)] + [up_weight[e] for e in range(held)], axis=1
    )
    down = down_weight.reshape(held * hidden, width)
    mid = held * hidden
    h2_chunks, acts, grads, mix_parts, back_parts, gate_parts = [], [], [], [], [], []
    moving, moving_w = hidden_two, weights
    for s in range(n_z):
        if s:
            moving = shift(moving, "fsdp", n_z)
            moving_w = shift(moving_w, "fsdp", n_z)
        block = jnp.concatenate([moving, swap(moving, "tp")], axis=0)
        block_w = jnp.concatenate([moving_w, swap(moving_w, "tp")], axis=1)
        mine_w = lax.dynamic_slice_in_dim(block_w, z * held, held, 0).T
        spread = jnp.broadcast_to(mine_w[:, :, None], (rows, held, hidden)).reshape(rows, mid)
        both = dot(block, gate_up, 1, 0)
        g, u = both[:, :mid], both[:, mid:]
        sig = jax.nn.sigmoid(g)
        silu = g * sig
        act = silu * u
        weighted = (act * spread).astype(BF)
        mix_parts.append(dot(weighted, down, 1, 0).astype(BF))
        dact = dot(grad_chunks[s], down, 1, 1)
        gate_grad = jnp.sum((act * dact).reshape(rows, held, hidden), axis=-1).T
        gate_parts.append(put(jnp.zeros((E, rows), F32), gate_grad, z * held, 0))
        dhid = dact * spread
        dg = (dhid * u * sig * (1.0 + g * (1.0 - sig))).astype(BF)
        du = (dhid * silu).astype(BF)
        dgu = jnp.concatenate([dg, du], axis=1)
        back_parts.append(dot(dgu, gate_up, 1, 1).astype(BF))
        h2_chunks.append(block)
        acts.append(weighted)
        grads.append(dgu)

    def home(parts, dim):
        halves = []
        for part in parts:
            size = part.shape[dim] // 2
            mine = lax.slice_in_dim(part, 0, size, axis=dim).astype(F32)
            theirs = lax.slice_in_dim(part, size, 2 * size, axis=dim)
            halves.append(mine + swap(theirs, "tp").astype(F32))
        moving = halves[1].astype(part.dtype)
        for s in range(2, n_z):
            moving = (shift(moving, "fsdp", n_z).astype(F32) + halves[s]).astype(part.dtype)
        return shift(moving, "fsdp", n_z).astype(F32) + halves[0]

    hidden_grad = home(back_parts, 0)
    gate_grad = home(gate_parts, 1) * kept_half
    mixture = home(mix_parts, 0)

    h2_all = jnp.concatenate(h2_chunks, axis=0)
    grad_gate_up = dot(h2_all, jnp.concatenate(grads, axis=0), 0, 0).astype(BF)
    grad_down = dot(
        jnp.concatenate(acts, axis=0), jnp.concatenate(grad_chunks, axis=0), 0, 0
    ).astype(BF)
    grad_gate_up = ctx_total(grad_gate_up, n_cx)
    grad_down = ctx_total(grad_down, n_cx)

    valid_half = pick(valid, tp, 2, 0)
    out_half = (valid_half * (residual + mixture)).astype(BF)
    out_other = swap(out_half, "tp")
    lead = tp == 0
    layer_out = jnp.concatenate(
        [jnp.where(lead, out_half, out_other), jnp.where(lead, out_other, out_half)], axis=0
    )

    logit_grad = (
        gates * (gate_grad - jnp.sum(gates * gate_grad, axis=0, keepdims=True))
    ).astype(BF)
    hidden_grad = hidden_grad + dot(logit_grad, router, 0, 0)
    grad_router = dot(logit_grad, hidden_two, 1, 0)
    grad_second = jnp.sum(hidden_grad * normed_two, axis=0, keepdims=True)
    branch_half = (
        grad_half.astype(F32) + norm_backward(hidden_grad, gain_second, inverse_two, normed_two)
    ).astype(BF)
    branch_other = swap(branch_half, "tp")
    branch = jnp.concatenate(
        [jnp.where(lead, branch_half, branch_other), jnp.where(lead, branch_other, branch_half)],
        axis=0,
    )

    attended_grad = dot(o_full, branch, 1, 1).astype(BF)
    grad_query_rot, grad_kv = attend_back(
        query, kv, attended, attended_grad, lse, info, group
    )
    grad_output = dot(attended, branch, 1, 0).astype(BF)
    by_core = grad_kv.reshape((n_cx, 2) + grad_kv.shape[1:])
    kv_sum = (
        lax.dynamic_index_in_dim(by_core, core, 1, False).astype(F32)
        + swap(lax.dynamic_index_in_dim(by_core, 1 - core, 1, False), "core").astype(F32)
    ).astype(BF)
    kv_grad = ring_reduce(
        lambda j: lax.dynamic_index_in_dim(kv_sum, j, 0, False).astype(F32), "cx", n_cx
    )
    query_grad = (rotate(grad_query_rot, cos, sin, True) * scale).astype(BF)
    key_grad = rotate(kv_grad[0], cos, sin, True).astype(BF)
    value_grad = kv_grad[1].astype(BF)
    grad_all = jnp.concatenate([query_grad, key_grad, value_grad], axis=0)
    first_part = dot(grad_all, w_full, 0, 1)
    grad_first = jnp.sum(first_part * normed_one, axis=0, keepdims=True)
    first_low = first_part.astype(BF)
    first_grad = first_low.astype(F32) + swap(first_low, "tp").astype(F32)
    grad_inputs = branch.astype(F32) + norm_backward(
        first_grad, gain_first, inverse_one, normed_one
    )
    grad_w = dot(hidden_one, grad_all, 0, 1).astype(BF)

    def owner_rows(v):
        blocks = v.reshape(n_z, v.shape[0] // n_z, v.shape[1])
        mine = core_halves(blocks, 1).astype(BF)
        mine = ring_reduce(lambda j: pick(mine, j, n_cx, 1).astype(F32), "cx", n_cx).astype(BF)
        mine = ring_reduce(
            lambda j: lax.dynamic_index_in_dim(mine, j, 0, False).astype(F32), "fsdp", n_z
        ).astype(BF)
        return core_join(ring_gather(mine, "cx", n_cx, 0), 0)

    def owner_columns(v):
        mine = core_halves(v, 0).astype(BF)
        mine = ring_reduce(lambda j: pick(mine, j, n_cx, 0).astype(F32), "cx", n_cx).astype(BF)
        mine = ring_reduce(lambda j: pick(mine, j, n_z, 1).astype(F32), "fsdp", n_z).astype(BF)
        return core_join(ring_gather(mine, "cx", n_cx, 0), 0)

    grad_w = owner_rows(grad_w).astype(F32)
    grad_output = owner_columns(grad_output).astype(F32)

    small_grad = jnp.concatenate([grad_first, grad_second, grad_router], axis=0)
    small_grad = small_grad + swap(small_grad, "tp")
    small_grad = small_grad + swap(small_grad, "core")
    total = small_grad
    moving = small_grad
    for s in range(1, n_cx):
        moving = shift(moving, "cx", n_cx)
        total = total + moving
    me = z
    moving = pick(total, (me + n_z - 1) % n_z, n_z, 1)
    for s in range(2, n_z):
        moving = shift(moving, "fsdp", n_z) + pick(total, (me + n_z - s) % n_z, n_z, 1)
    small_mine = shift(moving, "fsdp", n_z) + pick(total, me, n_z, 1)

    def experts_of(v):
        return jnp.stack(
            [v[:, e * hidden : (e + 1) * hidden] for e in range(held)]
        ).astype(F32)

    return (
        layer_out[None],
        grad_inputs[None],
        small_mine[0],
        grad_w[:, :q_width],
        grad_w[:, q_width : q_width + kv_width],
        grad_w[:, q_width + kv_width :],
        grad_output,
        small_mine[1],
        small_mine[2:].T,
        experts_of(grad_gate_up[:, :mid]),
        experts_of(grad_gate_up[:, mid:]),
        grad_down.reshape(held, hidden, width).astype(F32),
    )


def solution(mesh):
    n_z, n_ctx, n_tp = mesh.shape["fsdp"], mesh.shape["ctx"], mesh.shape["tp"]
    named = Mesh(
        mesh.devices.reshape(n_z, n_ctx // 2, 2, n_tp), ("fsdp", "cx", "core", "tp")
    )
    ctx = ("cx", "core")
    placed = (
        P("fsdp", ctx, None),
        P("fsdp"),
        P("fsdp", ctx, None),
        P("fsdp", ctx, None),
        P("fsdp", ctx, None),
        P("fsdp"),
        P("fsdp", "tp"),
        P("fsdp", "tp"),
        P("fsdp", "tp"),
        P("tp", "fsdp"),
        P("fsdp"),
        P("fsdp", None),
        P("fsdp", None, "tp"),
        P("fsdp", None, "tp"),
        P("fsdp", "tp", None),
    )
    return jax.shard_map(
        functools.partial(local, (n_z, n_ctx // 2)),
        mesh=named,
        in_specs=placed,
        out_specs=(
            P("fsdp", ctx, None),
            P("fsdp", ctx, None),
            P("fsdp"),
            P("fsdp", "tp"),
            P("fsdp", "tp"),
            P("fsdp", "tp"),
            P("tp", "fsdp"),
            P("fsdp"),
            P("fsdp", None),
            P("fsdp", None, "tp"),
            P("fsdp", None, "tp"),
            P("fsdp", "tp", None),
        ),
        check_vma=False,
    )
```

```python
import functools
import math

import jax
import jax.numpy as jnp
from jax import lax
from jax.experimental import pallas as pl
from jax.experimental.pallas import tpu as pltpu
from jax.sharding import Mesh
from jax.sharding import PartitionSpec as P

HEAD = 64
TOPK = 8
E = 16
CAP = 256
EPSILON = 1e-06
BF = jnp.bfloat16
F32 = jnp.float32
NEG = -1e30
FAR = 1e6


def dot(a, b, ca, cb):
    return lax.dot_general(a, b, (((ca,), (cb,)), ((), ())), preferred_element_type=F32)


def shift(v, axis, n, by=1):
    return lax.ppermute(v, axis, [(i, (i + by) % n) for i in range(n)])


def swap(v, axis):
    return lax.ppermute(v, axis, [(0, 1), (1, 0)])


def pick(v, index, parts, dim):
    size = v.shape[dim] // parts
    return lax.dynamic_slice_in_dim(v, index * size, size, dim)


def put(buffer, v, start, dim):
    return lax.dynamic_update_slice_in_dim(buffer, v, start, dim)


def after(v, *others):
    return lax.optimization_barrier((v,) + others)[0]


def direct_reduce(part, axis, n):
    me = lax.axis_index(axis)
    total = part(me)
    for s in range(1, n):
        total = total + shift(part((me + s) % n).astype(BF), axis, n, s).astype(F32)
    return total


def ring_reduce(part, axis, n, *others):
    me = lax.axis_index(axis)
    moving = part((me + n - 1) % n).astype(BF)
    for s in range(2, n):
        moving = (shift(moving, axis, n).astype(F32) + part((me + n - s) % n)).astype(BF)
    moving = shift(moving, axis, n)
    if others:
        moving = after(moving, *others)
    return moving.astype(F32) + part(me)


def core_halves(v, dim):
    core = lax.axis_index("core")
    mine = pick(v, core, 2, dim)
    theirs = pick(v, 1 - core, 2, dim)
    return mine.astype(F32) + swap(theirs.astype(BF), "core").astype(F32)


def core_join(v, dim):
    other = swap(v, "core")
    first = lax.axis_index("core") == 0
    return jnp.concatenate([jnp.where(first, v, other), jnp.where(first, other, v)], axis=dim)


def ring_gather(v, axis, n, dim):
    me = lax.axis_index(axis)
    size = v.shape[dim]
    shape = list(v.shape)
    shape[dim] = size * n
    out = put(jnp.zeros(shape, v.dtype), v, me * size, dim)
    moving = v
    for s in range(1, n):
        moving = shift(moving, axis, n)
        out = put(out, moving, ((me + n - s) % n) * size, dim)
    return out


def ctx_total(v, n_cx):
    half = core_halves(v, 0).astype(BF)
    part = ring_reduce(lambda j: pick(half, j, n_cx, 0).astype(F32), "cx", n_cx).astype(BF)
    return core_join(ring_gather(part, "cx", n_cx, 0), 0)


def normalize(values):
    inverse = lax.rsqrt(jnp.mean(values * values, axis=-1, keepdims=True) + EPSILON)
    return inverse, values * inverse


def norm_backward(grad, gain, inverse, normed):
    scaled = grad * gain
    return inverse * (scaled - normed * jnp.mean(scaled * normed, axis=-1, keepdims=True))


def rotate(v, cos, sin, inverse):
    rows = v.shape[1]
    shaped = v.reshape(-1, 2, HEAD // 2, rows)
    a, b = shaped[:, 0], shaped[:, 1]
    if inverse:
        out = jnp.stack([a * cos + b * sin, b * cos - a * sin], axis=1)
    else:
        out = jnp.stack([a * cos - b * sin, b * cos + a * sin], axis=1)
    return out.reshape(-1, rows)


def keep_plan(routes, order, live):
    rows = routes.shape[0]
    pairs = rows * TOPK
    token, choice = order // TOPK, order % TOPK
    rank = jnp.arange(pairs, dtype=jnp.int32)
    at_token = (jnp.arange(rows, dtype=jnp.int32)[:, None] == token[None, :]).astype(BF)
    at_choice = jnp.arange(TOPK, dtype=jnp.int32)[:, None] == choice[None, :]
    high = jnp.where(at_choice, (rank // 64)[None, :], 0).astype(BF)
    low = jnp.where(at_choice, (rank % 64)[None, :], 0).astype(BF)
    place = dot(at_token, jnp.concatenate([high, low], axis=0), 1, 1)
    place = place[:, :TOPK] * 64.0 + place[:, TOPK:]
    hits = routes[:, :, None] == jnp.arange(E, dtype=jnp.int32)[None, None, :]
    routed = jnp.any(hits, axis=1)
    place_e = jnp.sum(jnp.where(hits, place[:, :, None], 0.0), axis=1)
    place_e = jnp.where(routed & live[:, None], place_e, FAR)
    across = place_e.T
    earlier = jnp.sum((place_e[:, :, None] < across[None, :, :]).astype(F32), axis=0).T
    kept = routed & live[:, None] & (earlier < CAP)
    return routed, kept


def assemble(info_ref, own_ref, got_ref, other_ref, full_ref):
    z, core = info_ref[0], info_ref[1]
    rows = own_ref.shape[0]
    piece = rows // 2
    n_z = got_ref.shape[0] + 1
    full_ref[pl.ds(pl.multiple_of(z * rows, piece), rows), :] = own_ref[...]
    for s in range(1, n_z):
        start = ((z + n_z - s) % n_z) * rows
        mine = pl.multiple_of(start + core * piece, piece)
        theirs = pl.multiple_of(start + (1 - core) * piece, piece)
        full_ref[pl.ds(mine, piece), :] = got_ref[s - 1]
        full_ref[pl.ds(theirs, piece), :] = other_ref[s - 1]


def project_kernel(turned, scale, info_ref, own_ref, got_ref, other_ref, x_ref, cos_ref, sin_ref, out_ref, full_ref):
    assemble(info_ref, own_ref, got_ref, other_ref, full_ref)
    flat = jnp.dot(x_ref[...], full_ref[...], preferred_element_type=F32).T
    cos, sin = cos_ref[...], sin_ref[...]
    quarter = HEAD // 2
    for start in range(0, turned, HEAD):
        a = flat[start : start + quarter, :]
        b = flat[start + quarter : start + HEAD, :]
        out_ref[start : start + quarter, :] = ((a * cos - b * sin).astype(BF) * scale).astype(BF)
        out_ref[start + quarter : start + HEAD, :] = ((b * cos + a * sin).astype(BF) * scale).astype(BF)
    if turned < flat.shape[0]:
        out_ref[turned:, :] = flat[turned:, :].astype(BF)


def project(info, own, got, other, x, cos, sin, turned, scale):
    columns = own.shape[1]
    rows, width = x.shape
    return pl.pallas_call(
        functools.partial(project_kernel, turned, scale),
        name="project",
        grid_spec=pltpu.PrefetchScalarGridSpec(num_scalar_prefetch=1, grid=(1,),
            in_specs=[pl.BlockSpec(v.shape, lambda i, n, k=v.ndim: (0,) * k) for v in (own, got, other, x, cos, sin)],
            out_specs=[
                pl.BlockSpec((columns, rows), lambda i, n: (0, 0)),
                pl.BlockSpec((width, columns), lambda i, n: (0, 0)),
            ],
        ),
        out_shape=[
            jax.ShapeDtypeStruct((columns, rows), BF),
            jax.ShapeDtypeStruct((width, columns), BF),
        ],
        compiler_params=pltpu.CompilerParams(vmem_limit_bytes=40 << 20),
        cost_estimate=pl.CostEstimate(
            flops=2 * rows * width * columns,
            transcendentals=0,
            bytes_accessed=4 * width * columns + 2 * rows * (width + columns),
        ),
    )(info, own, got, other, x, cos, sin)


def assembled(info, own, got, other):
    rows, columns = own.shape
    full = (rows * (got.shape[0] + 1), columns)
    return pl.pallas_call(
        assemble,
        name="assembled",
        grid_spec=pltpu.PrefetchScalarGridSpec(num_scalar_prefetch=1, grid=(1,),
            in_specs=[pl.BlockSpec(v.shape, lambda i, n, k=v.ndim: (0,) * k) for v in (own, got, other)],
            out_specs=pl.BlockSpec(full, lambda i, n: (0, 0)),
        ),
        out_shape=jax.ShapeDtypeStruct(full, BF),
        compiler_params=pltpu.CompilerParams(vmem_limit_bytes=32 << 20),
        cost_estimate=pl.CostEstimate(flops=0, transcendentals=0, bytes_accessed=4 * rows * columns * 4),
    )(info, own, got, other)


def softmax_block(q, k, last, base, first_row, length):
    s = lax.dot_general(k, q, (((0,), (0,)), ((), ())), preferred_element_type=F32)
    if last:
        key = base + lax.broadcasted_iota(jnp.int32, s.shape, 0)
        query = first_row + lax.broadcasted_iota(jnp.int32, s.shape, 1)
        s = jnp.where((key <= query) & (key < length), s, NEG)
    return s


def slot_of(block, ctx, n_ctx):
    n_cx = n_ctx // 2
    steps = (ctx // 2 + n_cx - block // 2) % n_cx
    return ((ctx + block) % 2) * n_cx + steps


def attend_kernel(group, info_ref, q_ref, kv_ref, o_ref, lse_ref):
    count, first_row, length, ctx = info_ref[0], info_ref[1], info_ref[2], info_ref[3]
    rows = q_ref.shape[1]
    n_ctx = kv_ref.shape[0]
    keys = kv_ref.shape[3]
    for h in range(group):
        q = q_ref[h * HEAD : (h + 1) * HEAD, :]

        def step(j, carry, last):
            top, total, acc = carry
            slot = slot_of(j, ctx, n_ctx)
            k = kv_ref[slot, 0]
            v = kv_ref[slot, 1]
            s = softmax_block(q, k, last, j * keys, first_row, length)
            new_top = jnp.maximum(top, jnp.max(s, axis=0, keepdims=True))
            p = jnp.exp(s - new_top)
            fade = jnp.exp(top - new_top)
            total = total * fade + jnp.sum(p, axis=0, keepdims=True)
            acc = acc * fade + jnp.dot(v, p.astype(BF), preferred_element_type=F32)
            return new_top, total, acc

        carry = (
            jnp.full((1, rows), NEG, F32),
            jnp.zeros((1, rows), F32),
            jnp.zeros((HEAD, rows), F32),
        )
        carry = lax.fori_loop(0, count - 1, functools.partial(step, last=False), carry)
        top, total, acc = step(count - 1, carry, True)
        o_ref[h * HEAD : (h + 1) * HEAD, :] = (acc / total).astype(BF)
        lse_ref[0, h : h + 1, :] = top + jnp.log(total)


def attend(q, kv, info, group, start, heads):
    rows = q.shape[1]
    n_ctx, _, depth, keys = kv.shape
    return pl.pallas_call(
        functools.partial(attend_kernel, group),
        name="attend",
        grid_spec=pltpu.PrefetchScalarGridSpec(
            num_scalar_prefetch=1,
            grid=(heads,),
            in_specs=[
                pl.BlockSpec((group * HEAD, rows), lambda g, i: (start + g, 0)),
                pl.BlockSpec((n_ctx, 2, HEAD, keys), lambda g, i: (0, 0, start + g, 0)),
            ],
            out_specs=[
                pl.BlockSpec((group * HEAD, rows), lambda g, i: (g, 0)),
                pl.BlockSpec((1, 8, rows), lambda g, i: (g, 0, 0)),
            ],
        ),
        out_shape=[
            jax.ShapeDtypeStruct((heads * group * HEAD, rows), BF),
            jax.ShapeDtypeStruct((heads, 8, rows), F32),
        ],
        compiler_params=pltpu.CompilerParams(vmem_limit_bytes=48 << 20),
        cost_estimate=pl.CostEstimate(
            flops=4 * heads * group * HEAD * rows * n_ctx * keys,
            transcendentals=heads * group * rows * n_ctx * keys,
            bytes_accessed=2 * q.size + kv.size,
        ),
    )(info, q, kv)


def attend_back_kernel(group, info_ref, q_ref, kv_ref, o_ref, do_ref, lse_ref, dq_ref, dkv_ref):
    count, first_row, length, ctx = info_ref[0], info_ref[1], info_ref[2], info_ref[3]
    n_ctx = kv_ref.shape[0]
    keys = kv_ref.shape[3]
    delta = []
    for h in range(group):
        part = slice(h * HEAD, (h + 1) * HEAD)
        delta.append(
            jnp.sum(do_ref[part, :].astype(F32) * o_ref[part, :].astype(F32), axis=0, keepdims=True)
        )
    dq_ref[...] = jnp.zeros_like(dq_ref)

    def step(j, last):
        slot = slot_of(j, ctx, n_ctx)
        k = kv_ref[slot, 0]
        v = kv_ref[slot, 1]
        dk = jnp.zeros((keys, HEAD), F32)
        dv = jnp.zeros((keys, HEAD), F32)
        for h in range(group):
            part = slice(h * HEAD, (h + 1) * HEAD)
            q = q_ref[part, :]
            do = do_ref[part, :]
            s = softmax_block(q, k, last, j * keys, first_row, length)
            p = jnp.exp(s - lse_ref[0, h : h + 1, :])
            dp = lax.dot_general(v, do, (((0,), (0,)), ((), ())), preferred_element_type=F32)
            ds = (p * (dp - delta[h])).astype(BF)
            pb = p.astype(BF)
            dv += lax.dot_general(pb, do, (((1,), (1,)), ((), ())), preferred_element_type=F32)
            dk += lax.dot_general(ds, q, (((1,), (1,)), ((), ())), preferred_element_type=F32)
            dq_ref[part, :] += jnp.dot(k, ds, preferred_element_type=F32)
        dkv_ref[slot, 0] = dk.T.astype(BF)
        dkv_ref[slot, 1] = dv.T.astype(BF)

    @pl.loop(0, count - 1)
    def _(j):
        step(j, False)

    step(count - 1, True)

    @pl.loop(count, n_ctx)
    def _(j):
        dkv_ref[slot_of(j, ctx, n_ctx)] = jnp.zeros(dkv_ref.shape[1:], BF)


def attend_back(q, kv, o, do, lse, info, group):
    rows = q.shape[1]
    n_ctx, _, depth, keys = kv.shape
    heads = depth // HEAD
    wide = pl.BlockSpec((group * HEAD, rows), lambda g, i: (g, 0))
    blocks = pl.BlockSpec((n_ctx, 2, HEAD, keys), lambda g, i: (0, 0, g, 0))
    return pl.pallas_call(
        functools.partial(attend_back_kernel, group),
        name="attend_back",
        grid_spec=pltpu.PrefetchScalarGridSpec(
            num_scalar_prefetch=1,
            grid=(heads,),
            in_specs=[
                wide,
                blocks,
                wide,
                wide,
                pl.BlockSpec((1, 8, rows), lambda g, i: (g, 0, 0)),
            ],
            out_specs=[wide, blocks],
        ),
        out_shape=[
            jax.ShapeDtypeStruct(q.shape, F32),
            jax.ShapeDtypeStruct(kv.shape, BF),
        ],
        compiler_params=pltpu.CompilerParams(vmem_limit_bytes=48 << 20),
        cost_estimate=pl.CostEstimate(
            flops=10 * q.shape[0] * rows * n_ctx * keys,
            transcendentals=q.shape[0] // HEAD * rows * n_ctx * keys,
            bytes_accessed=10 * q.size + 4 * kv.size,
        ),
    )(info, q, kv, o, do, lse)


def expert_kernel(aliased, info_ref, near_in, far_in, near_do, far_do, gate_ref, up_ref, down_ref, *refs):
    if aliased:
        refs = refs[1:]
    near_out, far_out, mix_out, act_out, dg_out, du_out = refs[:6]
    rows_x, rows_do, shares_in, mix_sum, back_sum, shares_out = refs[6:]
    e = pl.program_id(0)
    half, width = near_do.shape[2:]
    rows = 2 * half

    @pl.when(e == 0)
    def _():
        rows_x[:half, :] = near_in[:, :width]
        rows_x[half:, :] = far_in[:, :width]
        rows_do[:half, :] = near_do[0, 0]
        rows_do[half:, :] = far_do[0, 0]
        shares_in[:half, :] = near_in[:, width:].astype(F32)
        shares_in[half:, :] = far_in[:, width:].astype(F32)

    lanes = lax.broadcasted_iota(jnp.int32, (rows, 128), 1)
    x = rows_x[...]
    do = rows_do[...]
    per, _, hidden = gate_ref.shape
    mix = back = share = None
    for i in range(per):
        chosen = info_ref[0] + e * per + i
        gate, up, down = gate_ref[i], up_ref[i], down_ref[i]
        weight = jnp.sum(
            jnp.where((lanes == chosen) | (lanes == chosen + E), shares_in[...], 0.0),
            axis=1,
            keepdims=True,
        )
        g = jnp.dot(x, gate, preferred_element_type=F32)
        u = jnp.dot(x, up, preferred_element_type=F32)
        dact = dot(do, down, 1, 1)
        sig = jax.nn.sigmoid(g)
        silu = g * sig
        act = silu * u
        share_i = jnp.where(lanes == chosen, jnp.sum(act * dact, axis=1, keepdims=True), 0.0)
        dhid = dact * weight
        part = slice(i * hidden, (i + 1) * hidden)
        act_out[:, part] = (act * weight).astype(BF)
        dg_out[:, part] = (dhid * u * (sig * (1.0 + g * (1.0 - sig)))).astype(BF)
        du_out[:, part] = (dhid * silu).astype(BF)
        mix_i = jnp.dot(act_out[:, part], down, preferred_element_type=F32)
        back_i = dot(dg_out[:, part], gate, 1, 1) + dot(du_out[:, part], up, 1, 1)
        mix = mix_i if mix is None else mix + mix_i
        back = back_i if back is None else back + back_i
        share = share_i if share is None else share + share_i

    @pl.when(e == 0)
    def _():
        mix_sum[...] = mix
        back_sum[...] = back
        shares_out[...] = share

    @pl.when(e > 0)
    def _():
        mix_sum[...] += mix
        back_sum[...] += back
        shares_out[...] += share

    @pl.when(e == pl.num_programs(0) - 1)
    def _():
        near_out[:, :width] = back_sum[:half, :].astype(BF)
        near_out[:, width:] = shares_out[:half, :].astype(BF)
        far_out[:, :width] = back_sum[half:, :].astype(BF)
        far_out[:, width:] = shares_out[half:, :].astype(BF)
        tp = info_ref[1]
        mix_out[0, tp] = mix_sum[:half, :].astype(BF)
        mix_out[0, 1 - tp] = mix_sum[half:, :].astype(BF)


def experts(info, near, far, do_near, do_far, n_z, gate, up, down, mix_all):
    half, wide = near.shape
    width = do_near.shape[3]
    held, _, hidden = gate.shape
    rows = 2 * half
    whole = lambda shape: pl.BlockSpec(shape, lambda e, i: (0, 0))
    per = 1
    each = lambda shape: pl.BlockSpec((per,) + shape, lambda e, i: (e, 0, 0))
    column = pl.BlockSpec((rows, per * hidden), lambda e, i: (0, e))
    mid = jax.ShapeDtypeStruct((rows, held * hidden), BF)
    message = jax.ShapeDtypeStruct((half, wide), BF)
    aliased = mix_all is not None
    return pl.pallas_call(
        functools.partial(expert_kernel, aliased),
        name="experts",
        grid_spec=pltpu.PrefetchScalarGridSpec(
            num_scalar_prefetch=1,
            grid=(held // per,),
            in_specs=[
                whole((half, wide)),
                whole((half, wide)),
                pl.BlockSpec((1, 1, half, width), lambda e, i: (i[3], i[4], 0, 0)),
                pl.BlockSpec((1, 1, half, width), lambda e, i: (i[5], i[4], 0, 0)),
                each((width, hidden)),
                each((width, hidden)),
                each((hidden, width)),
            ]
            + [pl.BlockSpec(memory_space=pl.ANY)] * aliased,
            out_specs=[
                whole((half, wide)),
                whole((half, wide)),
                pl.BlockSpec((1, 2, half, width), lambda e, i: (i[2], 0, 0, 0)),
                column,
                column,
                column,
            ],
            scratch_shapes=[
                pltpu.VMEM((rows, width), BF),
                pltpu.VMEM((rows, width), BF),
                pltpu.VMEM((rows, 128), F32),
                pltpu.VMEM((rows, width), F32),
                pltpu.VMEM((rows, width), F32),
                pltpu.VMEM((rows, 128), F32),
            ],
        ),
        out_shape=[
            message,
            message,
            jax.ShapeDtypeStruct((n_z, 2, half, width), BF),
            mid,
            mid,
            mid,
        ],
        input_output_aliases={8: 2} if aliased else {},
        compiler_params=pltpu.CompilerParams(vmem_limit_bytes=56 << 20),
        cost_estimate=pl.CostEstimate(
            flops=12 * rows * width * held * hidden,
            transcendentals=rows * held * hidden,
            bytes_accessed=6 * held * hidden * width + 16 * rows * width,
        ),
    )(info, near, far, do_near, do_far, gate, up, down, *([mix_all] if aliased else []))


def weight_grad_kernel(count, info_ref, *refs):
    lefts = refs[:count]
    rights = refs[count:-2]
    out, turned = refs[-2:]
    size = lefts[0].shape[0]

    @pl.when(pl.program_id(0) == 0)
    def _():
        for i, left in enumerate(lefts):
            turned[:, i * size : (i + 1) * size] = left[:, : turned.shape[0]].T

    half = len(rights) // 2
    for i, blocks in enumerate((rights[:half], rights[half:])):
        out[0, i] = jnp.dot(
            turned[...],
            jnp.concatenate([block[...] for block in blocks], axis=0),
            preferred_element_type=F32,
        ).astype(BF)


def weight_grads(info, chunks, firsts, seconds, held, width):
    size, wide = chunks[0].shape
    rows, mid = firsts[0].shape
    hidden = mid // held
    at = 1 + len(firsts)
    column = pl.BlockSpec((rows, hidden), lambda e, i: (0, i[at + e]))
    return pl.pallas_call(
        functools.partial(weight_grad_kernel, len(chunks)),
        name="weight_grads",
        grid_spec=pltpu.PrefetchScalarGridSpec(
            num_scalar_prefetch=1,
            grid=(held,),
            in_specs=[
                pl.BlockSpec((size, wide), lambda e, i: (0, 0), pipeline_mode=pl.Buffered(1))
                for _ in chunks
            ]
            + [column for _ in firsts + seconds],
            out_specs=pl.BlockSpec((1, 2, width, hidden), lambda e, i: (e, 0, 0, 0)),
            scratch_shapes=[pltpu.VMEM((width, size * len(chunks)), BF)],
        ),
        out_shape=jax.ShapeDtypeStruct((held, 2, width, hidden), BF),
        compiler_params=pltpu.CompilerParams(vmem_limit_bytes=58 << 20),
        cost_estimate=pl.CostEstimate(
            flops=4 * len(firsts) * rows * width * mid,
            transcendentals=0,
            bytes_accessed=4 * len(firsts) * rows * (width + mid),
        ),
    )(info, *chunks, *firsts, *seconds)


def down_grad_kernel(count, info_ref, *refs):
    rights = refs[: 2 * count]
    lefts = refs[2 * count : 3 * count]
    total = None
    for i, left in enumerate(lefts):
        right = jnp.concatenate([rights[2 * i][0, 0], rights[2 * i + 1][0, 0]], axis=0)
        term = dot(left[...], right, 0, 0)
        total = term if total is None else total + term
    refs[-1][0] = total.astype(BF)


def down_grads(info, do_all, acts, held):
    _, n_z, size, width = do_all.shape
    rows, mid = acts[0].shape
    hidden = mid // held
    at = 1 + n_z
    chunk = lambda other, s: pl.BlockSpec(
        (1, 1, size, width),
        lambda e, i: ((1 - i[0]) if other else i[0], i[1 + s], 0, 0),
        pipeline_mode=pl.Buffered(1),
    )
    return pl.pallas_call(
        functools.partial(down_grad_kernel, n_z),
        name="down_grads",
        grid_spec=pltpu.PrefetchScalarGridSpec(
            num_scalar_prefetch=1,
            grid=(held,),
            in_specs=[chunk(other, s) for s in range(n_z) for other in (False, True)]
            + [pl.BlockSpec((rows, hidden), lambda e, i: (0, i[at + e])) for _ in acts],
            out_specs=pl.BlockSpec((1, hidden, width), lambda e, i: (e, 0, 0)),
        ),
        out_shape=jax.ShapeDtypeStruct((held, hidden, width), BF),
        compiler_params=pltpu.CompilerParams(vmem_limit_bytes=56 << 20),
        cost_estimate=pl.CostEstimate(
            flops=2 * len(acts) * rows * width * mid,
            transcendentals=0,
            bytes_accessed=2 * len(acts) * rows * (width + mid),
        ),
    )(info, *([do_all] * (2 * n_z)), *acts)


def place_kernel(count, info_ref, *refs):
    for i, ref in enumerate(refs[:count]):

        @pl.when(pl.program_id(0) == i)
        def _():
            for k, out in enumerate(refs[count:]):
                out[0] = ref[0, k].astype(F32)


def place(info, parts):
    kinds = parts[0][0].shape[1]
    shape = parts[0][0].shape[2:]
    return pl.pallas_call(
        functools.partial(place_kernel, len(parts)),
        name="place",
        grid_spec=pltpu.PrefetchScalarGridSpec(
            num_scalar_prefetch=1,
            grid=(len(parts),),
            in_specs=[
                pl.BlockSpec((1, kinds) + shape, lambda e, i, k=k: (k, 0, 0, 0)) for _, k in parts
            ],
            out_specs=[pl.BlockSpec((1,) + shape, lambda e, i: (i[e], 0, 0))] * kinds,
        ),
        out_shape=[jax.ShapeDtypeStruct((len(parts),) + shape, F32)] * kinds,
        compiler_params=pltpu.CompilerParams(vmem_limit_bytes=48 << 20),
        cost_estimate=pl.CostEstimate(
            flops=0, transcendentals=0, bytes_accessed=6 * kinds * len(parts) * math.prod(shape)
        ),
    )(info, *[array for array, _ in parts])


def local(
    sizes,
    tokens,
    lengths,
    routes,
    visit_order,
    cotangent,
    first_gain,
    query_weight,
    key_matrix,
    value_matrix,
    output_weight,
    second_gain,
    router_weight,
    gate_weight,
    up_weight,
    down_weight,
):
    n_z, n_cx = sizes
    n_ctx = 2 * n_cx
    z = lax.axis_index("fsdp")
    cx = lax.axis_index("cx")
    core = lax.axis_index("core")
    tp = lax.axis_index("tp")
    ctx = cx * 2 + core
    rows, width = tokens.shape[1:]
    half = rows // 2
    shard = query_weight.shape[0]
    q_width = query_weight.shape[1]
    kv_width = key_matrix.shape[1]
    group = q_width // kv_width
    held = gate_weight.shape[0]
    hidden = gate_weight.shape[2]
    first_row = ctx * rows
    length = lengths[0]
    positions = first_row + jnp.arange(rows, dtype=jnp.int32)
    live = positions < length
    valid = live.astype(F32)[:, None]

    small = jnp.concatenate(
        [first_gain[None], second_gain[None], router_weight.T], axis=0
    )
    small_full = put(jnp.zeros((2 + E, width), BF), small, z * shard, 1)
    for s in range(1, n_z):
        small_full = put(small_full, shift(small, "fsdp", n_z, s), ((z + n_z - s) % n_z) * shard, 1)
    gain_first = small_full[0:1].astype(F32)
    gain_second = small_full[1:2].astype(F32)
    router = small_full[2:]

    grad_half = (pick(cotangent[0], tp, 2, 0).astype(F32) * pick(valid, tp, 2, 0)).astype(BF)
    grad_other = swap(grad_half, "tp")

    def bring(own):
        piece = pick(own, core, 2, 0)
        return own, [shift(piece, "fsdp", n_z, s) for s in range(1, n_z)]

    def spread(own, got):
        got = jnp.stack(got)
        return own, got, swap(got, "core")

    kv_pieces = spread(*bring(jnp.concatenate([key_matrix, value_matrix], axis=1)))
    q_own, q_got = bring(after(query_weight, kv_pieces[1]))
    here = jnp.stack([z, core]).astype(jnp.int32)

    routed, kept = keep_plan(routes[0], visit_order[0, 0], live)

    inputs = tokens[0].astype(F32)
    inverse_one, normed_one = normalize(inputs)
    hidden_one = (normed_one * gain_first).astype(BF)
    frequency = jnp.exp(
        jnp.arange(HEAD // 2, dtype=F32) * (-2.0 * math.log(10000.0) / HEAD)
    )
    angles = frequency[:, None] * positions.astype(F32)[None, :]
    cos, sin = jnp.cos(angles), jnp.sin(angles)
    scale = HEAD**-0.5
    kv_mine, w_kv = project(here, *kv_pieces, hidden_one, cos, sin, kv_width, 1.0)
    kv_mine = kv_mine.reshape(1, 2, kv_width, rows)
    near_kv = [kv_mine]
    for s in range(1, n_cx):
        near_kv.append(shift(near_kv[-1], "cx", n_cx))
    near_kv = jnp.concatenate(near_kv, axis=0)
    q_pieces = spread(q_own, [after(v, near_kv) for v in q_got])
    o_own, o_got = bring(after(output_weight.T, q_pieces[1]))
    grad_all = lax.all_gather(after(grad_half, q_pieces[1]), ("tp", "fsdp"))
    grad_all = grad_all.reshape(2, n_z, half, width)
    query, w_q = project(here, *q_pieces, hidden_one, cos, sin, q_width, scale)
    kv = jnp.concatenate([near_kv, swap(near_kv, "core")], axis=0)
    count = jnp.minimum(ctx + 1, (length + rows - 1) // rows)
    info = jnp.stack([count, first_row, length, ctx])
    kv_heads = kv_width // HEAD
    split = [(0, kv_heads // 2), (kv_heads // 2, kv_heads - kv_heads // 2)]
    early, early_lse = attend(after(query, grad_other), kv, info, group, *split[0])
    o_pieces = spread(o_own, [after(v, early) for v in o_got])
    later, later_lse = attend(after(query, early), kv, info, group, *split[1])
    attended = jnp.concatenate([early, later], axis=0)
    lse = jnp.concatenate([early_lse, later_lse], axis=0)
    o_full = assembled(here, *[after(v, later) for v in o_pieces])

    far = dot(pick(attended, 1 - tp, 2, 1), o_full, 0, 1).astype(BF)
    near = dot(pick(attended, tp, 2, 1), o_full, 0, 1)
    residual = pick(tokens[0], tp, 2, 0).astype(F32) + near + swap(far, "tp").astype(F32)
    inverse_two, normed_two = normalize(residual)
    hidden_two = (normed_two * gain_second).astype(BF)
    logits = dot(hidden_two, router, 1, 1)
    routed_half = pick(routed, tp, 2, 0)
    kept_half = pick(kept, tp, 2, 0).astype(F32)
    masked = jnp.where(routed_half, logits, NEG)
    raised = jnp.where(
        routed_half, jnp.exp(masked - jnp.max(masked, axis=1, keepdims=True)), 0.0
    )
    gates = raised / jnp.sum(raised, axis=1, keepdims=True)
    weights = gates * kept_half

    high = weights.astype(BF)
    low = (weights - high.astype(F32)).astype(BF)
    message = jnp.concatenate(
        [hidden_two, high, low, jnp.zeros((half, 128 - 2 * E), BF)], axis=1
    )
    blocks = [(z + n_z - s) % n_z for s in range(n_z)]
    near = [message]
    far = [swap(message, "tp")]
    coming = shift(message, "fsdp", n_z)
    done, mix_all, moving, joined = [], None, None, ()
    for s in range(n_z):
        first = near[s]
        if s + 1 < n_z:
            near.append(after(coming, *[d[0] for d in done[-1:]]))
            far.append(swap(near[-1], "tp"))
            first = after(first, near[-1])
            if s + 2 < n_z:
                coming = shift(near[-1], "fsdp", n_z)
        first = after(first, *joined)
        if s:
            info_s = [z * held, tp, blocks[s], tp, blocks[s], 1 - tp]
            rows_do = (grad_all, grad_all)
        else:
            info_s = [z * held, tp, blocks[s], 0, 0, 0]
            rows_do = (grad_half[None, None], grad_other[None, None])
        done.append(
            experts(
                jnp.stack([jnp.asarray(v, jnp.int32) for v in info_s]),
                first,
                far[s],
                *rows_do,
                n_z,
                gate_weight,
                up_weight,
                down_weight,
                mix_all,
            )
        )
        mix_all = done[s][2]
        if s > 1:
            part = done[s - 1][0].astype(F32) + swap(done[s - 1][1], "tp").astype(F32)
            if s > 2:
                part = shift(moving, "fsdp", n_z).astype(F32) + part
            moving = part.astype(BF)
            joined = (moving,)
    last = swap(done[-1][1], "tp")
    by_ctx = held == n_ctx and n_cx == 2
    if by_ctx:
        slots = [(1 - core) * 2 + 1 - cx, (1 - core) * 2 + cx, core * 2 + 1 - cx, core * 2 + cx]
    else:
        slots = list(range(held))
    order = jnp.stack([jnp.asarray(v, jnp.int32) for v in [tp] + blocks + slots])
    grad_pair = weight_grads(
        order,
        [v for s in range(n_z) for v in (near[s], far[s])],
        [done[s][4] for s in range(n_z)],
        [after(done[s][5], moving) for s in range(n_z)],
        held,
        width,
    )
    part = done[-1][0].astype(F32) + after(last, grad_pair).astype(F32)
    moving = (shift(moving, "fsdp", n_z).astype(F32) + part).astype(BF)
    own = done[0][0].astype(F32) + swap(after(done[0][1], last), "tp").astype(F32)
    grad_down = down_grads(
        order, grad_all, [after(done[s][3], moving) for s in range(n_z)], held
    )[:, None]
    back = shift(moving, "fsdp", n_z)

    half_held = held // 2

    def core_stage(v, *others):
        both = v[half_held:].astype(F32) + after(swap(v[:half_held], "core"), *others).astype(F32)
        return both, both[:1].astype(BF)

    if by_ctx:
        pair_half, pair_far = core_stage(grad_pair, grad_down)
        back, own = after(back, pair_far), after(own, pair_far)
        pair_far = swap(pair_far, "cx")
    back = back.astype(F32) + own
    hidden_grad = back[:, :width]
    gate_grad = back[:, width : width + E] * kept_half

    mixture = lax.psum_scatter(
        after(mix_all, back).reshape(2 * n_z * half, width),
        ("fsdp", "tp"),
        scatter_dimension=0,
        tiled=True,
    )

    logit_grad = (
        gates * (gate_grad - jnp.sum(gates * gate_grad, axis=1, keepdims=True))
    ).astype(BF)
    hidden_grad = hidden_grad + dot(logit_grad, router, 1, 0)
    grad_router = dot(logit_grad, hidden_two, 0, 0)
    grad_second = jnp.sum(hidden_grad * normed_two, axis=0, keepdims=True)
    branch_half = (
        grad_half.astype(F32) + norm_backward(hidden_grad, gain_second, inverse_two, normed_two)
    ).astype(BF)
    lead = tp == 0
    branch_other = swap(branch_half, "tp")
    if by_ctx:
        down_half, down_far = core_stage(grad_down)
        branch_other = after(branch_other, down_far)
        down_far = swap(down_far, "cx")
    branch = jnp.concatenate(
        [jnp.where(lead, branch_half, branch_other), jnp.where(lead, branch_other, branch_half)],
        axis=0,
    )

    attended_grad = dot(o_full, branch, 0, 1).astype(BF)
    grad_output = dot(attended, branch, 1, 0).astype(BF)
    attended_grad = after(attended_grad, grad_output)

    grad_query_rot, grad_kv = attend_back(
        query, kv, attended, attended_grad, lse, info, group
    )
    kv_sum = grad_kv[:n_cx].astype(F32) + swap(grad_kv[n_cx:], "core").astype(F32)
    kv_moving = kv_sum[1].astype(BF)
    for s in range(2, n_cx):
        kv_moving = (shift(kv_moving, "cx", n_cx).astype(F32) + kv_sum[s]).astype(BF)
    kv_grad = shift(kv_moving, "cx", n_cx).astype(F32) + kv_sum[0]
    query_grad = (rotate(grad_query_rot, cos, sin, True) * scale).astype(BF)
    key_grad = rotate(kv_grad[0], cos, sin, True).astype(BF)
    value_grad = kv_grad[1].astype(BF)
    grad_both = jnp.concatenate([key_grad, value_grad], axis=0)
    first_part = dot(query_grad, w_q, 0, 1) + dot(grad_both, w_kv, 0, 1)
    grad_first = jnp.sum(first_part * normed_one, axis=0, keepdims=True)
    first_low = first_part.astype(BF)
    first_other = swap(first_low, "tp")
    if by_ctx:
        down_total = (down_half[1:] + after(down_far, first_low).astype(F32)).astype(BF)
        pair_total = (pair_half[1:] + after(pair_far, first_low).astype(F32)).astype(BF)
    grad_q = dot(hidden_one, query_grad, 0, 1).astype(BF)
    grad_kv_w = dot(hidden_one, grad_both, 0, 1).astype(BF)

    def owned(v, dim, *others):
        if dim:
            mine = core_halves(v, 0).astype(BF)
            part = lambda j: pick(mine, j, n_z, 1)
        else:
            mine = core_halves(v.reshape(n_z, v.shape[0] // n_z, v.shape[1]), 1).astype(BF)
            part = lambda j: lax.dynamic_index_in_dim(mine, j, 0, False)
        total = part(z).astype(F32)
        for s in range(1, n_z):
            total = total + after(shift(part((z + s) % n_z), "fsdp", n_z, s), *others).astype(F32)
        everyone = ring_gather(total.astype(BF)[None], "cx", n_cx, 0)
        return core_join(jnp.sum(everyone.astype(F32), axis=0).astype(BF), 0)

    grad_q = owned(grad_q, 0, first_low).astype(F32)
    grad_kv_w = owned(grad_kv_w, 0).astype(F32)
    grad_output = owned(grad_output, 1, first_low).astype(F32)

    valid_half = pick(valid, tp, 2, 0)
    out_half = (valid_half * (residual + after(mixture, grad_kv).astype(F32))).astype(BF)
    out_other = swap(out_half, "tp")
    layer_out = jnp.concatenate(
        [jnp.where(lead, out_half, out_other), jnp.where(lead, out_other, out_half)], axis=0
    )

    def ctx_sum_generic(v):
        kinds, a, b = v.shape[1:]
        total = ctx_total(v.reshape(-1, b), n_cx).reshape(v.shape).astype(F32)
        return [total[:, k] for k in range(kinds)]

    def ctx_sum_end(total):
        both = jnp.concatenate([swap(total, "cx"), total], axis=0)
        others = swap(both, "core")
        return place(
            jnp.stack(slots).astype(jnp.int32), [(others, 0), (others, 1), (both, 0), (both, 1)]
        )

    if by_ctx:
        (grad_down,) = ctx_sum_end(down_total)
        grad_gate, grad_up = ctx_sum_end(pair_total)
    else:
        (grad_down,) = ctx_sum_generic(grad_down)
        grad_gate, grad_up = ctx_sum_generic(grad_pair)

    small_grad = jnp.concatenate([grad_first, grad_second, grad_router], axis=0)
    small_grad = small_grad + swap(small_grad, "tp")
    small_grad = small_grad + swap(small_grad, "core")
    everyone = ring_gather(small_grad[None], "cx", n_cx, 0)
    total = jnp.sum(everyone, axis=0)
    small_mine = pick(total, z, n_z, 1)
    for s in range(1, n_z):
        small_mine = small_mine + shift(pick(total, (z + s) % n_z, n_z, 1), "fsdp", n_z, s)

    first_grad = first_low.astype(F32) + after(first_other, small_mine).astype(F32)
    grad_inputs = branch.astype(F32) + norm_backward(
        first_grad, gain_first, inverse_one, normed_one
    )

    return (
        layer_out[None],
        grad_inputs[None],
        small_mine[0],
        grad_q,
        grad_kv_w[:, :kv_width],
        grad_kv_w[:, kv_width:],
        grad_output,
        small_mine[1],
        small_mine[2:].T,
        grad_gate,
        grad_up,
        grad_down,
    )


def solution(mesh):
    n_z, n_ctx, n_tp = mesh.shape["fsdp"], mesh.shape["ctx"], mesh.shape["tp"]
    named = Mesh(
        mesh.devices.reshape(n_z, n_ctx // 2, 2, n_tp), ("fsdp", "cx", "core", "tp")
    )
    ctx = ("cx", "core")
    placed = (
        P("fsdp", ctx, None),
        P("fsdp"),
        P("fsdp", ctx, None),
        P("fsdp", ctx, None),
        P("fsdp", ctx, None),
        P("fsdp"),
        P("fsdp", "tp"),
        P("fsdp", "tp"),
        P("fsdp", "tp"),
        P("tp", "fsdp"),
        P("fsdp"),
        P("fsdp", None),
        P("fsdp", None, "tp"),
        P("fsdp", None, "tp"),
        P("fsdp", "tp", None),
    )
    return jax.shard_map(
        functools.partial(local, (n_z, n_ctx // 2)),
        mesh=named,
        in_specs=placed,
        out_specs=(
            P("fsdp", ctx, None),
            P("fsdp", ctx, None),
            P("fsdp"),
            P("fsdp", "tp"),
            P("fsdp", "tp"),
            P("fsdp", "tp"),
            P("tp", "fsdp"),
            P("fsdp"),
            P("fsdp", None),
            P("fsdp", None, "tp"),
            P("fsdp", None, "tp"),
            P("fsdp", "tp", None),
        ),
        check_vma=False,
    )
```

```python
import functools
import math

import jax
import jax.numpy as jnp
from jax import lax
from jax.experimental import pallas as pl
from jax.experimental.pallas import tpu as pltpu
from jax.sharding import Mesh
from jax.sharding import PartitionSpec as P

HEAD = 64
TOPK = 8
E = 16
CAP = 256
EPSILON = 1e-06
BF = jnp.bfloat16
F32 = jnp.float32
NEG = -1e30
FAR = 1e6


def dot(a, b, ca, cb):
    return lax.dot_general(a, b, (((ca,), (cb,)), ((), ())), preferred_element_type=F32)


def shift(v, axis, n, by=1):
    return lax.ppermute(v, axis, [(i, (i + by) % n) for i in range(n)])


def swap(v, axis):
    return lax.ppermute(v, axis, [(0, 1), (1, 0)])


def pick(v, index, parts, dim):
    size = v.shape[dim] // parts
    return lax.dynamic_slice_in_dim(v, index * size, size, dim)


def put(buffer, v, start, dim):
    return lax.dynamic_update_slice_in_dim(buffer, v, start, dim)


def after(v, *others):
    return lax.optimization_barrier((v,) + others)[0]


def anchor_kernel(in_ref, out_ref):
    out_ref[...] = in_ref[...]


def anchor(*others):
    token = after(jnp.zeros((8, 128), F32), *others)
    return pl.pallas_call(
        anchor_kernel,
        name="anchor",
        out_shape=jax.ShapeDtypeStruct((8, 128), F32),
        cost_estimate=pl.CostEstimate(flops=10**11, transcendentals=0, bytes_accessed=8192),
    )(token)


def direct_reduce(part, axis, n):
    me = lax.axis_index(axis)
    total = part(me)
    for s in range(1, n):
        total = total + shift(part((me + s) % n).astype(BF), axis, n, s).astype(F32)
    return total


def ring_reduce(part, axis, n, *others):
    me = lax.axis_index(axis)
    moving = part((me + n - 1) % n).astype(BF)
    for s in range(2, n):
        moving = (shift(moving, axis, n).astype(F32) + part((me + n - s) % n)).astype(BF)
    moving = shift(moving, axis, n)
    if others:
        moving = after(moving, *others)
    return moving.astype(F32) + part(me)


def core_halves(v, dim):
    core = lax.axis_index("core")
    mine = pick(v, core, 2, dim)
    theirs = pick(v, 1 - core, 2, dim)
    return mine.astype(F32) + swap(theirs.astype(BF), "core").astype(F32)


def core_join(v, dim):
    other = swap(v, "core")
    first = lax.axis_index("core") == 0
    return jnp.concatenate([jnp.where(first, v, other), jnp.where(first, other, v)], axis=dim)


def ring_gather(v, axis, n, dim):
    me = lax.axis_index(axis)
    size = v.shape[dim]
    shape = list(v.shape)
    shape[dim] = size * n
    out = put(jnp.zeros(shape, v.dtype), v, me * size, dim)
    moving = v
    for s in range(1, n):
        moving = shift(moving, axis, n)
        out = put(out, moving, ((me + n - s) % n) * size, dim)
    return out


def ctx_total(v, n_cx):
    half = core_halves(v, 0).astype(BF)
    part = ring_reduce(lambda j: pick(half, j, n_cx, 0).astype(F32), "cx", n_cx).astype(BF)
    return core_join(ring_gather(part, "cx", n_cx, 0), 0)


def normalize(values):
    inverse = lax.rsqrt(jnp.mean(values * values, axis=-1, keepdims=True) + EPSILON)
    return inverse, values * inverse


def norm_backward(grad, gain, inverse, normed):
    scaled = grad * gain
    return inverse * (scaled - normed * jnp.mean(scaled * normed, axis=-1, keepdims=True))


def rotate(v, cos, sin, inverse):
    rows = v.shape[1]
    shaped = v.reshape(-1, 2, HEAD // 2, rows)
    a, b = shaped[:, 0], shaped[:, 1]
    if inverse:
        out = jnp.stack([a * cos + b * sin, b * cos - a * sin], axis=1)
    else:
        out = jnp.stack([a * cos - b * sin, b * cos + a * sin], axis=1)
    return out.reshape(-1, rows)


def keep_plan(routes, order, live):
    rows = routes.shape[0]
    pairs = rows * TOPK
    token, choice = order // TOPK, order % TOPK
    rank = jnp.arange(pairs, dtype=jnp.int32)
    at_token = (jnp.arange(rows, dtype=jnp.int32)[:, None] == token[None, :]).astype(BF)
    at_choice = jnp.arange(TOPK, dtype=jnp.int32)[:, None] == choice[None, :]
    high = jnp.where(at_choice, (rank // 64)[None, :], 0).astype(BF)
    low = jnp.where(at_choice, (rank % 64)[None, :], 0).astype(BF)
    place = dot(at_token, jnp.concatenate([high, low], axis=0), 1, 1)
    place = place[:, :TOPK] * 64.0 + place[:, TOPK:]
    hits = routes[:, :, None] == jnp.arange(E, dtype=jnp.int32)[None, None, :]
    routed = jnp.any(hits, axis=1)
    place_e = jnp.sum(jnp.where(hits, place[:, :, None], 0.0), axis=1)
    place_e = jnp.where(routed & live[:, None], place_e, FAR)
    across = place_e.T
    earlier = jnp.sum((place_e[:, :, None] < across[None, :, :]).astype(F32), axis=0).T
    kept = routed & live[:, None] & (earlier < CAP)
    return routed, kept


def assemble(info_ref, own_ref, got_ref, other_ref, full_ref):
    z, core, cx = info_ref[0], info_ref[1], info_ref[2]
    rows = own_ref.shape[0]
    chips, steps, piece, _ = got_ref.shape
    n_z = steps + 1
    full_ref[pl.ds(pl.multiple_of(z * rows, piece), rows), :] = own_ref[...]
    for k in range(chips):
        chip = (cx + chips - k) % chips
        for s in range(1, n_z):
            start = ((z + n_z - s) % n_z) * rows + chip * 2 * piece
            mine = pl.multiple_of(start + core * piece, piece)
            theirs = pl.multiple_of(start + (1 - core) * piece, piece)
            full_ref[pl.ds(mine, piece), :] = got_ref[k, s - 1]
            full_ref[pl.ds(theirs, piece), :] = other_ref[k, s - 1]


def project_kernel(turned, scale, info_ref, own_ref, got_ref, other_ref, x_ref, cos_ref, sin_ref, out_ref, full_ref):
    assemble(info_ref, own_ref, got_ref, other_ref, full_ref)
    flat = jnp.dot(x_ref[...], full_ref[...], preferred_element_type=F32).T
    cos, sin = cos_ref[...], sin_ref[...]
    quarter = HEAD // 2
    for start in range(0, turned, HEAD):
        a = flat[start : start + quarter, :]
        b = flat[start + quarter : start + HEAD, :]
        out_ref[start : start + quarter, :] = ((a * cos - b * sin).astype(BF) * scale).astype(BF)
        out_ref[start + quarter : start + HEAD, :] = ((b * cos + a * sin).astype(BF) * scale).astype(BF)
    if turned < flat.shape[0]:
        out_ref[turned:, :] = flat[turned:, :].astype(BF)


def project(info, own, got, other, x, cos, sin, turned, scale):
    columns = own.shape[1]
    rows, width = x.shape
    return pl.pallas_call(
        functools.partial(project_kernel, turned, scale),
        name="project",
        grid_spec=pltpu.PrefetchScalarGridSpec(num_scalar_prefetch=1, grid=(1,),
            in_specs=[pl.BlockSpec(v.shape, lambda i, n, k=v.ndim: (0,) * k) for v in (own, got, other, x, cos, sin)],
            out_specs=[
                pl.BlockSpec((columns, rows), lambda i, n: (0, 0)),
                pl.BlockSpec((width, columns), lambda i, n: (0, 0)),
            ],
        ),
        out_shape=[
            jax.ShapeDtypeStruct((columns, rows), BF),
            jax.ShapeDtypeStruct((width, columns), BF),
        ],
        compiler_params=pltpu.CompilerParams(vmem_limit_bytes=40 << 20),
        cost_estimate=pl.CostEstimate(
            flops=2 * rows * width * columns,
            transcendentals=0,
            bytes_accessed=4 * width * columns + 2 * rows * (width + columns),
        ),
    )(info, own, got, other, x, cos, sin)


def assembled(info, own, got, other):
    rows, columns = own.shape
    full = (rows * (got.shape[1] + 1), columns)
    return pl.pallas_call(
        assemble,
        name="assembled",
        grid_spec=pltpu.PrefetchScalarGridSpec(num_scalar_prefetch=1, grid=(1,),
            in_specs=[pl.BlockSpec(v.shape, lambda i, n, k=v.ndim: (0,) * k) for v in (own, got, other)],
            out_specs=pl.BlockSpec(full, lambda i, n: (0, 0)),
        ),
        out_shape=jax.ShapeDtypeStruct(full, BF),
        compiler_params=pltpu.CompilerParams(vmem_limit_bytes=32 << 20),
        cost_estimate=pl.CostEstimate(flops=0, transcendentals=0, bytes_accessed=4 * rows * columns * 4),
    )(info, own, got, other)


def softmax_block(q, k, last, base, first_row, length):
    s = lax.dot_general(k, q, (((0,), (0,)), ((), ())), preferred_element_type=F32)
    if last:
        key = base + lax.broadcasted_iota(jnp.int32, s.shape, 0)
        query = first_row + lax.broadcasted_iota(jnp.int32, s.shape, 1)
        s = jnp.where((key <= query) & (key < length), s, NEG)
    return s


def slot_of(block, ctx, n_ctx):
    n_cx = n_ctx // 2
    steps = (ctx // 2 + n_cx - block // 2) % n_cx
    return ((ctx + block) % 2) * n_cx + steps


def attend_kernel(group, info_ref, q_ref, kv_ref, o_ref, lse_ref):
    count, first_row, length, ctx = info_ref[0], info_ref[1], info_ref[2], info_ref[3]
    rows = q_ref.shape[1]
    n_ctx = kv_ref.shape[0]
    keys = kv_ref.shape[3]
    for h in range(group):
        q = q_ref[h * HEAD : (h + 1) * HEAD, :]

        def step(j, carry, last):
            top, total, acc = carry
            slot = slot_of(j, ctx, n_ctx)
            k = kv_ref[slot, 0]
            v = kv_ref[slot, 1]
            s = softmax_block(q, k, last, j * keys, first_row, length)
            new_top = jnp.maximum(top, jnp.max(s, axis=0, keepdims=True))
            p = jnp.exp(s - new_top)
            fade = jnp.exp(top - new_top)
            total = total * fade + jnp.sum(p, axis=0, keepdims=True)
            acc = acc * fade + jnp.dot(v, p.astype(BF), preferred_element_type=F32)
            return new_top, total, acc

        carry = (
            jnp.full((1, rows), NEG, F32),
            jnp.zeros((1, rows), F32),
            jnp.zeros((HEAD, rows), F32),
        )
        carry = lax.fori_loop(0, count - 1, functools.partial(step, last=False), carry)
        top, total, acc = step(count - 1, carry, True)
        o_ref[h * HEAD : (h + 1) * HEAD, :] = (acc / total).astype(BF)
        lse_ref[0, h : h + 1, :] = top + jnp.log(total)


def attend(q, kv, info, group, start, heads):
    rows = q.shape[1]
    n_ctx, _, depth, keys = kv.shape
    return pl.pallas_call(
        functools.partial(attend_kernel, group),
        name="attend",
        grid_spec=pltpu.PrefetchScalarGridSpec(
            num_scalar_prefetch=1,
            grid=(heads,),
            in_specs=[
                pl.BlockSpec((group * HEAD, rows), lambda g, i: (start + g, 0)),
                pl.BlockSpec((n_ctx, 2, HEAD, keys), lambda g, i: (0, 0, start + g, 0)),
            ],
            out_specs=[
                pl.BlockSpec((group * HEAD, rows), lambda g, i: (g, 0)),
                pl.BlockSpec((1, 8, rows), lambda g, i: (g, 0, 0)),
            ],
        ),
        out_shape=[
            jax.ShapeDtypeStruct((heads * group * HEAD, rows), BF),
            jax.ShapeDtypeStruct((heads, 8, rows), F32),
        ],
        compiler_params=pltpu.CompilerParams(vmem_limit_bytes=48 << 20),
        cost_estimate=pl.CostEstimate(
            flops=4 * heads * group * HEAD * rows * n_ctx * keys,
            transcendentals=heads * group * rows * n_ctx * keys,
            bytes_accessed=2 * q.size + kv.size,
        ),
    )(info, q, kv)


def attend_back_kernel(group, info_ref, q_ref, kv_ref, o_ref, do_ref, lse_ref, dq_ref, dkv_ref):
    count, first_row, length, ctx = info_ref[0], info_ref[1], info_ref[2], info_ref[3]
    n_ctx = kv_ref.shape[0]
    keys = kv_ref.shape[3]
    delta = []
    for h in range(group):
        part = slice(h * HEAD, (h + 1) * HEAD)
        delta.append(
            jnp.sum(do_ref[part, :].astype(F32) * o_ref[part, :].astype(F32), axis=0, keepdims=True)
        )
    dq_ref[...] = jnp.zeros_like(dq_ref)

    def step(j, last):
        slot = slot_of(j, ctx, n_ctx)
        k = kv_ref[slot, 0]
        v = kv_ref[slot, 1]
        dk = jnp.zeros((keys, HEAD), F32)
        dv = jnp.zeros((keys, HEAD), F32)
        for h in range(group):
            part = slice(h * HEAD, (h + 1) * HEAD)
            q = q_ref[part, :]
            do = do_ref[part, :]
            s = softmax_block(q, k, last, j * keys, first_row, length)
            p = jnp.exp(s - lse_ref[0, h : h + 1, :])
            dp = lax.dot_general(v, do, (((0,), (0,)), ((), ())), preferred_element_type=F32)
            ds = (p * (dp - delta[h])).astype(BF)
            pb = p.astype(BF)
            dv += lax.dot_general(pb, do, (((1,), (1,)), ((), ())), preferred_element_type=F32)
            dk += lax.dot_general(ds, q, (((1,), (1,)), ((), ())), preferred_element_type=F32)
            dq_ref[part, :] += jnp.dot(k, ds, preferred_element_type=F32)
        dkv_ref[slot, 0] = dk.T.astype(BF)
        dkv_ref[slot, 1] = dv.T.astype(BF)

    @pl.loop(0, count - 1)
    def _(j):
        step(j, False)

    step(count - 1, True)

    @pl.loop(count, n_ctx)
    def _(j):
        dkv_ref[slot_of(j, ctx, n_ctx)] = jnp.zeros(dkv_ref.shape[1:], BF)


def attend_back(q, kv, o, do, lse, info, group):
    rows = q.shape[1]
    n_ctx, _, depth, keys = kv.shape
    heads = depth // HEAD
    wide = pl.BlockSpec((group * HEAD, rows), lambda g, i: (g, 0))
    blocks = pl.BlockSpec((n_ctx, 2, HEAD, keys), lambda g, i: (0, 0, g, 0))
    return pl.pallas_call(
        functools.partial(attend_back_kernel, group),
        name="attend_back",
        grid_spec=pltpu.PrefetchScalarGridSpec(
            num_scalar_prefetch=1,
            grid=(heads,),
            in_specs=[
                wide,
                blocks,
                wide,
                wide,
                pl.BlockSpec((1, 8, rows), lambda g, i: (g, 0, 0)),
            ],
            out_specs=[wide, blocks],
        ),
        out_shape=[
            jax.ShapeDtypeStruct(q.shape, F32),
            jax.ShapeDtypeStruct(kv.shape, BF),
        ],
        compiler_params=pltpu.CompilerParams(vmem_limit_bytes=48 << 20),
        cost_estimate=pl.CostEstimate(
            flops=10 * q.shape[0] * rows * n_ctx * keys,
            transcendentals=q.shape[0] // HEAD * rows * n_ctx * keys,
            bytes_accessed=10 * q.size + 4 * kv.size,
        ),
    )(info, q, kv, o, do, lse)


def expert_kernel(info_ref, near_in, far_in, near_do, far_do, gate_ref, up_ref, down_ref, *refs):
    near_out, far_out, mix_out, act_out, dg_out, du_out = refs[:6]
    rows_x, rows_do, shares_in, mix_sum, back_sum, shares_out = refs[6:]
    e = pl.program_id(0)
    half, width = near_do.shape[2:]
    rows = 2 * half

    @pl.when(e == 0)
    def _():
        rows_x[:half, :] = near_in[:, :width]
        rows_x[half:, :] = far_in[:, :width]
        rows_do[:half, :] = near_do[0, 0]
        rows_do[half:, :] = far_do[0, 0]
        shares_in[:half, :] = near_in[:, width:].astype(F32)
        shares_in[half:, :] = far_in[:, width:].astype(F32)

    lanes = lax.broadcasted_iota(jnp.int32, (rows, 128), 1)
    x = rows_x[...]
    do = rows_do[...]
    per, _, hidden = gate_ref.shape
    mix = back = share = None
    for i in range(per):
        chosen = info_ref[0] + e * per + i
        gate, up, down = gate_ref[i], up_ref[i], down_ref[i]
        weight = jnp.sum(
            jnp.where((lanes == chosen) | (lanes == chosen + E), shares_in[...], 0.0),
            axis=1,
            keepdims=True,
        )
        g = jnp.dot(x, gate, preferred_element_type=F32)
        u = jnp.dot(x, up, preferred_element_type=F32)
        dact = dot(do, down, 1, 1)
        sig = jax.nn.sigmoid(g)
        silu = g * sig
        act = silu * u
        share_i = jnp.where(lanes == chosen, jnp.sum(act * dact, axis=1, keepdims=True), 0.0)
        dhid = dact * weight
        part = slice(i * hidden, (i + 1) * hidden)
        act_out[:, part] = (act * weight).astype(BF)
        dg_out[:, part] = (dhid * u * (sig * (1.0 + g * (1.0 - sig)))).astype(BF)
        du_out[:, part] = (dhid * silu).astype(BF)
        mix_i = jnp.dot(act_out[:, part], down, preferred_element_type=F32)
        back_i = dot(dg_out[:, part], gate, 1, 1) + dot(du_out[:, part], up, 1, 1)
        mix = mix_i if mix is None else mix + mix_i
        back = back_i if back is None else back + back_i
        share = share_i if share is None else share + share_i

    @pl.when(e == 0)
    def _():
        mix_sum[...] = mix
        back_sum[...] = back
        shares_out[...] = share

    @pl.when(e > 0)
    def _():
        mix_sum[...] += mix
        back_sum[...] += back
        shares_out[...] += share

    @pl.when(e == pl.num_programs(0) - 1)
    def _():
        near_out[:, :width] = back_sum[:half, :].astype(BF)
        near_out[:, width:] = shares_out[:half, :].astype(BF)
        far_out[:, :width] = back_sum[half:, :].astype(BF)
        far_out[:, width:] = shares_out[half:, :].astype(BF)
        mix_out[...] = mix_sum[...].astype(BF)


def experts(info, near, far, do_near, do_far, gate, up, down, weight):
    half, wide = near.shape
    width = do_near.shape[3]
    held, _, hidden = gate.shape
    rows = 2 * half
    whole = lambda shape: pl.BlockSpec(shape, lambda e, i: (0, 0))
    per = 1
    each = lambda shape: pl.BlockSpec((per,) + shape, lambda e, i: (e, 0, 0))
    column = pl.BlockSpec((rows, per * hidden), lambda e, i: (0, e))
    mid = jax.ShapeDtypeStruct((rows, held * hidden), BF)
    message = jax.ShapeDtypeStruct((half, wide), BF)
    return pl.pallas_call(
        expert_kernel,
        name="experts",
        grid_spec=pltpu.PrefetchScalarGridSpec(
            num_scalar_prefetch=1,
            grid=(held // per,),
            in_specs=[
                whole((half, wide)),
                whole((half, wide)),
                pl.BlockSpec((1, 1, half, width), lambda e, i: (i[3], i[4], 0, 0)),
                pl.BlockSpec((1, 1, half, width), lambda e, i: (i[5], i[4], 0, 0)),
                each((width, hidden)),
                each((width, hidden)),
                each((hidden, width)),
            ],
            out_specs=[
                whole((half, wide)),
                whole((half, wide)),
                whole((rows, width)),
                column,
                column,
                column,
            ],
            scratch_shapes=[
                pltpu.VMEM((rows, width), BF),
                pltpu.VMEM((rows, width), BF),
                pltpu.VMEM((rows, 128), F32),
                pltpu.VMEM((rows, width), F32),
                pltpu.VMEM((rows, width), F32),
                pltpu.VMEM((rows, 128), F32),
            ],
        ),
        out_shape=[
            message,
            message,
            jax.ShapeDtypeStruct((rows, width), BF),
            mid,
            mid,
            mid,
        ],
        compiler_params=pltpu.CompilerParams(vmem_limit_bytes=56 << 20),
        cost_estimate=pl.CostEstimate(
            flops=12 * weight * rows * width * held * hidden,
            transcendentals=rows * held * hidden,
            bytes_accessed=6 * held * hidden * width + 16 * rows * width,
        ),
    )(info, near, far, do_near, do_far, gate, up, down)


def expert_grad_kernel(count, info_ref, *refs):
    rows_x, rows_do = refs[: 2 * count], refs[2 * count : 4 * count]
    acts, dgs, dus = (refs[(4 + k) * count : (5 + k) * count] for k in range(3))
    out = refs[-1]
    width = rows_do[0].shape[-1]
    hidden = acts[0].shape[1]
    down = both = None
    for s in range(count):
        do = jnp.concatenate([rows_do[2 * s][0, 0], rows_do[2 * s + 1][0, 0]], axis=0)
        x = jnp.concatenate([rows_x[2 * s][:, :width], rows_x[2 * s + 1][:, :width]], axis=0)
        dgu = jnp.concatenate([dgs[s][...], dus[s][...]], axis=1)
        first, second = dot(acts[s][...], do, 0, 0), dot(dgu, x, 0, 0)
        down = first if down is None else down + first
        both = second if both is None else both + second
    out[0, 0] = down.astype(BF)
    out[0, 1] = both[:hidden].astype(BF)
    out[0, 2] = both[hidden:].astype(BF)


def expert_grads(info, chunks, do_all, acts, dgs, dus, held, start, count):
    n_z = len(acts)
    if n_z > 4:
        total = 0.0
        for b in range(0, n_z, 4):
            part = slice(b, b + 4)
            here = jnp.concatenate([info[:1], info[1 + b : 5 + b], info[1 + n_z :]])
            total = total + expert_grads(
                here,
                chunks[2 * b : 2 * b + 8],
                do_all,
                acts[part],
                dgs[part],
                dus[part],
                held,
                start,
                count,
            ).astype(F32)
        return total.astype(BF)
    size, width = do_all.shape[2:]
    wide = chunks[0].shape[1]
    rows, mid = acts[0].shape
    hidden = mid // held
    at = 1 + n_z + start
    chunk = pl.BlockSpec((size, wide), lambda e, i: (0, 0), pipeline_mode=pl.Buffered(1))
    do_chunk = lambda other, s: pl.BlockSpec(
        (1, 1, size, width),
        lambda e, i: ((1 - i[0]) if other else i[0], i[1 + s], 0, 0),
        pipeline_mode=pl.Buffered(1),
    )
    column = pl.BlockSpec((rows, hidden), lambda e, i: (0, i[at + e]))
    return pl.pallas_call(
        functools.partial(expert_grad_kernel, n_z),
        name="expert_grads",
        grid_spec=pltpu.PrefetchScalarGridSpec(
            num_scalar_prefetch=1,
            grid=(count,),
            in_specs=[chunk for _ in chunks]
            + [do_chunk(other, s) for s in range(n_z) for other in (False, True)]
            + [column] * (3 * n_z),
            out_specs=pl.BlockSpec((1, 3, hidden, width), lambda e, i: (e, 0, 0, 0)),
        ),
        out_shape=jax.ShapeDtypeStruct((count, 3, hidden, width), BF),
        compiler_params=pltpu.CompilerParams(vmem_limit_bytes=58 << 20),
        cost_estimate=pl.CostEstimate(
            flops=60 * n_z * rows * width * hidden * count,
            transcendentals=0,
            bytes_accessed=4 * n_z * rows * (width + hidden * count),
        ),
    )(info, *chunks, *([do_all] * (2 * n_z)), *acts, *dgs, *dus)


def place_kernel(count, info_ref, *refs):
    down, gate, up = refs[count:]
    for i, ref in enumerate(refs[:count]):

        @pl.when(pl.program_id(0) == i)
        def _():
            down[0] = ref[0, 0].astype(F32)
            gate[0] = ref[0, 1].astype(F32).T
            up[0] = ref[0, 2].astype(F32).T


def place(info, parts):
    hidden, width = parts[0][0].shape[2:]
    count = len(parts)
    out = lambda *shape: pl.BlockSpec((1,) + shape, lambda e, i: (i[e], 0, 0))
    return pl.pallas_call(
        functools.partial(place_kernel, count),
        name="place",
        grid_spec=pltpu.PrefetchScalarGridSpec(
            num_scalar_prefetch=1,
            grid=(count,),
            in_specs=[
                pl.BlockSpec((1, 3, hidden, width), lambda e, i, k=k: (k, 0, 0, 0)) for _, k in parts
            ],
            out_specs=[out(hidden, width), out(width, hidden), out(width, hidden)],
        ),
        out_shape=[
            jax.ShapeDtypeStruct((count, hidden, width), F32),
            jax.ShapeDtypeStruct((count, width, hidden), F32),
            jax.ShapeDtypeStruct((count, width, hidden), F32),
        ],
        compiler_params=pltpu.CompilerParams(vmem_limit_bytes=48 << 20),
        cost_estimate=pl.CostEstimate(
            flops=0, transcendentals=0, bytes_accessed=18 * count * hidden * width
        ),
    )(info, *[array for array, _ in parts])


def local(
    sizes,
    tokens,
    lengths,
    routes,
    visit_order,
    cotangent,
    first_gain,
    query_weight,
    key_matrix,
    value_matrix,
    output_weight,
    second_gain,
    router_weight,
    gate_weight,
    up_weight,
    down_weight,
):
    n_z, n_cx = sizes
    n_ctx = 2 * n_cx
    z = lax.axis_index("fsdp")
    cx = lax.axis_index("cx")
    core = lax.axis_index("core")
    tp = lax.axis_index("tp")
    ctx = cx * 2 + core
    rows, width = tokens.shape[1:]
    half = rows // 2
    shard = query_weight.shape[0]
    q_width = query_weight.shape[1]
    kv_width = key_matrix.shape[1]
    group = q_width // kv_width
    held = gate_weight.shape[0]
    hidden = gate_weight.shape[2]
    first_row = ctx * rows
    length = lengths[0]
    positions = first_row + jnp.arange(rows, dtype=jnp.int32)
    live = positions < length
    valid = live.astype(F32)[:, None]

    small = jnp.concatenate(
        [first_gain[None], second_gain[None], router_weight.T], axis=0
    )
    small_full = put(jnp.zeros((2 + E, width), BF), small, z * shard, 1)
    for s in range(1, n_z):
        small_full = put(small_full, shift(small, "fsdp", n_z, s), ((z + n_z - s) % n_z) * shard, 1)
    gain_first = small_full[0:1].astype(F32)
    gain_second = small_full[1:2].astype(F32)
    router = small_full[2:]

    grad_half = (pick(cotangent[0], tp, 2, 0).astype(F32) * pick(valid, tp, 2, 0)).astype(BF)
    grad_other = swap(grad_half, "tp")

    wide_split = n_cx == 2 and (shard // 4) % 16 == 0

    def bring(own, over_chips):
        piece = pick(own, ctx, n_ctx, 0) if over_chips else pick(own, core, 2, 0)
        return own, [shift(piece, "fsdp", n_z, s) for s in range(1, n_z)]

    def spread(own, got, over_chips):
        got = jnp.stack(got)[None]
        if over_chips:
            got = jnp.concatenate([got, swap(got, "cx")], axis=0)
        return own, got, swap(got, "core")

    kv_pieces = spread(*bring(jnp.concatenate([key_matrix, value_matrix], axis=1), False), False)
    q_own, q_got = bring(after(query_weight, kv_pieces[1]), wide_split)
    here = jnp.stack([z, core, cx]).astype(jnp.int32)

    routed, kept = keep_plan(routes[0], visit_order[0, 0], live)

    inputs = tokens[0].astype(F32)
    inverse_one, normed_one = normalize(inputs)
    hidden_one = after((normed_one * gain_first).astype(BF), grad_other)
    frequency = jnp.exp(
        jnp.arange(HEAD // 2, dtype=F32) * (-2.0 * math.log(10000.0) / HEAD)
    )
    angles = frequency[:, None] * positions.astype(F32)[None, :]
    cos, sin = jnp.cos(angles), jnp.sin(angles)
    scale = HEAD**-0.5
    kv_mine, w_kv = project(here, *kv_pieces, hidden_one, cos, sin, kv_width, 1.0)
    kv_mine = kv_mine.reshape(1, 2, kv_width, rows)
    near_kv = [kv_mine]
    for s in range(1, n_cx):
        near_kv.append(shift(near_kv[-1], "cx", n_cx))
    near_kv = jnp.concatenate(near_kv, axis=0)
    q_got = [after(v, near_kv) for v in q_got]
    q_pieces = spread(q_own, q_got, wide_split)
    o_own, o_got = bring(after(output_weight.T, *q_got), wide_split)
    grad_all = lax.all_gather(after(grad_half, *q_got), ("tp", "fsdp"))
    grad_all = grad_all.reshape(2, n_z, half, width)
    query, w_q = project(here, *q_pieces, hidden_one, cos, sin, q_width, scale)
    kv = jnp.concatenate([near_kv, swap(near_kv, "core")], axis=0)
    count = jnp.minimum(ctx + 1, (length + rows - 1) // rows)
    info = jnp.stack([count, first_row, length, ctx])
    kv_heads = kv_width // HEAD
    split = [(0, kv_heads // 2), (kv_heads // 2, kv_heads - kv_heads // 2)]
    early, early_lse = attend(after(query, grad_other), kv, info, group, *split[0])
    o_pieces = spread(o_own, [after(v, early) for v in o_got], wide_split)
    later, later_lse = attend(after(query, early), kv, info, group, *split[1])
    attended = jnp.concatenate([early, later], axis=0)
    lse = jnp.concatenate([early_lse, later_lse], axis=0)
    o_full = assembled(here, *[after(v, later) for v in o_pieces])

    far = dot(pick(attended, 1 - tp, 2, 1), o_full, 0, 1).astype(BF)
    near = dot(pick(attended, tp, 2, 1), o_full, 0, 1)
    residual = pick(tokens[0], tp, 2, 0).astype(F32) + near + swap(far, "tp").astype(F32)
    inverse_two, normed_two = normalize(residual)
    hidden_two = (normed_two * gain_second).astype(BF)
    logits = dot(hidden_two, router, 1, 1)
    routed_half = pick(routed, tp, 2, 0)
    kept_half = pick(kept, tp, 2, 0).astype(F32)
    masked = jnp.where(routed_half, logits, NEG)
    raised = jnp.where(
        routed_half, jnp.exp(masked - jnp.max(masked, axis=1, keepdims=True)), 0.0
    )
    gates = raised / jnp.sum(raised, axis=1, keepdims=True)
    weights = gates * kept_half

    high = weights.astype(BF)
    low = (weights - high.astype(F32)).astype(BF)
    message = jnp.concatenate(
        [hidden_two, high, low, jnp.zeros((half, 128 - 2 * E), BF)], axis=1
    )
    blocks = [(z + n_z - s) % n_z for s in range(n_z)]
    near = [message]
    far = [swap(message, "tp")]
    coming = shift(message, "fsdp", n_z)
    done, moving, joined = [], None, ()
    for s in range(n_z):
        first = near[s]
        if s + 1 < n_z:
            near.append(after(coming, *[d[0] for d in done[-1:]]))
            far.append(swap(near[-1], "tp"))
            first = after(first, near[-1])
            if s + 2 < n_z:
                coming = shift(near[-1], "fsdp", n_z)
        first = after(first, *joined)
        if s:
            info_s = [z * held, tp, blocks[s], tp, blocks[s], 1 - tp]
            rows_do = (grad_all, grad_all)
        else:
            info_s = [z * held, tp, blocks[s], 0, 0, 0]
            rows_do = (grad_half[None, None], grad_other[None, None])
        done.append(
            experts(
                jnp.stack([jnp.asarray(v, jnp.int32) for v in info_s]),
                first,
                far[s],
                *rows_do,
                gate_weight,
                up_weight,
                down_weight,
                10 if s else 1,
            )
        )
        if s > 1:
            part = done[s - 1][0].astype(F32) + swap(done[s - 1][1], "tp").astype(F32)
            if s > 2:
                part = shift(moving, "fsdp", n_z).astype(F32) + part
            moving = part.astype(BF)
            joined = (moving,)
    last = swap(done[-1][1], "tp")
    by_core = held % 2 == 0
    first_slot = held // 2 if by_core else 0
    slots = [((1 - core) * first_slot + k) % held for k in range(first_slot)]
    slots += [core * first_slot + k for k in range(held - first_slot)]
    order = jnp.stack([jnp.asarray(v, jnp.int32) for v in [tp] + blocks + slots])
    grad_args = (
        [v for s in range(n_z) for v in (near[s], far[s])],
        grad_all,
        [done[s][3] for s in range(n_z)],
        [done[s][4] for s in range(n_z)],
        [done[s][5] for s in range(n_z)],
        held,
    )
    theirs = expert_grads(after(order, moving), *grad_args, 0, first_slot) if by_core else None
    mix_moving = shift(done[1][2], "fsdp", n_z)
    part = done[-1][0].astype(F32) + after(last, theirs if by_core else moving).astype(F32)
    moving = (shift(moving, "fsdp", n_z).astype(F32) + part).astype(BF)
    own = done[0][0].astype(F32) + swap(after(done[0][1], last), "tp").astype(F32)
    mine = expert_grads(after(order, moving), *grad_args, first_slot, held - first_slot)
    back = shift(moving, "fsdp", n_z)

    if by_core:
        expert_half = mine.astype(F32) + after(swap(theirs, "core"), mine).astype(F32)
        expert_half = expert_half.astype(BF)
        expert_sum = lax.psum(expert_half, "cx")
        back, own = after(back, expert_half), after(own, expert_half)
    else:
        expert_sum = lax.psum(mine, ("cx", "core"))
    back = back.astype(F32) + own
    hidden_grad = back[:, :width]
    gate_grad = back[:, width : width + E] * kept_half

    logit_grad = (
        gates * (gate_grad - jnp.sum(gates * gate_grad, axis=1, keepdims=True))
    ).astype(BF)
    hidden_grad = hidden_grad + dot(logit_grad, router, 1, 0)
    grad_router = dot(logit_grad, hidden_two, 0, 0)
    grad_second = jnp.sum(hidden_grad * normed_two, axis=0, keepdims=True)
    branch_half = (
        grad_half.astype(F32) + norm_backward(hidden_grad, gain_second, inverse_two, normed_two)
    ).astype(BF)
    lead = tp == 0
    branch_other = swap(branch_half, "tp")
    branch = jnp.concatenate(
        [jnp.where(lead, branch_half, branch_other), jnp.where(lead, branch_other, branch_half)],
        axis=0,
    )

    attended_grad = dot(o_full, branch, 0, 1).astype(BF)
    grad_output = dot(branch, attended, 0, 1).astype(BF)
    attended_grad = after(attended_grad, grad_output)

    grad_query_rot, grad_kv = attend_back(
        query, kv, attended, attended_grad, lse, info, group
    )
    def mix_step(arrived, s, *others):
        return (after(arrived, *others).astype(F32) + done[s][2].astype(F32)).astype(BF)

    for s in range(2, n_z):
        mix_moving = mix_step(mix_moving, s, *((theirs,) if s == 2 and by_core else (grad_kv,)))
        mix_moving = shift(mix_moving, "fsdp", n_z)
    kv_sum = grad_kv[:n_cx].astype(F32) + swap(grad_kv[n_cx:], "core").astype(F32)
    kv_moving = kv_sum[1].astype(BF)
    for s in range(2, n_cx):
        kv_moving = (shift(kv_moving, "cx", n_cx).astype(F32) + kv_sum[s]).astype(BF)
    kv_far = shift(kv_moving, "cx", n_cx)
    query_grad = (rotate(grad_query_rot, cos, sin, True) * scale).astype(BF)

    def by_core_halves(v):
        blocks = v.reshape(n_z, v.shape[0] // n_z, v.shape[1])
        theirs = pick(blocks, 1 - core, 2, 1)
        return pick(blocks, core, 2, 1).astype(F32), theirs, swap(theirs, "core")

    def by_fsdp(mine, came, *others):
        half = (mine + after(came, *others).astype(F32)).astype(BF)
        return half, lax.all_to_all(half, "fsdp", 0, 0)

    def by_chip(came, *others):
        total = jnp.sum(after(came, *others).astype(F32), axis=0).astype(BF)
        return total, ring_gather(total[None], "cx", n_cx, 0)

    def whole_of(came, *others):
        total = jnp.sum(after(came, *others).astype(F32), axis=0).astype(BF)
        return core_join(total, 0).astype(F32)

    grad_q = dot(hidden_one, query_grad, 0, 1).astype(BF)
    o_mine, o_theirs, o_came = by_core_halves(grad_output)
    q_mine, q_theirs, q_came = by_core_halves(grad_q)
    started = anchor(kv_moving, o_theirs, q_theirs)
    o_half, o_came = by_fsdp(o_mine, o_came, started)
    q_half, q_came = by_fsdp(q_mine, q_came, started)
    started = anchor(started, o_half, q_half)

    kv_grad = after(kv_far, started).astype(F32) + kv_sum[0]
    key_grad = rotate(kv_grad[0], cos, sin, True).astype(BF)
    value_grad = kv_grad[1].astype(BF)
    grad_both = jnp.concatenate([key_grad, value_grad], axis=0)
    first_part = dot(query_grad, w_q, 0, 1) + dot(grad_both, w_kv, 0, 1)
    grad_first = jnp.sum(first_part * normed_one, axis=0, keepdims=True)
    first_low = first_part.astype(BF)
    first_other = swap(first_low, "tp")
    small_grad = jnp.concatenate([grad_first, grad_second, grad_router], axis=0)
    small_other = swap(small_grad, "tp")
    grad_kv_w = dot(hidden_one, grad_both, 0, 1).astype(BF)
    kv_mine, kv_theirs, kv_came = by_core_halves(grad_kv_w)
    started = anchor(first_low, small_grad, kv_theirs)
    kv_half, kv_came = by_fsdp(kv_mine, kv_came, started)
    small_grad = small_grad + after(small_other, started)
    small_other = swap(small_grad, "core")
    started = anchor(kv_half, small_grad)

    mixed = mix_step(mix_moving, 0, started)
    mix_other = swap(mixed[half:], "tp")
    o_total, o_came = by_chip(o_came, started)
    q_total, q_came = by_chip(q_came, started)
    small_grad = small_grad + after(small_other, started)
    everyone = ring_gather(small_grad[None], "cx", n_cx, 0)
    started = anchor(mixed, o_total, q_total, small_grad)

    first_grad = first_low.astype(F32) + after(first_other, started).astype(F32)
    grad_inputs = branch.astype(F32) + norm_backward(
        first_grad, gain_first, inverse_one, normed_one
    )
    mixture = mixed[:half].astype(F32) + after(mix_other, first_grad).astype(F32)
    out_half = (pick(valid, tp, 2, 0) * (residual + mixture)).astype(BF)
    out_other = swap(out_half, "tp")
    kv_total, kv_came = by_chip(kv_came, started)
    total = jnp.sum(after(everyone, started), axis=0)
    small_mine = jnp.sum(
        lax.all_to_all(total, "fsdp", 1, 0, tiled=True).reshape(n_z, 2 + E, shard), axis=0
    )
    parts = [(expert_sum, k) for k in range(held - first_slot)]
    if by_core:
        others = swap(after(expert_sum, started), "core")
        parts = [(others, k) for k in range(first_slot)] + parts
    grad_q = whole_of(q_came, started)
    grad_output = whole_of(o_came, started).T
    started = anchor(out_half, kv_total)
    grad_down, grad_gate, grad_up = place(order[1 + n_z :], parts)
    grad_kv_w = whole_of(kv_came, started)
    out_other = after(out_other, started)
    layer_out = jnp.concatenate(
        [jnp.where(lead, out_half, out_other), jnp.where(lead, out_other, out_half)], axis=0
    )

    return (
        layer_out[None],
        grad_inputs[None],
        small_mine[0],
        grad_q,
        grad_kv_w[:, :kv_width],
        grad_kv_w[:, kv_width:],
        grad_output,
        small_mine[1],
        small_mine[2:].T,
        grad_gate,
        grad_up,
        grad_down,
    )


def solution(mesh):
    n_z, n_ctx, n_tp = mesh.shape["fsdp"], mesh.shape["ctx"], mesh.shape["tp"]
    named = Mesh(
        mesh.devices.reshape(n_z, n_ctx // 2, 2, n_tp), ("fsdp", "cx", "core", "tp")
    )
    ctx = ("cx", "core")
    placed = (
        P("fsdp", ctx, None),
        P("fsdp"),
        P("fsdp", ctx, None),
        P("fsdp", ctx, None),
        P("fsdp", ctx, None),
        P("fsdp"),
        P("fsdp", "tp"),
        P("fsdp", "tp"),
        P("fsdp", "tp"),
        P("tp", "fsdp"),
        P("fsdp"),
        P("fsdp", None),
        P("fsdp", None, "tp"),
        P("fsdp", None, "tp"),
        P("fsdp", "tp", None),
    )
    return jax.shard_map(
        functools.partial(local, (n_z, n_ctx // 2)),
        mesh=named,
        in_specs=placed,
        out_specs=(
            P("fsdp", ctx, None),
            P("fsdp", ctx, None),
            P("fsdp"),
            P("fsdp", "tp"),
            P("fsdp", "tp"),
            P("fsdp", "tp"),
            P("tp", "fsdp"),
            P("fsdp"),
            P("fsdp", None),
            P("fsdp", None, "tp"),
            P("fsdp", None, "tp"),
            P("fsdp", "tp", None),
        ),
        check_vma=False,
    )
```

```python
import functools
import math

import jax
import jax.numpy as jnp
from jax import lax
from jax.experimental import pallas as pl
from jax.experimental.pallas import tpu as pltpu
from jax.sharding import Mesh
from jax.sharding import PartitionSpec as P

HEAD = 64
TOPK = 8
E = 16
CAP = 256
EPSILON = 1e-06
BF = jnp.bfloat16
F32 = jnp.float32
NEG = -1e30
FAR = 1e6


def dot(a, b, ca, cb):
    return lax.dot_general(a, b, (((ca,), (cb,)), ((), ())), preferred_element_type=F32)


def shift(v, axis, n, by=1):
    return lax.ppermute(v, axis, [(i, (i + by) % n) for i in range(n)])


def swap(v, axis):
    return lax.ppermute(v, axis, [(0, 1), (1, 0)])


def pick(v, index, parts, dim):
    size = v.shape[dim] // parts
    return lax.dynamic_slice_in_dim(v, index * size, size, dim)


def put(buffer, v, start, dim):
    return lax.dynamic_update_slice_in_dim(buffer, v, start, dim)


def after(v, *others):
    return lax.optimization_barrier((v,) + others)[0]


def anchor_kernel(in_ref, out_ref):
    out_ref[...] = in_ref[...]


def anchor(*others):
    token = after(jnp.zeros((8, 128), F32), *others)
    return pl.pallas_call(
        anchor_kernel,
        name="anchor",
        out_shape=jax.ShapeDtypeStruct((8, 128), F32),
        cost_estimate=pl.CostEstimate(flops=10**11, transcendentals=0, bytes_accessed=8192),
    )(token)


def direct_reduce(part, axis, n):
    me = lax.axis_index(axis)
    total = part(me)
    for s in range(1, n):
        total = total + shift(part((me + s) % n).astype(BF), axis, n, s).astype(F32)
    return total


def ring_reduce(part, axis, n, *others):
    me = lax.axis_index(axis)
    moving = part((me + n - 1) % n).astype(BF)
    for s in range(2, n):
        moving = (shift(moving, axis, n).astype(F32) + part((me + n - s) % n)).astype(BF)
    moving = shift(moving, axis, n)
    if others:
        moving = after(moving, *others)
    return moving.astype(F32) + part(me)


def core_halves(v, dim):
    core = lax.axis_index("core")
    mine = pick(v, core, 2, dim)
    theirs = pick(v, 1 - core, 2, dim)
    return mine.astype(F32) + swap(theirs.astype(BF), "core").astype(F32)


def core_join(v, dim):
    other = swap(v, "core")
    first = lax.axis_index("core") == 0
    return jnp.concatenate([jnp.where(first, v, other), jnp.where(first, other, v)], axis=dim)


def ring_gather(v, axis, n, dim):
    me = lax.axis_index(axis)
    size = v.shape[dim]
    shape = list(v.shape)
    shape[dim] = size * n
    out = put(jnp.zeros(shape, v.dtype), v, me * size, dim)
    moving = v
    for s in range(1, n):
        moving = shift(moving, axis, n)
        out = put(out, moving, ((me + n - s) % n) * size, dim)
    return out


def ctx_total(v, n_cx):
    half = core_halves(v, 0).astype(BF)
    part = ring_reduce(lambda j: pick(half, j, n_cx, 0).astype(F32), "cx", n_cx).astype(BF)
    return core_join(ring_gather(part, "cx", n_cx, 0), 0)


def normalize(values):
    inverse = lax.rsqrt(jnp.mean(values * values, axis=-1, keepdims=True) + EPSILON)
    return inverse, values * inverse


def norm_backward(grad, gain, inverse, normed):
    scaled = grad * gain
    return inverse * (scaled - normed * jnp.mean(scaled * normed, axis=-1, keepdims=True))


def rotate(v, cos, sin, inverse):
    rows = v.shape[1]
    shaped = v.reshape(-1, 2, HEAD // 2, rows)
    a, b = shaped[:, 0], shaped[:, 1]
    if inverse:
        out = jnp.stack([a * cos + b * sin, b * cos - a * sin], axis=1)
    else:
        out = jnp.stack([a * cos - b * sin, b * cos + a * sin], axis=1)
    return out.reshape(-1, rows)


def keep_plan(routes, order, live):
    rows = routes.shape[0]
    pairs = rows * TOPK
    token, choice = order // TOPK, order % TOPK
    rank = jnp.arange(pairs, dtype=jnp.int32)
    at_token = (jnp.arange(rows, dtype=jnp.int32)[:, None] == token[None, :]).astype(BF)
    at_choice = jnp.arange(TOPK, dtype=jnp.int32)[:, None] == choice[None, :]
    high = jnp.where(at_choice, (rank // 64)[None, :], 0).astype(BF)
    low = jnp.where(at_choice, (rank % 64)[None, :], 0).astype(BF)
    place = dot(at_token, jnp.concatenate([high, low], axis=0), 1, 1)
    place = place[:, :TOPK] * 64.0 + place[:, TOPK:]
    hits = routes[:, :, None] == jnp.arange(E, dtype=jnp.int32)[None, None, :]
    routed = jnp.any(hits, axis=1)
    place_e = jnp.sum(jnp.where(hits, place[:, :, None], 0.0), axis=1)
    place_e = jnp.where(routed & live[:, None], place_e, FAR)
    across = place_e.T
    earlier = jnp.sum((place_e[:, :, None] < across[None, :, :]).astype(F32), axis=0).T
    kept = routed & live[:, None] & (earlier < CAP)
    return routed, kept


def assemble(info_ref, own_ref, got_ref, other_ref, full_ref):
    z, core, cx = info_ref[0], info_ref[1], info_ref[2]
    rows = own_ref.shape[0]
    chips, steps, piece, _ = got_ref.shape
    n_z = steps + 1
    full_ref[pl.ds(pl.multiple_of(z * rows, piece), rows), :] = own_ref[...]
    for k in range(chips):
        chip = (cx + chips - k) % chips
        for s in range(1, n_z):
            start = ((z + n_z - s) % n_z) * rows + chip * 2 * piece
            mine = pl.multiple_of(start + core * piece, piece)
            theirs = pl.multiple_of(start + (1 - core) * piece, piece)
            full_ref[pl.ds(mine, piece), :] = got_ref[k, s - 1]
            full_ref[pl.ds(theirs, piece), :] = other_ref[k, s - 1]


def project_kernel(turned, scale, info_ref, own_ref, got_ref, other_ref, x_ref, cos_ref, sin_ref, out_ref, full_ref):
    assemble(info_ref, own_ref, got_ref, other_ref, full_ref)
    flat = jnp.dot(x_ref[...], full_ref[...], preferred_element_type=F32).T
    cos, sin = cos_ref[...], sin_ref[...]
    quarter = HEAD // 2
    for start in range(0, turned, HEAD):
        a = flat[start : start + quarter, :]
        b = flat[start + quarter : start + HEAD, :]
        out_ref[start : start + quarter, :] = ((a * cos - b * sin).astype(BF) * scale).astype(BF)
        out_ref[start + quarter : start + HEAD, :] = ((b * cos + a * sin).astype(BF) * scale).astype(BF)
    if turned < flat.shape[0]:
        out_ref[turned:, :] = flat[turned:, :].astype(BF)


def project(info, own, got, other, x, cos, sin, turned, scale):
    columns = own.shape[1]
    rows, width = x.shape
    return pl.pallas_call(
        functools.partial(project_kernel, turned, scale),
        name="project",
        grid_spec=pltpu.PrefetchScalarGridSpec(num_scalar_prefetch=1, grid=(1,),
            in_specs=[pl.BlockSpec(v.shape, lambda i, n, k=v.ndim: (0,) * k) for v in (own, got, other, x, cos, sin)],
            out_specs=[
                pl.BlockSpec((columns, rows), lambda i, n: (0, 0)),
                pl.BlockSpec((width, columns), lambda i, n: (0, 0)),
            ],
        ),
        out_shape=[
            jax.ShapeDtypeStruct((columns, rows), BF),
            jax.ShapeDtypeStruct((width, columns), BF),
        ],
        compiler_params=pltpu.CompilerParams(vmem_limit_bytes=40 << 20),
        cost_estimate=pl.CostEstimate(
            flops=2 * rows * width * columns,
            transcendentals=0,
            bytes_accessed=4 * width * columns + 2 * rows * (width + columns),
        ),
    )(info, own, got, other, x, cos, sin)


def assembled(info, own, got, other):
    rows, columns = own.shape
    full = (rows * (got.shape[1] + 1), columns)
    return pl.pallas_call(
        assemble,
        name="assembled",
        grid_spec=pltpu.PrefetchScalarGridSpec(num_scalar_prefetch=1, grid=(1,),
            in_specs=[pl.BlockSpec(v.shape, lambda i, n, k=v.ndim: (0,) * k) for v in (own, got, other)],
            out_specs=pl.BlockSpec(full, lambda i, n: (0, 0)),
        ),
        out_shape=jax.ShapeDtypeStruct(full, BF),
        compiler_params=pltpu.CompilerParams(vmem_limit_bytes=32 << 20),
        cost_estimate=pl.CostEstimate(flops=0, transcendentals=0, bytes_accessed=4 * rows * columns * 4),
    )(info, own, got, other)


def softmax_block(q, k, last, base, first_row, length):
    s = lax.dot_general(k, q, (((0,), (0,)), ((), ())), preferred_element_type=F32)
    if last:
        key = base + lax.broadcasted_iota(jnp.int32, s.shape, 0)
        query = first_row + lax.broadcasted_iota(jnp.int32, s.shape, 1)
        s = jnp.where((key <= query) & (key < length), s, NEG)
    return s


def slot_of(block, ctx, n_ctx):
    n_cx = n_ctx // 2
    steps = (ctx // 2 + n_cx - block // 2) % n_cx
    return ((ctx + block) % 2) * n_cx + steps


def attend_kernel(group, info_ref, q_ref, kv_ref, o_ref, lse_ref):
    count, first_row, length, ctx = info_ref[0], info_ref[1], info_ref[2], info_ref[3]
    rows = q_ref.shape[1]
    n_ctx = kv_ref.shape[0]
    keys = kv_ref.shape[3]
    for h in range(group):
        q = q_ref[h * HEAD : (h + 1) * HEAD, :]

        def step(j, carry, last):
            top, total, acc = carry
            slot = slot_of(j, ctx, n_ctx)
            k = kv_ref[slot, 0]
            v = kv_ref[slot, 1]
            s = softmax_block(q, k, last, j * keys, first_row, length)
            new_top = jnp.maximum(top, jnp.max(s, axis=0, keepdims=True))
            p = jnp.exp(s - new_top)
            fade = jnp.exp(top - new_top)
            total = total * fade + jnp.sum(p, axis=0, keepdims=True)
            acc = acc * fade + jnp.dot(v, p.astype(BF), preferred_element_type=F32)
            return new_top, total, acc

        carry = (
            jnp.full((1, rows), NEG, F32),
            jnp.zeros((1, rows), F32),
            jnp.zeros((HEAD, rows), F32),
        )
        carry = lax.fori_loop(0, count - 1, functools.partial(step, last=False), carry)
        top, total, acc = step(count - 1, carry, True)
        o_ref[h * HEAD : (h + 1) * HEAD, :] = (acc / total).astype(BF)
        lse_ref[0, h : h + 1, :] = top + jnp.log(total)


def attend(q, kv, info, group, start, heads):
    rows = q.shape[1]
    n_ctx, _, depth, keys = kv.shape
    return pl.pallas_call(
        functools.partial(attend_kernel, group),
        name="attend",
        grid_spec=pltpu.PrefetchScalarGridSpec(
            num_scalar_prefetch=1,
            grid=(heads,),
            in_specs=[
                pl.BlockSpec((group * HEAD, rows), lambda g, i: (start + g, 0)),
                pl.BlockSpec((n_ctx, 2, HEAD, keys), lambda g, i: (0, 0, start + g, 0)),
            ],
            out_specs=[
                pl.BlockSpec((group * HEAD, rows), lambda g, i: (g, 0)),
                pl.BlockSpec((1, 8, rows), lambda g, i: (g, 0, 0)),
            ],
        ),
        out_shape=[
            jax.ShapeDtypeStruct((heads * group * HEAD, rows), BF),
            jax.ShapeDtypeStruct((heads, 8, rows), F32),
        ],
        compiler_params=pltpu.CompilerParams(vmem_limit_bytes=48 << 20),
        cost_estimate=pl.CostEstimate(
            flops=4 * heads * group * HEAD * rows * n_ctx * keys,
            transcendentals=heads * group * rows * n_ctx * keys,
            bytes_accessed=2 * q.size + kv.size,
        ),
    )(info, q, kv)


def attend_back_kernel(group, info_ref, q_ref, kv_ref, o_ref, do_ref, lse_ref, dq_ref, dkv_ref):
    count, first_row, length, ctx = info_ref[0], info_ref[1], info_ref[2], info_ref[3]
    n_ctx = kv_ref.shape[0]
    keys = kv_ref.shape[3]
    delta = []
    for h in range(group):
        part = slice(h * HEAD, (h + 1) * HEAD)
        delta.append(
            jnp.sum(do_ref[part, :].astype(F32) * o_ref[part, :].astype(F32), axis=0, keepdims=True)
        )
    dq_ref[...] = jnp.zeros_like(dq_ref)

    def step(j, last):
        slot = slot_of(j, ctx, n_ctx)
        k = kv_ref[slot, 0]
        v = kv_ref[slot, 1]
        dk = jnp.zeros((keys, HEAD), F32)
        dv = jnp.zeros((keys, HEAD), F32)
        for h in range(group):
            part = slice(h * HEAD, (h + 1) * HEAD)
            q = q_ref[part, :]
            do = do_ref[part, :]
            s = softmax_block(q, k, last, j * keys, first_row, length)
            p = jnp.exp(s - lse_ref[0, h : h + 1, :])
            dp = lax.dot_general(v, do, (((0,), (0,)), ((), ())), preferred_element_type=F32)
            ds = (p * (dp - delta[h])).astype(BF)
            pb = p.astype(BF)
            dv += lax.dot_general(pb, do, (((1,), (1,)), ((), ())), preferred_element_type=F32)
            dk += lax.dot_general(ds, q, (((1,), (1,)), ((), ())), preferred_element_type=F32)
            dq_ref[part, :] += jnp.dot(k, ds, preferred_element_type=F32)
        dkv_ref[slot, 0] = dk.T.astype(BF)
        dkv_ref[slot, 1] = dv.T.astype(BF)

    @pl.loop(0, count - 1)
    def _(j):
        step(j, False)

    step(count - 1, True)

    @pl.loop(count, n_ctx)
    def _(j):
        dkv_ref[slot_of(j, ctx, n_ctx)] = jnp.zeros(dkv_ref.shape[1:], BF)


def attend_back(q, kv, o, do, lse, info, group):
    rows = q.shape[1]
    n_ctx, _, depth, keys = kv.shape
    heads = depth // HEAD
    wide = pl.BlockSpec((group * HEAD, rows), lambda g, i: (g, 0))
    blocks = pl.BlockSpec((n_ctx, 2, HEAD, keys), lambda g, i: (0, 0, g, 0))
    return pl.pallas_call(
        functools.partial(attend_back_kernel, group),
        name="attend_back",
        grid_spec=pltpu.PrefetchScalarGridSpec(
            num_scalar_prefetch=1,
            grid=(heads,),
            in_specs=[
                wide,
                blocks,
                wide,
                wide,
                pl.BlockSpec((1, 8, rows), lambda g, i: (g, 0, 0)),
            ],
            out_specs=[wide, blocks],
        ),
        out_shape=[
            jax.ShapeDtypeStruct(q.shape, F32),
            jax.ShapeDtypeStruct(kv.shape, BF),
        ],
        compiler_params=pltpu.CompilerParams(vmem_limit_bytes=48 << 20),
        cost_estimate=pl.CostEstimate(
            flops=10 * q.shape[0] * rows * n_ctx * keys,
            transcendentals=q.shape[0] // HEAD * rows * n_ctx * keys,
            bytes_accessed=10 * q.size + 4 * kv.size,
        ),
    )(info, q, kv, o, do, lse)


def expert_kernel(info_ref, near_in, far_in, near_do, far_do, gate_ref, up_ref, down_ref, *refs):
    near_out, far_out, mix_out, act_out, dg_out, du_out = refs[:6]
    rows_x, rows_do, shares_in, mix_sum, back_sum, shares_out = refs[6:]
    e = pl.program_id(0)
    half, width = near_do.shape[2:]
    rows = 2 * half

    @pl.when(e == 0)
    def _():
        rows_x[:half, :] = near_in[:, :width]
        rows_x[half:, :] = far_in[:, :width]
        rows_do[:half, :] = near_do[0, 0]
        rows_do[half:, :] = far_do[0, 0]
        shares_in[:half, :] = near_in[:, width:].astype(F32)
        shares_in[half:, :] = far_in[:, width:].astype(F32)

    lanes = lax.broadcasted_iota(jnp.int32, (rows, 128), 1)
    x = rows_x[...]
    do = rows_do[...]
    per, _, hidden = gate_ref.shape
    mix = back = share = None
    for i in range(per):
        chosen = info_ref[0] + e * per + i
        gate, up, down = gate_ref[i], up_ref[i], down_ref[i]
        weight = jnp.sum(
            jnp.where((lanes == chosen) | (lanes == chosen + E), shares_in[...], 0.0),
            axis=1,
            keepdims=True,
        )
        g = jnp.dot(x, gate, preferred_element_type=F32)
        u = jnp.dot(x, up, preferred_element_type=F32)
        dact = dot(do, down, 1, 1)
        sig = jax.nn.sigmoid(g)
        silu = g * sig
        act = silu * u
        share_i = jnp.where(lanes == chosen, jnp.sum(act * dact, axis=1, keepdims=True), 0.0)
        dhid = dact * weight
        part = slice(i * hidden, (i + 1) * hidden)
        act_out[:, part] = (act * weight).astype(BF)
        dg_out[:, part] = (dhid * u * (sig * (1.0 + g * (1.0 - sig)))).astype(BF)
        du_out[:, part] = (dhid * silu).astype(BF)
        mix_i = jnp.dot(act_out[:, part], down, preferred_element_type=F32)
        back_i = dot(dg_out[:, part], gate, 1, 1) + dot(du_out[:, part], up, 1, 1)
        mix = mix_i if mix is None else mix + mix_i
        back = back_i if back is None else back + back_i
        share = share_i if share is None else share + share_i

    @pl.when(e == 0)
    def _():
        mix_sum[...] = mix
        back_sum[...] = back
        shares_out[...] = share

    @pl.when(e > 0)
    def _():
        mix_sum[...] += mix
        back_sum[...] += back
        shares_out[...] += share

    @pl.when(e == pl.num_programs(0) - 1)
    def _():
        near_out[:, :width] = back_sum[:half, :].astype(BF)
        near_out[:, width:] = shares_out[:half, :].astype(BF)
        far_out[:, :width] = back_sum[half:, :].astype(BF)
        far_out[:, width:] = shares_out[half:, :].astype(BF)
        mix_out[...] = mix_sum[...].astype(BF)


def experts(info, near, far, do_near, do_far, gate, up, down, weight):
    half, wide = near.shape
    width = do_near.shape[3]
    held, _, hidden = gate.shape
    rows = 2 * half
    whole = lambda shape: pl.BlockSpec(shape, lambda e, i: (0, 0))
    per = 1
    each = lambda shape: pl.BlockSpec((per,) + shape, lambda e, i: (e, 0, 0))
    column = pl.BlockSpec((rows, per * hidden), lambda e, i: (0, e))
    mid = jax.ShapeDtypeStruct((rows, held * hidden), BF)
    message = jax.ShapeDtypeStruct((half, wide), BF)
    return pl.pallas_call(
        expert_kernel,
        name="experts",
        grid_spec=pltpu.PrefetchScalarGridSpec(
            num_scalar_prefetch=1,
            grid=(held // per,),
            in_specs=[
                whole((half, wide)),
                whole((half, wide)),
                pl.BlockSpec((1, 1, half, width), lambda e, i: (i[3], i[4], 0, 0)),
                pl.BlockSpec((1, 1, half, width), lambda e, i: (i[5], i[4], 0, 0)),
                each((width, hidden)),
                each((width, hidden)),
                each((hidden, width)),
            ],
            out_specs=[
                whole((half, wide)),
                whole((half, wide)),
                whole((rows, width)),
                column,
                column,
                column,
            ],
            scratch_shapes=[
                pltpu.VMEM((rows, width), BF),
                pltpu.VMEM((rows, width), BF),
                pltpu.VMEM((rows, 128), F32),
                pltpu.VMEM((rows, width), F32),
                pltpu.VMEM((rows, width), F32),
                pltpu.VMEM((rows, 128), F32),
            ],
        ),
        out_shape=[
            message,
            message,
            jax.ShapeDtypeStruct((rows, width), BF),
            mid,
            mid,
            mid,
        ],
        compiler_params=pltpu.CompilerParams(vmem_limit_bytes=56 << 20),
        cost_estimate=pl.CostEstimate(
            flops=12 * weight * rows * width * held * hidden,
            transcendentals=rows * held * hidden,
            bytes_accessed=6 * held * hidden * width + 16 * rows * width,
        ),
    )(info, near, far, do_near, do_far, gate, up, down)


def expert_grad_kernel(count, info_ref, *refs):
    rows_x, rows_do = refs[: 2 * count], refs[2 * count : 4 * count]
    acts, dgs, dus = (refs[(4 + k) * count : (5 + k) * count] for k in range(3))
    out = refs[-1]
    width = rows_do[0].shape[-1]
    hidden = acts[0].shape[1]
    down = both = None
    for s in range(count):
        do = jnp.concatenate([rows_do[2 * s][0, 0], rows_do[2 * s + 1][0, 0]], axis=0)
        x = jnp.concatenate([rows_x[2 * s][:, :width], rows_x[2 * s + 1][:, :width]], axis=0)
        dgu = jnp.concatenate([dgs[s][...], dus[s][...]], axis=1)
        first, second = dot(acts[s][...], do, 0, 0), dot(dgu, x, 0, 0)
        down = first if down is None else down + first
        both = second if both is None else both + second
    out[0, 0] = down.astype(BF)
    out[0, 1] = both[:hidden].astype(BF)
    out[0, 2] = both[hidden:].astype(BF)


def expert_grads(info, chunks, do_all, acts, dgs, dus, held, start, count):
    n_z = len(acts)
    if n_z > 4:
        total = 0.0
        for b in range(0, n_z, 4):
            part = slice(b, b + 4)
            here = jnp.concatenate([info[:1], info[1 + b : 5 + b], info[1 + n_z :]])
            total = total + expert_grads(
                here,
                chunks[2 * b : 2 * b + 8],
                do_all,
                acts[part],
                dgs[part],
                dus[part],
                held,
                start,
                count,
            ).astype(F32)
        return total.astype(BF)
    size, width = do_all.shape[2:]
    wide = chunks[0].shape[1]
    rows, mid = acts[0].shape
    hidden = mid // held
    at = 1 + n_z + start
    chunk = pl.BlockSpec((size, wide), lambda e, i: (0, 0), pipeline_mode=pl.Buffered(1))
    do_chunk = lambda other, s: pl.BlockSpec(
        (1, 1, size, width),
        lambda e, i: ((1 - i[0]) if other else i[0], i[1 + s], 0, 0),
        pipeline_mode=pl.Buffered(1),
    )
    column = pl.BlockSpec((rows, hidden), lambda e, i: (0, i[at + e]))
    return pl.pallas_call(
        functools.partial(expert_grad_kernel, n_z),
        name="expert_grads",
        grid_spec=pltpu.PrefetchScalarGridSpec(
            num_scalar_prefetch=1,
            grid=(count,),
            in_specs=[chunk for _ in chunks]
            + [do_chunk(other, s) for s in range(n_z) for other in (False, True)]
            + [column] * (3 * n_z),
            out_specs=pl.BlockSpec((1, 3, hidden, width), lambda e, i: (e, 0, 0, 0)),
        ),
        out_shape=jax.ShapeDtypeStruct((count, 3, hidden, width), BF),
        compiler_params=pltpu.CompilerParams(vmem_limit_bytes=58 << 20),
        cost_estimate=pl.CostEstimate(
            flops=60 * n_z * rows * width * hidden * count,
            transcendentals=0,
            bytes_accessed=4 * n_z * rows * (width + hidden * count),
        ),
    )(info, *chunks, *([do_all] * (2 * n_z)), *acts, *dgs, *dus)


def place_kernel(count, info_ref, *refs):
    down, gate, up = refs[count:]
    for i, ref in enumerate(refs[:count]):

        @pl.when(pl.program_id(0) == i)
        def _():
            down[0] = ref[0, 0].astype(F32)
            gate[0] = ref[0, 1].astype(F32).T
            up[0] = ref[0, 2].astype(F32).T


def place(info, parts):
    hidden, width = parts[0][0].shape[2:]
    count = len(parts)
    out = lambda *shape: pl.BlockSpec((1,) + shape, lambda e, i: (i[e], 0, 0))
    return pl.pallas_call(
        functools.partial(place_kernel, count),
        name="place",
        grid_spec=pltpu.PrefetchScalarGridSpec(
            num_scalar_prefetch=1,
            grid=(count,),
            in_specs=[
                pl.BlockSpec((1, 3, hidden, width), lambda e, i, k=k: (k, 0, 0, 0)) for _, k in parts
            ],
            out_specs=[out(hidden, width), out(width, hidden), out(width, hidden)],
        ),
        out_shape=[
            jax.ShapeDtypeStruct((count, hidden, width), F32),
            jax.ShapeDtypeStruct((count, width, hidden), F32),
            jax.ShapeDtypeStruct((count, width, hidden), F32),
        ],
        compiler_params=pltpu.CompilerParams(vmem_limit_bytes=48 << 20),
        cost_estimate=pl.CostEstimate(
            flops=0, transcendentals=0, bytes_accessed=18 * count * hidden * width
        ),
    )(info, *[array for array, _ in parts])


def local(
    sizes,
    tokens,
    lengths,
    routes,
    visit_order,
    cotangent,
    first_gain,
    query_weight,
    key_matrix,
    value_matrix,
    output_weight,
    second_gain,
    router_weight,
    gate_weight,
    up_weight,
    down_weight,
):
    n_z, n_cx = sizes
    n_ctx = 2 * n_cx
    z = lax.axis_index("fsdp")
    cx = lax.axis_index("cx")
    core = lax.axis_index("core")
    tp = lax.axis_index("tp")
    ctx = cx * 2 + core
    rows, width = tokens.shape[1:]
    half = rows // 2
    shard = query_weight.shape[0]
    q_width = query_weight.shape[1]
    kv_width = key_matrix.shape[1]
    group = q_width // kv_width
    held = gate_weight.shape[0]
    hidden = gate_weight.shape[2]
    first_row = ctx * rows
    length = lengths[0]
    positions = first_row + jnp.arange(rows, dtype=jnp.int32)
    live = positions < length
    valid = live.astype(F32)[:, None]

    wide_split = n_cx == 2 and (shard // 4) % 16 == 0

    def bring(own, over_chips):
        piece = pick(own, ctx, n_ctx, 0) if over_chips else pick(own, core, 2, 0)
        return own, [shift(piece, "fsdp", n_z, s) for s in range(1, n_z)]

    def spread(own, got, over_chips):
        got = jnp.stack(got)[None]
        if over_chips:
            got = jnp.concatenate([got, swap(got, "cx")], axis=0)
        return own, got, swap(got, "core")

    kv_own, kv_got = bring(jnp.concatenate([key_matrix, value_matrix], axis=1), False)

    small = jnp.concatenate([first_gain[None], second_gain[None], router_weight.T], axis=0)
    small_full = lax.all_to_all(jnp.broadcast_to(small[None], (n_z, 2 + E, shard)), "fsdp", 0, 0)
    small_full = jnp.transpose(small_full, (1, 0, 2)).reshape(2 + E, width)
    gain_first = small_full[0:1].astype(F32)
    gain_second = small_full[1:2].astype(F32)
    router = small_full[2:]

    grad_half = (pick(cotangent[0], tp, 2, 0).astype(F32) * pick(valid, tp, 2, 0)).astype(BF)
    grad_other = swap(grad_half, "tp")

    kv_pieces = spread(kv_own, kv_got, False)
    q_own, q_got = bring(after(query_weight, *kv_got), wide_split)
    started = anchor(*kv_got)
    kv_pieces = (kv_own, kv_pieces[1], after(kv_pieces[2], started))
    here = jnp.stack([z, core, cx]).astype(jnp.int32)

    routed, kept = keep_plan(routes[0], visit_order[0, 0], live)

    inputs = tokens[0].astype(F32)
    inverse_one, normed_one = normalize(inputs)
    hidden_one = after((normed_one * gain_first).astype(BF), grad_other)
    frequency = jnp.exp(
        jnp.arange(HEAD // 2, dtype=F32) * (-2.0 * math.log(10000.0) / HEAD)
    )
    angles = frequency[:, None] * positions.astype(F32)[None, :]
    cos, sin = jnp.cos(angles), jnp.sin(angles)
    scale = HEAD**-0.5
    kv_mine, w_kv = project(here, *kv_pieces, hidden_one, cos, sin, kv_width, 1.0)
    kv_mine = kv_mine.reshape(1, 2, kv_width, rows)
    near_kv = [kv_mine]
    for s in range(1, n_cx):
        near_kv.append(shift(near_kv[-1], "cx", n_cx))
    near_kv = jnp.concatenate([near_kv[0]] + [after(v, anchor(kv_mine)) for v in near_kv[1:]], axis=0)
    started = anchor(kv_mine)
    q_got = [after(v, started) for v in q_got]
    q_pieces = spread(q_own, q_got, wide_split)
    o_own, o_got = bring(after(output_weight.T, *q_got), wide_split)
    grad_all = lax.all_gather(after(grad_half, *q_got), ("tp", "fsdp"))
    grad_all = grad_all.reshape(2, n_z, half, width)
    query, w_q = project(here, *q_pieces, hidden_one, cos, sin, q_width, scale)
    kv = jnp.concatenate([near_kv, swap(near_kv, "core")], axis=0)
    count = jnp.minimum(ctx + 1, (length + rows - 1) // rows)
    info = jnp.stack([count, first_row, length, ctx])
    kv_heads = kv_width // HEAD
    split = [(0, kv_heads // 2), (kv_heads // 2, kv_heads - kv_heads // 2)]
    early, early_lse = attend(after(query, grad_other), kv, info, group, *split[0])
    o_pieces = spread(o_own, [after(v, early) for v in o_got], wide_split)
    later, later_lse = attend(after(query, early), kv, info, group, *split[1])
    attended = jnp.concatenate([early, later], axis=0)
    lse = jnp.concatenate([early_lse, later_lse], axis=0)
    o_full = assembled(here, *[after(v, later) for v in o_pieces])

    far = dot(pick(attended, 1 - tp, 2, 1), o_full, 0, 1).astype(BF)
    near = dot(pick(attended, tp, 2, 1), o_full, 0, 1)
    residual = pick(tokens[0], tp, 2, 0).astype(F32) + near + swap(far, "tp").astype(F32)
    inverse_two, normed_two = normalize(residual)
    hidden_two = (normed_two * gain_second).astype(BF)
    logits = dot(hidden_two, router, 1, 1)
    routed_half = pick(routed, tp, 2, 0)
    kept_half = pick(kept, tp, 2, 0).astype(F32)
    masked = jnp.where(routed_half, logits, NEG)
    raised = jnp.where(
        routed_half, jnp.exp(masked - jnp.max(masked, axis=1, keepdims=True)), 0.0
    )
    gates = raised / jnp.sum(raised, axis=1, keepdims=True)
    weights = gates * kept_half

    high = weights.astype(BF)
    low = (weights - high.astype(F32)).astype(BF)
    message = jnp.concatenate(
        [hidden_two, high, low, jnp.zeros((half, 128 - 2 * E), BF)], axis=1
    )
    blocks = [(z + n_z - s) % n_z for s in range(n_z)]
    near = [message]
    far = [swap(message, "tp")]
    coming = shift(message, "fsdp", n_z)
    done, moving, joined = [], None, ()
    for s in range(n_z):
        first = near[s]
        if s + 1 < n_z:
            near.append(after(coming, *[d[0] for d in done[-1:]]))
            far.append(swap(near[-1], "tp"))
            first = after(first, near[-1])
            if s + 2 < n_z:
                coming = shift(near[-1], "fsdp", n_z)
        first = after(first, *joined)
        if s:
            info_s = [z * held, tp, blocks[s], tp, blocks[s], 1 - tp]
            rows_do = (grad_all, grad_all)
        else:
            info_s = [z * held, tp, blocks[s], 0, 0, 0]
            rows_do = (grad_half[None, None], grad_other[None, None])
        done.append(
            experts(
                jnp.stack([jnp.asarray(v, jnp.int32) for v in info_s]),
                first,
                far[s],
                *rows_do,
                gate_weight,
                up_weight,
                down_weight,
                10 if s else 1,
            )
        )
        if s > 1:
            part = done[s - 1][0].astype(F32) + swap(done[s - 1][1], "tp").astype(F32)
            if s > 2:
                part = shift(moving, "fsdp", n_z).astype(F32) + part
            moving = part.astype(BF)
            joined = (moving,)
    last = swap(done[-1][1], "tp")
    by_core = held % 2 == 0
    first_slot = held // 2 if by_core else 0
    slots = [((1 - core) * first_slot + k) % held for k in range(first_slot)]
    slots += [core * first_slot + k for k in range(held - first_slot)]
    order = jnp.stack([jnp.asarray(v, jnp.int32) for v in [tp] + blocks + slots])
    grad_args = (
        [v for s in range(n_z) for v in (near[s], far[s])],
        grad_all,
        [done[s][3] for s in range(n_z)],
        [done[s][4] for s in range(n_z)],
        [done[s][5] for s in range(n_z)],
        held,
    )
    theirs = expert_grads(after(order, moving), *grad_args, 0, first_slot) if by_core else None
    mix_moving = shift(done[1][2], "fsdp", n_z)
    part = done[-1][0].astype(F32) + after(last, theirs if by_core else moving).astype(F32)
    moving = (shift(moving, "fsdp", n_z).astype(F32) + part).astype(BF)
    own = done[0][0].astype(F32) + swap(after(done[0][1], last), "tp").astype(F32)
    mine = expert_grads(after(order, moving), *grad_args, first_slot, held - first_slot)
    back = shift(moving, "fsdp", n_z)

    if by_core:
        expert_half = mine.astype(F32) + after(swap(theirs, "core"), mine).astype(F32)
        expert_half = expert_half.astype(BF)
        expert_sum = lax.psum(expert_half, "cx")
        back, own = after(back, expert_half), after(own, expert_half)
    else:
        expert_sum = lax.psum(mine, ("cx", "core"))
    back = back.astype(F32) + own
    hidden_grad = back[:, :width]
    gate_grad = back[:, width : width + E] * kept_half

    logit_grad = (
        gates * (gate_grad - jnp.sum(gates * gate_grad, axis=1, keepdims=True))
    ).astype(BF)
    hidden_grad = hidden_grad + dot(logit_grad, router, 1, 0)
    grad_router = dot(logit_grad, hidden_two, 0, 0)
    grad_second = jnp.sum(hidden_grad * normed_two, axis=0, keepdims=True)
    branch_half = (
        grad_half.astype(F32) + norm_backward(hidden_grad, gain_second, inverse_two, normed_two)
    ).astype(BF)
    lead = tp == 0
    branch_other = swap(branch_half, "tp")
    branch = jnp.concatenate(
        [jnp.where(lead, branch_half, branch_other), jnp.where(lead, branch_other, branch_half)],
        axis=0,
    )

    attended_grad = dot(o_full, branch, 0, 1).astype(BF)
    grad_output = dot(branch, attended, 0, 1).astype(BF)
    attended_grad = after(attended_grad, grad_output)

    grad_query_rot, grad_kv = attend_back(
        query, kv, attended, attended_grad, lse, info, group
    )
    def mix_step(arrived, s, *others):
        return (after(arrived, *others).astype(F32) + done[s][2].astype(F32)).astype(BF)

    for s in range(2, n_z):
        mix_moving = mix_step(mix_moving, s, *((theirs,) if s == 2 and by_core else (grad_kv,)))
        mix_moving = shift(mix_moving, "fsdp", n_z)
    kv_sum = grad_kv[:n_cx].astype(F32) + swap(grad_kv[n_cx:], "core").astype(F32)
    kv_moving = kv_sum[1].astype(BF)
    for s in range(2, n_cx):
        kv_moving = (shift(kv_moving, "cx", n_cx).astype(F32) + kv_sum[s]).astype(BF)
    kv_far = shift(kv_moving, "cx", n_cx)
    query_grad = (rotate(grad_query_rot, cos, sin, True) * scale).astype(BF)

    def by_core_halves(v):
        blocks = v.reshape(n_z, v.shape[0] // n_z, v.shape[1])
        theirs = pick(blocks, 1 - core, 2, 1)
        return pick(blocks, core, 2, 1).astype(F32), theirs, swap(theirs, "core")

    def by_fsdp(mine, came, *others):
        half = (mine + after(came, *others).astype(F32)).astype(BF)
        return half, lax.all_to_all(half, "fsdp", 0, 0)

    def by_chip(came, *others):
        total = jnp.sum(after(came, *others).astype(F32), axis=0).astype(BF)
        return total, ring_gather(total[None], "cx", n_cx, 0)

    def whole_of(came, *others):
        total = jnp.sum(after(came, *others).astype(F32), axis=0).astype(BF)
        return core_join(total, 0).astype(F32)

    grad_q = dot(hidden_one, query_grad, 0, 1).astype(BF)
    o_mine, o_theirs, o_came = by_core_halves(grad_output)
    q_mine, q_theirs, q_came = by_core_halves(grad_q)
    started = anchor(kv_moving, o_theirs, q_theirs)
    o_half, o_came = by_fsdp(o_mine, o_came, started)
    q_half, q_came = by_fsdp(q_mine, q_came, started)
    started = anchor(started, o_half, q_half)

    kv_grad = after(kv_far, started).astype(F32) + kv_sum[0]
    key_grad = rotate(kv_grad[0], cos, sin, True).astype(BF)
    value_grad = kv_grad[1].astype(BF)
    grad_both = jnp.concatenate([key_grad, value_grad], axis=0)
    first_part = dot(query_grad, w_q, 0, 1) + dot(grad_both, w_kv, 0, 1)
    grad_first = jnp.sum(first_part * normed_one, axis=0, keepdims=True)
    first_low = first_part.astype(BF)
    first_other = swap(first_low, "tp")
    small_grad = jnp.concatenate([grad_first, grad_second, grad_router], axis=0)
    small_other = swap(small_grad, "tp")
    grad_kv_w = dot(hidden_one, grad_both, 0, 1).astype(BF)
    kv_mine, kv_theirs, kv_came = by_core_halves(grad_kv_w)
    started = anchor(first_low, small_grad, kv_theirs)
    kv_half, kv_came = by_fsdp(kv_mine, kv_came, started)
    small_grad = small_grad + after(small_other, started)
    small_other = swap(small_grad, "core")
    started = anchor(kv_half, small_grad)

    mixed = mix_step(mix_moving, 0, started)
    mix_other = swap(mixed[half:], "tp")
    o_total, o_came = by_chip(o_came, started)
    q_total, q_came = by_chip(q_came, started)
    small_grad = small_grad + after(small_other, started)
    everyone = ring_gather(small_grad[None], "cx", n_cx, 0)
    started = anchor(mixed, o_total, q_total, small_grad)

    first_grad = first_low.astype(F32) + after(first_other, started).astype(F32)
    grad_inputs = branch.astype(F32) + norm_backward(
        first_grad, gain_first, inverse_one, normed_one
    )
    mixture = mixed[:half].astype(F32) + after(mix_other, first_grad).astype(F32)
    out_half = (pick(valid, tp, 2, 0) * (residual + mixture)).astype(BF)
    out_other = swap(out_half, "tp")
    kv_total, kv_came = by_chip(kv_came, started)
    total = jnp.sum(after(everyone, started), axis=0)
    small_mine = jnp.sum(
        lax.all_to_all(total, "fsdp", 1, 0, tiled=True).reshape(n_z, 2 + E, shard), axis=0
    )
    parts = [(expert_sum, k) for k in range(held - first_slot)]
    if by_core:
        others = swap(after(expert_sum, started), "core")
        parts = [(others, k) for k in range(first_slot)] + parts
    grad_q = whole_of(q_came, started)
    grad_output = whole_of(o_came, started).T
    started = anchor(out_half, kv_total)
    grad_down, grad_gate, grad_up = place(order[1 + n_z :], parts)
    grad_kv_w = whole_of(kv_came, started)
    out_other = after(out_other, started)
    layer_out = jnp.concatenate(
        [jnp.where(lead, out_half, out_other), jnp.where(lead, out_other, out_half)], axis=0
    )

    return (
        layer_out[None],
        grad_inputs[None],
        small_mine[0],
        grad_q,
        grad_kv_w[:, :kv_width],
        grad_kv_w[:, kv_width:],
        grad_output,
        small_mine[1],
        small_mine[2:].T,
        grad_gate,
        grad_up,
        grad_down,
    )


def solution(mesh):
    n_z, n_ctx, n_tp = mesh.shape["fsdp"], mesh.shape["ctx"], mesh.shape["tp"]
    named = Mesh(
        mesh.devices.reshape(n_z, n_ctx // 2, 2, n_tp), ("fsdp", "cx", "core", "tp")
    )
    ctx = ("cx", "core")
    placed = (
        P("fsdp", ctx, None),
        P("fsdp"),
        P("fsdp", ctx, None),
        P("fsdp", ctx, None),
        P("fsdp", ctx, None),
        P("fsdp"),
        P("fsdp", "tp"),
        P("fsdp", "tp"),
        P("fsdp", "tp"),
        P("tp", "fsdp"),
        P("fsdp"),
        P("fsdp", None),
        P("fsdp", None, "tp"),
        P("fsdp", None, "tp"),
        P("fsdp", "tp", None),
    )
    return jax.shard_map(
        functools.partial(local, (n_z, n_ctx // 2)),
        mesh=named,
        in_specs=placed,
        out_specs=(
            P("fsdp", ctx, None),
            P("fsdp", ctx, None),
            P("fsdp"),
            P("fsdp", "tp"),
            P("fsdp", "tp"),
            P("fsdp", "tp"),
            P("tp", "fsdp"),
            P("fsdp"),
            P("fsdp", None),
            P("fsdp", None, "tp"),
            P("fsdp", None, "tp"),
            P("fsdp", "tp", None),
        ),
        check_vma=False,
    )
```

```python
import functools
import math

import jax
import jax.numpy as jnp
from jax import lax
from jax.experimental import pallas as pl
from jax.experimental.pallas import tpu as pltpu
from jax.sharding import Mesh
from jax.sharding import PartitionSpec as P

HEAD = 64
TOPK = 8
E = 16
CAP = 256
EPSILON = 1e-06
BF = jnp.bfloat16
F32 = jnp.float32
NEG = -1e30
FAR = 1e6


def dot(a, b, ca, cb):
    return lax.dot_general(a, b, (((ca,), (cb,)), ((), ())), preferred_element_type=F32)


def shift(v, axis, n, by=1):
    return lax.ppermute(v, axis, [(i, (i + by) % n) for i in range(n)])


def swap(v, axis):
    return lax.ppermute(v, axis, [(0, 1), (1, 0)])


def pick(v, index, parts, dim):
    size = v.shape[dim] // parts
    return lax.dynamic_slice_in_dim(v, index * size, size, dim)


def put(buffer, v, start, dim):
    return lax.dynamic_update_slice_in_dim(buffer, v, start, dim)


def after(v, *others):
    return lax.optimization_barrier((v,) + others)[0]


def anchor_kernel(in_ref, out_ref):
    out_ref[...] = in_ref[...]


def anchor(*others):
    token = after(jnp.zeros((8, 128), F32), *others)
    return pl.pallas_call(
        anchor_kernel,
        name="anchor",
        out_shape=jax.ShapeDtypeStruct((8, 128), F32),
        cost_estimate=pl.CostEstimate(flops=10**11, transcendentals=0, bytes_accessed=8192),
    )(token)


def direct_reduce(part, axis, n):
    me = lax.axis_index(axis)
    total = part(me)
    for s in range(1, n):
        total = total + shift(part((me + s) % n).astype(BF), axis, n, s).astype(F32)
    return total


def ring_reduce(part, axis, n, *others):
    me = lax.axis_index(axis)
    moving = part((me + n - 1) % n).astype(BF)
    for s in range(2, n):
        moving = (shift(moving, axis, n).astype(F32) + part((me + n - s) % n)).astype(BF)
    moving = shift(moving, axis, n)
    if others:
        moving = after(moving, *others)
    return moving.astype(F32) + part(me)


def core_halves(v, dim):
    core = lax.axis_index("core")
    mine = pick(v, core, 2, dim)
    theirs = pick(v, 1 - core, 2, dim)
    return mine.astype(F32) + swap(theirs.astype(BF), "core").astype(F32)


def core_join(v, dim):
    other = swap(v, "core")
    first = lax.axis_index("core") == 0
    return jnp.concatenate([jnp.where(first, v, other), jnp.where(first, other, v)], axis=dim)


def ring_gather(v, axis, n, dim):
    me = lax.axis_index(axis)
    size = v.shape[dim]
    shape = list(v.shape)
    shape[dim] = size * n
    out = put(jnp.zeros(shape, v.dtype), v, me * size, dim)
    moving = v
    for s in range(1, n):
        moving = shift(moving, axis, n)
        out = put(out, moving, ((me + n - s) % n) * size, dim)
    return out


def ctx_total(v, n_cx):
    half = core_halves(v, 0).astype(BF)
    part = ring_reduce(lambda j: pick(half, j, n_cx, 0).astype(F32), "cx", n_cx).astype(BF)
    return core_join(ring_gather(part, "cx", n_cx, 0), 0)


def normalize(values):
    inverse = lax.rsqrt(jnp.mean(values * values, axis=-1, keepdims=True) + EPSILON)
    return inverse, values * inverse


def norm_backward(grad, gain, inverse, normed):
    scaled = grad * gain
    return inverse * (scaled - normed * jnp.mean(scaled * normed, axis=-1, keepdims=True))


def rotate(v, cos, sin, inverse):
    rows = v.shape[1]
    shaped = v.reshape(-1, 2, HEAD // 2, rows)
    a, b = shaped[:, 0], shaped[:, 1]
    if inverse:
        out = jnp.stack([a * cos + b * sin, b * cos - a * sin], axis=1)
    else:
        out = jnp.stack([a * cos - b * sin, b * cos + a * sin], axis=1)
    return out.reshape(-1, rows)


def keep_plan(routes, order, live):
    rows = routes.shape[0]
    pairs = rows * TOPK
    token, choice = order // TOPK, order % TOPK
    rank = jnp.arange(pairs, dtype=jnp.int32)
    at_token = (jnp.arange(rows, dtype=jnp.int32)[:, None] == token[None, :]).astype(BF)
    at_choice = jnp.arange(TOPK, dtype=jnp.int32)[:, None] == choice[None, :]
    high = jnp.where(at_choice, (rank // 64)[None, :], 0).astype(BF)
    low = jnp.where(at_choice, (rank % 64)[None, :], 0).astype(BF)
    place = dot(at_token, jnp.concatenate([high, low], axis=0), 1, 1)
    place = place[:, :TOPK] * 64.0 + place[:, TOPK:]
    hits = routes[:, :, None] == jnp.arange(E, dtype=jnp.int32)[None, None, :]
    routed = jnp.any(hits, axis=1)
    place_e = jnp.sum(jnp.where(hits, place[:, :, None], 0.0), axis=1)
    place_e = jnp.where(routed & live[:, None], place_e, FAR)
    across = place_e.T
    earlier = jnp.sum((place_e[:, :, None] < across[None, :, :]).astype(F32), axis=0).T
    kept = routed & live[:, None] & (earlier < CAP)
    return routed, kept


def assemble(info_ref, own_ref, got_ref, other_ref, full_ref):
    z, core, cx = info_ref[0], info_ref[1], info_ref[2]
    rows = own_ref.shape[0]
    chips, steps, piece, _ = got_ref.shape
    n_z = steps + 1
    full_ref[pl.ds(pl.multiple_of(z * rows, piece), rows), :] = own_ref[...]
    for k in range(chips):
        chip = (cx + chips - k) % chips
        for s in range(1, n_z):
            start = ((z + n_z - s) % n_z) * rows + chip * 2 * piece
            mine = pl.multiple_of(start + core * piece, piece)
            theirs = pl.multiple_of(start + (1 - core) * piece, piece)
            full_ref[pl.ds(mine, piece), :] = got_ref[k, s - 1]
            full_ref[pl.ds(theirs, piece), :] = other_ref[k, s - 1]


def project_kernel(turned, scale, info_ref, own_ref, got_ref, other_ref, x_ref, cos_ref, sin_ref, out_ref, full_ref):
    assemble(info_ref, own_ref, got_ref, other_ref, full_ref)
    flat = jnp.dot(x_ref[...], full_ref[...], preferred_element_type=F32).T
    cos, sin = cos_ref[...], sin_ref[...]
    quarter = HEAD // 2
    for start in range(0, turned, HEAD):
        a = flat[start : start + quarter, :]
        b = flat[start + quarter : start + HEAD, :]
        out_ref[start : start + quarter, :] = ((a * cos - b * sin).astype(BF) * scale).astype(BF)
        out_ref[start + quarter : start + HEAD, :] = ((b * cos + a * sin).astype(BF) * scale).astype(BF)
    if turned < flat.shape[0]:
        out_ref[turned:, :] = flat[turned:, :].astype(BF)


def project(info, own, got, other, x, cos, sin, turned, scale):
    columns = own.shape[1]
    rows, width = x.shape
    return pl.pallas_call(
        functools.partial(project_kernel, turned, scale),
        name="project",
        grid_spec=pltpu.PrefetchScalarGridSpec(num_scalar_prefetch=1, grid=(1,),
            in_specs=[pl.BlockSpec(v.shape, lambda i, n, k=v.ndim: (0,) * k) for v in (own, got, other, x, cos, sin)],
            out_specs=[
                pl.BlockSpec((columns, rows), lambda i, n: (0, 0)),
                pl.BlockSpec((width, columns), lambda i, n: (0, 0)),
            ],
        ),
        out_shape=[
            jax.ShapeDtypeStruct((columns, rows), BF),
            jax.ShapeDtypeStruct((width, columns), BF),
        ],
        compiler_params=pltpu.CompilerParams(vmem_limit_bytes=40 << 20),
        cost_estimate=pl.CostEstimate(
            flops=2 * rows * width * columns,
            transcendentals=0,
            bytes_accessed=4 * width * columns + 2 * rows * (width + columns),
        ),
    )(info, own, got, other, x, cos, sin)


def assembled(info, own, got, other):
    rows, columns = own.shape
    full = (rows * (got.shape[1] + 1), columns)
    return pl.pallas_call(
        assemble,
        name="assembled",
        grid_spec=pltpu.PrefetchScalarGridSpec(num_scalar_prefetch=1, grid=(1,),
            in_specs=[pl.BlockSpec(v.shape, lambda i, n, k=v.ndim: (0,) * k) for v in (own, got, other)],
            out_specs=pl.BlockSpec(full, lambda i, n: (0, 0)),
        ),
        out_shape=jax.ShapeDtypeStruct(full, BF),
        compiler_params=pltpu.CompilerParams(vmem_limit_bytes=32 << 20),
        cost_estimate=pl.CostEstimate(flops=0, transcendentals=0, bytes_accessed=4 * rows * columns * 4),
    )(info, own, got, other)


def softmax_block(q, k, last, base, first_row, length):
    s = lax.dot_general(k, q, (((0,), (0,)), ((), ())), preferred_element_type=F32)
    if last:
        key = base + lax.broadcasted_iota(jnp.int32, s.shape, 0)
        query = first_row + lax.broadcasted_iota(jnp.int32, s.shape, 1)
        s = jnp.where((key <= query) & (key < length), s, NEG)
    return s


def slot_of(block, ctx, n_ctx):
    n_cx = n_ctx // 2
    steps = (ctx // 2 + n_cx - block // 2) % n_cx
    return ((ctx + block) % 2) * n_cx + steps


def attend_kernel(group, info_ref, q_ref, kv_ref, o_ref, lse_ref):
    count, first_row, length, ctx = info_ref[0], info_ref[1], info_ref[2], info_ref[3]
    rows = q_ref.shape[1]
    n_ctx = kv_ref.shape[0]
    keys = kv_ref.shape[3]
    for h in range(group):
        q = q_ref[h * HEAD : (h + 1) * HEAD, :]

        def step(j, carry, last):
            top, total, acc = carry
            slot = slot_of(j, ctx, n_ctx)
            k = kv_ref[slot, 0]
            v = kv_ref[slot, 1]
            s = softmax_block(q, k, last, j * keys, first_row, length)
            new_top = jnp.maximum(top, jnp.max(s, axis=0, keepdims=True))
            p = jnp.exp(s - new_top)
            fade = jnp.exp(top - new_top)
            total = total * fade + jnp.sum(p, axis=0, keepdims=True)
            acc = acc * fade + jnp.dot(v, p.astype(BF), preferred_element_type=F32)
            return new_top, total, acc

        carry = (
            jnp.full((1, rows), NEG, F32),
            jnp.zeros((1, rows), F32),
            jnp.zeros((HEAD, rows), F32),
        )
        carry = lax.fori_loop(0, count - 1, functools.partial(step, last=False), carry)
        top, total, acc = step(count - 1, carry, True)
        o_ref[h * HEAD : (h + 1) * HEAD, :] = (acc / total).astype(BF)
        lse_ref[0, h : h + 1, :] = top + jnp.log(total)


def attend(q, kv, info, group, start, heads):
    rows = q.shape[1]
    n_ctx, _, depth, keys = kv.shape
    return pl.pallas_call(
        functools.partial(attend_kernel, group),
        name="attend",
        grid_spec=pltpu.PrefetchScalarGridSpec(
            num_scalar_prefetch=1,
            grid=(heads,),
            in_specs=[
                pl.BlockSpec((group * HEAD, rows), lambda g, i: (start + g, 0)),
                pl.BlockSpec((n_ctx, 2, HEAD, keys), lambda g, i: (0, 0, start + g, 0)),
            ],
            out_specs=[
                pl.BlockSpec((group * HEAD, rows), lambda g, i: (g, 0)),
                pl.BlockSpec((1, 8, rows), lambda g, i: (g, 0, 0)),
            ],
        ),
        out_shape=[
            jax.ShapeDtypeStruct((heads * group * HEAD, rows), BF),
            jax.ShapeDtypeStruct((heads, 8, rows), F32),
        ],
        compiler_params=pltpu.CompilerParams(vmem_limit_bytes=48 << 20),
        cost_estimate=pl.CostEstimate(
            flops=4 * heads * group * HEAD * rows * n_ctx * keys,
            transcendentals=heads * group * rows * n_ctx * keys,
            bytes_accessed=2 * q.size + kv.size,
        ),
    )(info, q, kv)


def attend_back_kernel(group, info_ref, q_ref, kv_ref, o_ref, do_ref, lse_ref, dq_ref, dkv_ref):
    count, first_row, length, ctx = info_ref[0], info_ref[1], info_ref[2], info_ref[3]
    n_ctx = kv_ref.shape[0]
    keys = kv_ref.shape[3]
    delta = []
    for h in range(group):
        part = slice(h * HEAD, (h + 1) * HEAD)
        delta.append(
            jnp.sum(do_ref[part, :].astype(F32) * o_ref[part, :].astype(F32), axis=0, keepdims=True)
        )
    dq_ref[...] = jnp.zeros_like(dq_ref)

    def step(j, last):
        slot = slot_of(j, ctx, n_ctx)
        k = kv_ref[slot, 0]
        v = kv_ref[slot, 1]
        dk = jnp.zeros((keys, HEAD), F32)
        dv = jnp.zeros((keys, HEAD), F32)
        for h in range(group):
            part = slice(h * HEAD, (h + 1) * HEAD)
            q = q_ref[part, :]
            do = do_ref[part, :]
            s = softmax_block(q, k, last, j * keys, first_row, length)
            p = jnp.exp(s - lse_ref[0, h : h + 1, :])
            dp = lax.dot_general(v, do, (((0,), (0,)), ((), ())), preferred_element_type=F32)
            ds = (p * (dp - delta[h])).astype(BF)
            pb = p.astype(BF)
            dv += lax.dot_general(pb, do, (((1,), (1,)), ((), ())), preferred_element_type=F32)
            dk += lax.dot_general(ds, q, (((1,), (1,)), ((), ())), preferred_element_type=F32)
            dq_ref[part, :] += jnp.dot(k, ds, preferred_element_type=F32)
        dkv_ref[slot, 0] = dk.T.astype(BF)
        dkv_ref[slot, 1] = dv.T.astype(BF)

    @pl.loop(0, count - 1)
    def _(j):
        step(j, False)

    step(count - 1, True)

    @pl.loop(count, n_ctx)
    def _(j):
        dkv_ref[slot_of(j, ctx, n_ctx)] = jnp.zeros(dkv_ref.shape[1:], BF)


def attend_back(q, kv, o, do, lse, info, group):
    rows = q.shape[1]
    n_ctx, _, depth, keys = kv.shape
    heads = depth // HEAD
    wide = pl.BlockSpec((group * HEAD, rows), lambda g, i: (g, 0))
    blocks = pl.BlockSpec((n_ctx, 2, HEAD, keys), lambda g, i: (0, 0, g, 0))
    return pl.pallas_call(
        functools.partial(attend_back_kernel, group),
        name="attend_back",
        grid_spec=pltpu.PrefetchScalarGridSpec(
            num_scalar_prefetch=1,
            grid=(heads,),
            in_specs=[
                wide,
                blocks,
                wide,
                wide,
                pl.BlockSpec((1, 8, rows), lambda g, i: (g, 0, 0)),
            ],
            out_specs=[wide, blocks],
        ),
        out_shape=[
            jax.ShapeDtypeStruct(q.shape, F32),
            jax.ShapeDtypeStruct(kv.shape, BF),
        ],
        compiler_params=pltpu.CompilerParams(vmem_limit_bytes=48 << 20),
        cost_estimate=pl.CostEstimate(
            flops=10 * q.shape[0] * rows * n_ctx * keys,
            transcendentals=q.shape[0] // HEAD * rows * n_ctx * keys,
            bytes_accessed=10 * q.size + 4 * kv.size,
        ),
    )(info, q, kv, o, do, lse)


def expert_kernel(info_ref, near_in, far_in, near_do, far_do, gate_ref, up_ref, down_ref, *refs):
    near_out, far_out, mix_out, act_out, dg_out, du_out = refs[:6]
    rows_x, rows_do, shares_in, mix_sum, back_sum, shares_out = refs[6:]
    e = pl.program_id(0)
    half, width = near_do.shape[2:]
    rows = 2 * half

    @pl.when(e == 0)
    def _():
        rows_x[:half, :] = near_in[:, :width]
        rows_x[half:, :] = far_in[:, :width]
        rows_do[:half, :] = near_do[0, 0]
        rows_do[half:, :] = far_do[0, 0]
        shares_in[:half, :] = near_in[:, width:].astype(F32)
        shares_in[half:, :] = far_in[:, width:].astype(F32)

    lanes = lax.broadcasted_iota(jnp.int32, (rows, 128), 1)
    x = rows_x[...]
    do = rows_do[...]
    per, _, hidden = gate_ref.shape
    mix = back = share = None
    for i in range(per):
        chosen = info_ref[0] + e * per + i
        gate, up, down = gate_ref[i], up_ref[i], down_ref[i]
        weight = jnp.sum(
            jnp.where((lanes == chosen) | (lanes == chosen + E), shares_in[...], 0.0),
            axis=1,
            keepdims=True,
        )
        g = jnp.dot(x, gate, preferred_element_type=F32)
        u = jnp.dot(x, up, preferred_element_type=F32)
        dact = dot(do, down, 1, 1)
        sig = jax.nn.sigmoid(g)
        silu = g * sig
        act = silu * u
        share_i = jnp.where(lanes == chosen, jnp.sum(act * dact, axis=1, keepdims=True), 0.0)
        dhid = dact * weight
        part = slice(i * hidden, (i + 1) * hidden)
        act_out[:, part] = (act * weight).astype(BF)
        dg_out[:, part] = (dhid * u * (sig * (1.0 + g * (1.0 - sig)))).astype(BF)
        du_out[:, part] = (dhid * silu).astype(BF)
        mix_i = jnp.dot(act_out[:, part], down, preferred_element_type=F32)
        back_i = dot(dg_out[:, part], gate, 1, 1) + dot(du_out[:, part], up, 1, 1)
        mix = mix_i if mix is None else mix + mix_i
        back = back_i if back is None else back + back_i
        share = share_i if share is None else share + share_i

    @pl.when(e == 0)
    def _():
        mix_sum[...] = mix
        back_sum[...] = back
        shares_out[...] = share

    @pl.when(e > 0)
    def _():
        mix_sum[...] += mix
        back_sum[...] += back
        shares_out[...] += share

    @pl.when(e == pl.num_programs(0) - 1)
    def _():
        near_out[:, :width] = back_sum[:half, :].astype(BF)
        near_out[:, width:] = shares_out[:half, :].astype(BF)
        far_out[:, :width] = back_sum[half:, :].astype(BF)
        far_out[:, width:] = shares_out[half:, :].astype(BF)
        mix_out[...] = mix_sum[...].astype(BF)


def experts(info, near, far, do_near, do_far, gate, up, down, weight):
    half, wide = near.shape
    width = do_near.shape[3]
    held, _, hidden = gate.shape
    rows = 2 * half
    whole = lambda shape: pl.BlockSpec(shape, lambda e, i: (0, 0))
    per = 1
    each = lambda shape: pl.BlockSpec((per,) + shape, lambda e, i: (e, 0, 0))
    column = pl.BlockSpec((rows, per * hidden), lambda e, i: (0, e))
    mid = jax.ShapeDtypeStruct((rows, held * hidden), BF)
    message = jax.ShapeDtypeStruct((half, wide), BF)
    return pl.pallas_call(
        expert_kernel,
        name="experts",
        grid_spec=pltpu.PrefetchScalarGridSpec(
            num_scalar_prefetch=1,
            grid=(held // per,),
            in_specs=[
                whole((half, wide)),
                whole((half, wide)),
                pl.BlockSpec((1, 1, half, width), lambda e, i: (i[3], i[4], 0, 0)),
                pl.BlockSpec((1, 1, half, width), lambda e, i: (i[5], i[4], 0, 0)),
                each((width, hidden)),
                each((width, hidden)),
                each((hidden, width)),
            ],
            out_specs=[
                whole((half, wide)),
                whole((half, wide)),
                whole((rows, width)),
                column,
                column,
                column,
            ],
            scratch_shapes=[
                pltpu.VMEM((rows, width), BF),
                pltpu.VMEM((rows, width), BF),
                pltpu.VMEM((rows, 128), F32),
                pltpu.VMEM((rows, width), F32),
                pltpu.VMEM((rows, width), F32),
                pltpu.VMEM((rows, 128), F32),
            ],
        ),
        out_shape=[
            message,
            message,
            jax.ShapeDtypeStruct((rows, width), BF),
            mid,
            mid,
            mid,
        ],
        compiler_params=pltpu.CompilerParams(vmem_limit_bytes=56 << 20),
        cost_estimate=pl.CostEstimate(
            flops=12 * weight * rows * width * held * hidden,
            transcendentals=rows * held * hidden,
            bytes_accessed=6 * held * hidden * width + 16 * rows * width,
        ),
    )(info, near, far, do_near, do_far, gate, up, down)


def expert_grad_kernel(count, info_ref, *refs):
    rows_x, rows_do = refs[: 2 * count], refs[2 * count : 4 * count]
    acts, dgs, dus = (refs[(4 + k) * count : (5 + k) * count] for k in range(3))
    out = refs[-1]
    width = rows_do[0].shape[-1]
    hidden = acts[0].shape[1]
    down = both = None
    for s in range(count):
        do = jnp.concatenate([rows_do[2 * s][0, 0], rows_do[2 * s + 1][0, 0]], axis=0)
        x = jnp.concatenate([rows_x[2 * s][:, :width], rows_x[2 * s + 1][:, :width]], axis=0)
        dgu = jnp.concatenate([dgs[s][...], dus[s][...]], axis=1)
        first, second = dot(acts[s][...], do, 0, 0), dot(dgu, x, 0, 0)
        down = first if down is None else down + first
        both = second if both is None else both + second
    out[0, 0] = down.astype(BF)
    out[0, 1] = both[:hidden].astype(BF)
    out[0, 2] = both[hidden:].astype(BF)


def expert_grads(info, chunks, do_all, acts, dgs, dus, held, start, count):
    n_z = len(acts)
    if n_z > 4:
        total = 0.0
        for b in range(0, n_z, 4):
            part = slice(b, b + 4)
            here = jnp.concatenate([info[:1], info[1 + b : 5 + b], info[1 + n_z :]])
            total = total + expert_grads(
                here,
                chunks[2 * b : 2 * b + 8],
                do_all,
                acts[part],
                dgs[part],
                dus[part],
                held,
                start,
                count,
            ).astype(F32)
        return total.astype(BF)
    size, width = do_all.shape[2:]
    wide = chunks[0].shape[1]
    rows, mid = acts[0].shape
    hidden = mid // held
    at = 1 + n_z + start
    chunk = pl.BlockSpec((size, wide), lambda e, i: (0, 0), pipeline_mode=pl.Buffered(1))
    do_chunk = lambda other, s: pl.BlockSpec(
        (1, 1, size, width),
        lambda e, i: ((1 - i[0]) if other else i[0], i[1 + s], 0, 0),
        pipeline_mode=pl.Buffered(1),
    )
    column = pl.BlockSpec((rows, hidden), lambda e, i: (0, i[at + e]))
    return pl.pallas_call(
        functools.partial(expert_grad_kernel, n_z),
        name="expert_grads",
        grid_spec=pltpu.PrefetchScalarGridSpec(
            num_scalar_prefetch=1,
            grid=(count,),
            in_specs=[chunk for _ in chunks]
            + [do_chunk(other, s) for s in range(n_z) for other in (False, True)]
            + [column] * (3 * n_z),
            out_specs=pl.BlockSpec((1, 3, hidden, width), lambda e, i: (e, 0, 0, 0)),
        ),
        out_shape=jax.ShapeDtypeStruct((count, 3, hidden, width), BF),
        compiler_params=pltpu.CompilerParams(vmem_limit_bytes=58 << 20),
        cost_estimate=pl.CostEstimate(
            flops=60 * n_z * rows * width * hidden * count,
            transcendentals=0,
            bytes_accessed=4 * n_z * rows * (width + hidden * count),
        ),
    )(info, *chunks, *([do_all] * (2 * n_z)), *acts, *dgs, *dus)


def place_kernel(count, info_ref, *refs):
    down, gate, up = refs[count:]
    for i, ref in enumerate(refs[:count]):

        @pl.when(pl.program_id(0) == i)
        def _():
            down[0] = ref[0, 0].astype(F32)
            gate[0] = ref[0, 1].astype(F32).T
            up[0] = ref[0, 2].astype(F32).T


def place(info, parts):
    hidden, width = parts[0][0].shape[2:]
    count = len(parts)
    out = lambda *shape: pl.BlockSpec((1,) + shape, lambda e, i: (i[e], 0, 0))
    return pl.pallas_call(
        functools.partial(place_kernel, count),
        name="place",
        grid_spec=pltpu.PrefetchScalarGridSpec(
            num_scalar_prefetch=1,
            grid=(count,),
            in_specs=[
                pl.BlockSpec((1, 3, hidden, width), lambda e, i, k=k: (k, 0, 0, 0)) for _, k in parts
            ],
            out_specs=[out(hidden, width), out(width, hidden), out(width, hidden)],
        ),
        out_shape=[
            jax.ShapeDtypeStruct((count, hidden, width), F32),
            jax.ShapeDtypeStruct((count, width, hidden), F32),
            jax.ShapeDtypeStruct((count, width, hidden), F32),
        ],
        compiler_params=pltpu.CompilerParams(vmem_limit_bytes=48 << 20),
        cost_estimate=pl.CostEstimate(
            flops=0, transcendentals=0, bytes_accessed=18 * count * hidden * width
        ),
    )(info, *[array for array, _ in parts])


def local(
    sizes,
    tokens,
    lengths,
    routes,
    visit_order,
    cotangent,
    first_gain,
    query_weight,
    key_matrix,
    value_matrix,
    output_weight,
    second_gain,
    router_weight,
    gate_weight,
    up_weight,
    down_weight,
):
    n_z, n_cx = sizes
    n_ctx = 2 * n_cx
    z = lax.axis_index("fsdp")
    cx = lax.axis_index("cx")
    core = lax.axis_index("core")
    tp = lax.axis_index("tp")
    ctx = cx * 2 + core
    rows, width = tokens.shape[1:]
    half = rows // 2
    shard = query_weight.shape[0]
    q_width = query_weight.shape[1]
    kv_width = key_matrix.shape[1]
    group = q_width // kv_width
    held = gate_weight.shape[0]
    hidden = gate_weight.shape[2]
    first_row = ctx * rows
    length = lengths[0]
    positions = first_row + jnp.arange(rows, dtype=jnp.int32)
    live = positions < length
    valid = live.astype(F32)[:, None]

    wide_split = n_cx == 2 and (shard // 4) % 16 == 0

    def bring(own, over_chips):
        piece = pick(own, ctx, n_ctx, 0) if over_chips else pick(own, core, 2, 0)
        return own, [shift(piece, "fsdp", n_z, s) for s in range(1, n_z)]

    def spread(own, got, over_chips):
        got = jnp.stack(got)[None]
        if over_chips:
            got = jnp.concatenate([got, swap(got, "cx")], axis=0)
        return own, got, swap(got, "core")

    kv_own, kv_got = bring(jnp.concatenate([key_matrix, value_matrix], axis=1), False)

    small = jnp.concatenate([first_gain[None], second_gain[None], router_weight.T], axis=0)
    small_full = lax.all_to_all(jnp.broadcast_to(small[None], (n_z, 2 + E, shard)), "fsdp", 0, 0)
    small_full = jnp.transpose(small_full, (1, 0, 2)).reshape(2 + E, width)
    gain_first = small_full[0:1].astype(F32)
    gain_second = small_full[1:2].astype(F32)
    router = small_full[2:]

    grad_half = (pick(cotangent[0], tp, 2, 0).astype(F32) * pick(valid, tp, 2, 0)).astype(BF)
    grad_other = swap(grad_half, "tp")

    kv_pieces = spread(kv_own, kv_got, False)
    q_own, q_got = bring(after(query_weight, *kv_got), wide_split)
    started = anchor(*kv_got)
    kv_pieces = (kv_own, kv_pieces[1], after(kv_pieces[2], started))
    here = jnp.stack([z, core, cx]).astype(jnp.int32)

    routed, kept = keep_plan(routes[0], visit_order[0, 0], live)

    inputs = tokens[0].astype(F32)
    inverse_one, normed_one = normalize(inputs)
    hidden_one = after((normed_one * gain_first).astype(BF), grad_other)
    frequency = jnp.exp(
        jnp.arange(HEAD // 2, dtype=F32) * (-2.0 * math.log(10000.0) / HEAD)
    )
    angles = frequency[:, None] * positions.astype(F32)[None, :]
    cos, sin = jnp.cos(angles), jnp.sin(angles)
    scale = HEAD**-0.5
    kv_mine, w_kv = project(here, *kv_pieces, hidden_one, cos, sin, kv_width, 1.0)
    kv_mine = kv_mine.reshape(1, 2, kv_width, rows)
    near_kv = [kv_mine]
    for s in range(1, n_cx):
        near_kv.append(shift(near_kv[-1], "cx", n_cx))
    near_kv = jnp.concatenate([near_kv[0]] + [after(v, anchor(kv_mine)) for v in near_kv[1:]], axis=0)
    started = anchor(kv_mine)
    q_got = [after(v, started) for v in q_got]
    q_pieces = spread(q_own, q_got, wide_split)
    o_own, o_got = bring(after(output_weight.T, *q_got), wide_split)
    grad_all = lax.all_gather(after(grad_half, *q_got), ("tp", "fsdp"))
    grad_all = grad_all.reshape(2, n_z, half, width)
    query, w_q = project(here, *q_pieces, hidden_one, cos, sin, q_width, scale)
    kv = jnp.concatenate([near_kv, swap(near_kv, "core")], axis=0)
    count = jnp.minimum(ctx + 1, (length + rows - 1) // rows)
    info = jnp.stack([count, first_row, length, ctx])
    kv_heads = kv_width // HEAD
    split = [(0, kv_heads // 2), (kv_heads // 2, kv_heads - kv_heads // 2)]
    early, early_lse = attend(after(query, grad_other), kv, info, group, *split[0])
    o_pieces = spread(o_own, [after(v, early) for v in o_got], wide_split)
    later, later_lse = attend(after(query, early), kv, info, group, *split[1])
    attended = jnp.concatenate([early, later], axis=0)
    lse = jnp.concatenate([early_lse, later_lse], axis=0)
    o_full = assembled(here, *[after(v, later) for v in o_pieces])

    far = dot(pick(attended, 1 - tp, 2, 1), o_full, 0, 1).astype(BF)
    near = dot(pick(attended, tp, 2, 1), o_full, 0, 1)
    residual = pick(tokens[0], tp, 2, 0).astype(F32) + near + swap(far, "tp").astype(F32)
    inverse_two, normed_two = normalize(residual)
    hidden_two = (normed_two * gain_second).astype(BF)
    logits = dot(hidden_two, router, 1, 1)
    routed_half = pick(routed, tp, 2, 0)
    kept_half = pick(kept, tp, 2, 0).astype(F32)
    masked = jnp.where(routed_half, logits, NEG)
    raised = jnp.where(
        routed_half, jnp.exp(masked - jnp.max(masked, axis=1, keepdims=True)), 0.0
    )
    gates = raised / jnp.sum(raised, axis=1, keepdims=True)
    weights = gates * kept_half

    high = weights.astype(BF)
    low = (weights - high.astype(F32)).astype(BF)
    message = jnp.concatenate(
        [hidden_two, high, low, jnp.zeros((half, 128 - 2 * E), BF)], axis=1
    )
    blocks = [(z + n_z - s) % n_z for s in range(n_z)]
    near = [message]
    far = [swap(message, "tp")]
    coming = shift(message, "fsdp", n_z)
    done, moving, joined = [], None, ()
    for s in range(n_z):
        first = near[s]
        if s + 1 < n_z:
            near.append(after(coming, *[d[0] for d in done[-1:]]))
            far.append(swap(near[-1], "tp"))
            first = after(first, near[-1])
            if s + 2 < n_z:
                coming = shift(near[-1], "fsdp", n_z)
        first = after(first, *joined)
        if s:
            info_s = [z * held, tp, blocks[s], tp, blocks[s], 1 - tp]
            rows_do = (grad_all, grad_all)
        else:
            info_s = [z * held, tp, blocks[s], 0, 0, 0]
            rows_do = (grad_half[None, None], grad_other[None, None])
        done.append(
            experts(
                jnp.stack([jnp.asarray(v, jnp.int32) for v in info_s]),
                first,
                far[s],
                *rows_do,
                gate_weight,
                up_weight,
                down_weight,
                10 if s else 1,
            )
        )
        if s > 1:
            part = done[s - 1][0].astype(F32) + swap(done[s - 1][1], "tp").astype(F32)
            if s > 2:
                part = shift(moving, "fsdp", n_z).astype(F32) + part
            moving = part.astype(BF)
            joined = (moving,)
    last = swap(done[-1][1], "tp")
    by_core = held % 2 == 0
    first_slot = held // 2 if by_core else 0
    slots = [((1 - core) * first_slot + k) % held for k in range(first_slot)]
    slots += [core * first_slot + k for k in range(held - first_slot)]
    order = jnp.stack([jnp.asarray(v, jnp.int32) for v in [tp] + blocks + slots])
    grad_args = (
        [v for s in range(n_z) for v in (near[s], far[s])],
        grad_all,
        [done[s][3] for s in range(n_z)],
        [done[s][4] for s in range(n_z)],
        [done[s][5] for s in range(n_z)],
        held,
    )
    theirs = expert_grads(after(order, moving), *grad_args, 0, first_slot) if by_core else None
    mix_moving = shift(done[1][2], "fsdp", n_z)
    part = done[-1][0].astype(F32) + after(last, theirs if by_core else moving).astype(F32)
    moving = (shift(moving, "fsdp", n_z).astype(F32) + part).astype(BF)
    own = done[0][0].astype(F32) + swap(after(done[0][1], last), "tp").astype(F32)
    mine = expert_grads(after(order, moving), *grad_args, first_slot, held - first_slot)
    back = shift(moving, "fsdp", n_z)

    if by_core:
        expert_half = mine.astype(F32) + after(swap(theirs, "core"), mine).astype(F32)
        expert_half = expert_half.astype(BF)
        expert_sum = lax.psum(expert_half, "cx")
        back, own = after(back, expert_half), after(own, expert_half)
    else:
        expert_sum = lax.psum(mine, ("cx", "core"))
    back = back.astype(F32) + own
    hidden_grad = back[:, :width]
    gate_grad = back[:, width : width + E] * kept_half

    logit_grad = (
        gates * (gate_grad - jnp.sum(gates * gate_grad, axis=1, keepdims=True))
    ).astype(BF)
    hidden_grad = hidden_grad + dot(logit_grad, router, 1, 0)
    grad_router = dot(logit_grad, hidden_two, 0, 0)
    grad_second = jnp.sum(hidden_grad * normed_two, axis=0, keepdims=True)
    branch_half = (
        grad_half.astype(F32) + norm_backward(hidden_grad, gain_second, inverse_two, normed_two)
    ).astype(BF)
    lead = tp == 0
    branch_other = swap(branch_half, "tp")
    branch = jnp.concatenate(
        [jnp.where(lead, branch_half, branch_other), jnp.where(lead, branch_other, branch_half)],
        axis=0,
    )

    attended_grad = dot(o_full, branch, 0, 1).astype(BF)
    grad_output = dot(branch, attended, 0, 1).astype(BF)
    attended_grad = after(attended_grad, grad_output)

    grad_query_rot, grad_kv = attend_back(
        query, kv, attended, attended_grad, lse, info, group
    )
    def mix_step(arrived, s, *others):
        return (after(arrived, *others).astype(F32) + done[s][2].astype(F32)).astype(BF)

    for s in range(2, n_z):
        mix_moving = mix_step(mix_moving, s, *((theirs,) if s == 2 and by_core else (grad_kv,)))
        mix_moving = shift(mix_moving, "fsdp", n_z)
    kv_sum = grad_kv[:n_cx].astype(F32) + swap(grad_kv[n_cx:], "core").astype(F32)
    kv_moving = kv_sum[1].astype(BF)
    for s in range(2, n_cx):
        kv_moving = (shift(kv_moving, "cx", n_cx).astype(F32) + kv_sum[s]).astype(BF)
    kv_far = shift(kv_moving, "cx", n_cx)
    query_grad = (rotate(grad_query_rot, cos, sin, True) * scale).astype(BF)

    def by_core_halves(v):
        blocks = v.reshape(n_z, v.shape[0] // n_z, v.shape[1])
        theirs = pick(blocks, 1 - core, 2, 1)
        return pick(blocks, core, 2, 1).astype(F32), theirs, swap(theirs, "core")

    def by_fsdp(mine, came, *others):
        half = (mine + after(came, *others).astype(F32)).astype(BF)
        return half, lax.all_to_all(half, "fsdp", 0, 0)

    def by_chip(came, *others):
        total = jnp.sum(after(came, *others).astype(F32), axis=0).astype(BF)
        return total, ring_gather(total[None], "cx", n_cx, 0)

    def whole_of(came, *others):
        total = jnp.sum(after(came, *others).astype(F32), axis=0).astype(BF)
        return core_join(total, 0).astype(F32)

    grad_q = dot(hidden_one, query_grad, 0, 1).astype(BF)
    o_mine, o_theirs, o_came = by_core_halves(grad_output)
    q_mine, q_theirs, q_came = by_core_halves(grad_q)
    started = anchor(kv_moving, o_theirs, q_theirs)
    o_half, o_came = by_fsdp(o_mine, o_came, started)
    q_half = (q_mine + after(q_came, started).astype(F32)).astype(BF)
    started = anchor(started, o_half, q_half)

    kv_grad = after(kv_far, started).astype(F32) + kv_sum[0]
    key_grad = rotate(kv_grad[0], cos, sin, True).astype(BF)
    value_grad = kv_grad[1].astype(BF)
    grad_both = jnp.concatenate([key_grad, value_grad], axis=0)
    first_part = dot(query_grad, w_q, 0, 1) + dot(grad_both, w_kv, 0, 1)
    grad_first = jnp.sum(first_part * normed_one, axis=0, keepdims=True)
    first_low = first_part.astype(BF)
    first_other = swap(first_low, "tp")
    small_grad = jnp.concatenate([grad_first, grad_second, grad_router], axis=0)
    small_other = swap(small_grad, "tp")
    grad_kv_w = dot(hidden_one, grad_both, 0, 1).astype(BF)
    kv_mine, kv_theirs, kv_came = by_core_halves(grad_kv_w)
    started = anchor(first_low, small_grad, kv_theirs)
    kv_half = (kv_mine + after(kv_came, started).astype(F32)).astype(BF)
    kv_half = jnp.concatenate([q_half, kv_half], axis=2)
    kv_came = lax.all_to_all(kv_half, "fsdp", 0, 0)
    small_grad = small_grad + after(small_other, started)
    small_other = swap(small_grad, "core")
    started = anchor(kv_half, small_grad)

    mixed = mix_step(mix_moving, 0, started)
    mix_other = swap(mixed[half:], "tp")
    o_total, o_came = by_chip(o_came, started)
    small_grad = small_grad + after(small_other, started)
    everyone = ring_gather(small_grad[None], "cx", n_cx, 0)
    started = anchor(mixed, o_total, small_grad)

    first_grad = first_low.astype(F32) + after(first_other, started).astype(F32)
    grad_inputs = branch.astype(F32) + norm_backward(
        first_grad, gain_first, inverse_one, normed_one
    )
    mixture = mixed[:half].astype(F32) + after(mix_other, first_grad).astype(F32)
    out_half = (pick(valid, tp, 2, 0) * (residual + mixture)).astype(BF)
    out_other = swap(out_half, "tp")
    kv_total, kv_came = by_chip(kv_came, started)
    total = jnp.sum(after(everyone, started), axis=0)
    small_mine = jnp.sum(
        lax.all_to_all(total, "fsdp", 1, 0, tiled=True).reshape(n_z, 2 + E, shard), axis=0
    )
    parts = [(expert_sum, k) for k in range(held - first_slot)]
    if by_core:
        others = swap(after(expert_sum, started), "core")
        parts = [(others, k) for k in range(first_slot)] + parts
    grad_output = whole_of(o_came, started).T
    started = anchor(out_half, kv_total)
    grad_down, grad_gate, grad_up = place(order[1 + n_z :], parts)
    grad_kv_w = whole_of(kv_came, started, grad_down)
    grad_q, grad_kv_w = grad_kv_w[:, :q_width], grad_kv_w[:, q_width:]
    out_other = after(out_other, started)
    layer_out = jnp.concatenate(
        [jnp.where(lead, out_half, out_other), jnp.where(lead, out_other, out_half)], axis=0
    )

    return (
        layer_out[None],
        grad_inputs[None],
        small_mine[0],
        grad_q,
        grad_kv_w[:, :kv_width],
        grad_kv_w[:, kv_width:],
        grad_output,
        small_mine[1],
        small_mine[2:].T,
        grad_gate,
        grad_up,
        grad_down,
    )


def solution(mesh):
    n_z, n_ctx, n_tp = mesh.shape["fsdp"], mesh.shape["ctx"], mesh.shape["tp"]
    named = Mesh(
        mesh.devices.reshape(n_z, n_ctx // 2, 2, n_tp), ("fsdp", "cx", "core", "tp")
    )
    ctx = ("cx", "core")
    placed = (
        P("fsdp", ctx, None),
        P("fsdp"),
        P("fsdp", ctx, None),
        P("fsdp", ctx, None),
        P("fsdp", ctx, None),
        P("fsdp"),
        P("fsdp", "tp"),
        P("fsdp", "tp"),
        P("fsdp", "tp"),
        P("tp", "fsdp"),
        P("fsdp"),
        P("fsdp", None),
        P("fsdp", None, "tp"),
        P("fsdp", None, "tp"),
        P("fsdp", "tp", None),
    )
    return jax.shard_map(
        functools.partial(local, (n_z, n_ctx // 2)),
        mesh=named,
        in_specs=placed,
        out_specs=(
            P("fsdp", ctx, None),
            P("fsdp", ctx, None),
            P("fsdp"),
            P("fsdp", "tp"),
            P("fsdp", "tp"),
            P("fsdp", "tp"),
            P("tp", "fsdp"),
            P("fsdp"),
            P("fsdp", None),
            P("fsdp", None, "tp"),
            P("fsdp", None, "tp"),
            P("fsdp", "tp", None),
        ),
        check_vma=False,
    )
```

```python
import functools
import math

import jax
import jax.numpy as jnp
from jax import lax
from jax.experimental import pallas as pl
from jax.experimental.pallas import tpu as pltpu
from jax.sharding import Mesh
from jax.sharding import PartitionSpec as P

HEAD = 64
TOPK = 8
E = 16
CAP = 256
EPSILON = 1e-06
BF = jnp.bfloat16
F32 = jnp.float32
NEG = -1e30
FAR = 1e6


def dot(a, b, ca, cb):
    return lax.dot_general(a, b, (((ca,), (cb,)), ((), ())), preferred_element_type=F32)


def shift(v, axis, n, by=1):
    return lax.ppermute(v, axis, [(i, (i + by) % n) for i in range(n)])


def swap(v, axis):
    return lax.ppermute(v, axis, [(0, 1), (1, 0)])


def pick(v, index, parts, dim):
    size = v.shape[dim] // parts
    return lax.dynamic_slice_in_dim(v, index * size, size, dim)


def put(buffer, v, start, dim):
    return lax.dynamic_update_slice_in_dim(buffer, v, start, dim)


def after(v, *others):
    return lax.optimization_barrier((v,) + others)[0]


def anchor_kernel(in_ref, out_ref):
    out_ref[...] = in_ref[...]


def anchor(*others):
    token = after(jnp.zeros((8, 128), F32), *others)
    return pl.pallas_call(
        anchor_kernel,
        name="anchor",
        out_shape=jax.ShapeDtypeStruct((8, 128), F32),
        cost_estimate=pl.CostEstimate(flops=10**11, transcendentals=0, bytes_accessed=8192),
    )(token)


def direct_reduce(part, axis, n):
    me = lax.axis_index(axis)
    total = part(me)
    for s in range(1, n):
        total = total + shift(part((me + s) % n).astype(BF), axis, n, s).astype(F32)
    return total


def ring_reduce(part, axis, n, *others):
    me = lax.axis_index(axis)
    moving = part((me + n - 1) % n).astype(BF)
    for s in range(2, n):
        moving = (shift(moving, axis, n).astype(F32) + part((me + n - s) % n)).astype(BF)
    moving = shift(moving, axis, n)
    if others:
        moving = after(moving, *others)
    return moving.astype(F32) + part(me)


def core_halves(v, dim):
    core = lax.axis_index("core")
    mine = pick(v, core, 2, dim)
    theirs = pick(v, 1 - core, 2, dim)
    return mine.astype(F32) + swap(theirs.astype(BF), "core").astype(F32)


def core_join(v, dim):
    other = swap(v, "core")
    first = lax.axis_index("core") == 0
    return jnp.concatenate([jnp.where(first, v, other), jnp.where(first, other, v)], axis=dim)


def ring_gather(v, axis, n, dim):
    me = lax.axis_index(axis)
    size = v.shape[dim]
    shape = list(v.shape)
    shape[dim] = size * n
    out = put(jnp.zeros(shape, v.dtype), v, me * size, dim)
    moving = v
    for s in range(1, n):
        moving = shift(moving, axis, n)
        out = put(out, moving, ((me + n - s) % n) * size, dim)
    return out


def ctx_total(v, n_cx):
    half = core_halves(v, 0).astype(BF)
    part = ring_reduce(lambda j: pick(half, j, n_cx, 0).astype(F32), "cx", n_cx).astype(BF)
    return core_join(ring_gather(part, "cx", n_cx, 0), 0)


def normalize(values):
    inverse = lax.rsqrt(jnp.mean(values * values, axis=-1, keepdims=True) + EPSILON)
    return inverse, values * inverse


def norm_backward(grad, gain, inverse, normed):
    scaled = grad * gain
    return inverse * (scaled - normed * jnp.mean(scaled * normed, axis=-1, keepdims=True))


def rotate(v, cos, sin, inverse):
    rows = v.shape[1]
    shaped = v.reshape(-1, 2, HEAD // 2, rows)
    a, b = shaped[:, 0], shaped[:, 1]
    if inverse:
        out = jnp.stack([a * cos + b * sin, b * cos - a * sin], axis=1)
    else:
        out = jnp.stack([a * cos - b * sin, b * cos + a * sin], axis=1)
    return out.reshape(-1, rows)


def keep_plan(routes, order, live):
    rows = routes.shape[0]
    pairs = rows * TOPK
    token, choice = order // TOPK, order % TOPK
    rank = jnp.arange(pairs, dtype=jnp.int32)
    at_token = (jnp.arange(rows, dtype=jnp.int32)[:, None] == token[None, :]).astype(BF)
    at_choice = jnp.arange(TOPK, dtype=jnp.int32)[:, None] == choice[None, :]
    high = jnp.where(at_choice, (rank // 64)[None, :], 0).astype(BF)
    low = jnp.where(at_choice, (rank % 64)[None, :], 0).astype(BF)
    place = dot(at_token, jnp.concatenate([high, low], axis=0), 1, 1)
    place = place[:, :TOPK] * 64.0 + place[:, TOPK:]
    hits = routes[:, :, None] == jnp.arange(E, dtype=jnp.int32)[None, None, :]
    routed = jnp.any(hits, axis=1)
    place_e = jnp.sum(jnp.where(hits, place[:, :, None], 0.0), axis=1)
    place_e = jnp.where(routed & live[:, None], place_e, FAR)
    across = place_e.T
    earlier = jnp.sum((place_e[:, :, None] < across[None, :, :]).astype(F32), axis=0).T
    kept = routed & live[:, None] & (earlier < CAP)
    return routed, kept


def assemble(info_ref, own_ref, got_ref, other_ref, full_ref):
    z, core, cx = info_ref[0], info_ref[1], info_ref[2]
    rows = own_ref.shape[0]
    chips, steps, piece, _ = got_ref.shape
    n_z = steps + 1
    full_ref[pl.ds(pl.multiple_of(z * rows, piece), rows), :] = own_ref[...]
    for k in range(chips):
        chip = (cx + chips - k) % chips
        for s in range(1, n_z):
            start = ((z + n_z - s) % n_z) * rows + chip * 2 * piece
            mine = pl.multiple_of(start + core * piece, piece)
            theirs = pl.multiple_of(start + (1 - core) * piece, piece)
            full_ref[pl.ds(mine, piece), :] = got_ref[k, s - 1]
            full_ref[pl.ds(theirs, piece), :] = other_ref[k, s - 1]


def project_kernel(turned, scale, info_ref, own_ref, got_ref, other_ref, x_ref, cos_ref, sin_ref, out_ref, full_ref):
    assemble(info_ref, own_ref, got_ref, other_ref, full_ref)
    flat = jnp.dot(x_ref[...], full_ref[...], preferred_element_type=F32).T
    cos, sin = cos_ref[...], sin_ref[...]
    quarter = HEAD // 2
    for start in range(0, turned, HEAD):
        a = flat[start : start + quarter, :]
        b = flat[start + quarter : start + HEAD, :]
        out_ref[start : start + quarter, :] = ((a * cos - b * sin).astype(BF) * scale).astype(BF)
        out_ref[start + quarter : start + HEAD, :] = ((b * cos + a * sin).astype(BF) * scale).astype(BF)
    if turned < flat.shape[0]:
        out_ref[turned:, :] = flat[turned:, :].astype(BF)


def project(info, own, got, other, x, cos, sin, turned, scale):
    columns = own.shape[1]
    rows, width = x.shape
    return pl.pallas_call(
        functools.partial(project_kernel, turned, scale),
        name="project",
        grid_spec=pltpu.PrefetchScalarGridSpec(num_scalar_prefetch=1, grid=(1,),
            in_specs=[pl.BlockSpec(v.shape, lambda i, n, k=v.ndim: (0,) * k) for v in (own, got, other, x, cos, sin)],
            out_specs=[
                pl.BlockSpec((columns, rows), lambda i, n: (0, 0)),
                pl.BlockSpec((width, columns), lambda i, n: (0, 0)),
            ],
        ),
        out_shape=[
            jax.ShapeDtypeStruct((columns, rows), BF),
            jax.ShapeDtypeStruct((width, columns), BF),
        ],
        compiler_params=pltpu.CompilerParams(vmem_limit_bytes=40 << 20),
        cost_estimate=pl.CostEstimate(
            flops=2 * rows * width * columns,
            transcendentals=0,
            bytes_accessed=4 * width * columns + 2 * rows * (width + columns),
        ),
    )(info, own, got, other, x, cos, sin)


def assembled(info, own, got, other):
    rows, columns = own.shape
    full = (rows * (got.shape[1] + 1), columns)
    return pl.pallas_call(
        assemble,
        name="assembled",
        grid_spec=pltpu.PrefetchScalarGridSpec(num_scalar_prefetch=1, grid=(1,),
            in_specs=[pl.BlockSpec(v.shape, lambda i, n, k=v.ndim: (0,) * k) for v in (own, got, other)],
            out_specs=pl.BlockSpec(full, lambda i, n: (0, 0)),
        ),
        out_shape=jax.ShapeDtypeStruct(full, BF),
        compiler_params=pltpu.CompilerParams(vmem_limit_bytes=32 << 20),
        cost_estimate=pl.CostEstimate(flops=0, transcendentals=0, bytes_accessed=4 * rows * columns * 4),
    )(info, own, got, other)


def softmax_block(q, k, last, base, first_row, length):
    s = lax.dot_general(k, q, (((0,), (0,)), ((), ())), preferred_element_type=F32)
    if last:
        key = base + lax.broadcasted_iota(jnp.int32, s.shape, 0)
        query = first_row + lax.broadcasted_iota(jnp.int32, s.shape, 1)
        s = jnp.where((key <= query) & (key < length), s, NEG)
    return s


def slot_of(block, ctx, n_ctx):
    n_cx = n_ctx // 2
    steps = (ctx // 2 + n_cx - block // 2) % n_cx
    return ((ctx + block) % 2) * n_cx + steps


def attend_kernel(group, info_ref, q_ref, kv_ref, o_ref, lse_ref):
    count, first_row, length, ctx = info_ref[0], info_ref[1], info_ref[2], info_ref[3]
    rows = q_ref.shape[1]
    n_ctx = kv_ref.shape[0]
    keys = kv_ref.shape[3]
    for h in range(group):
        q = q_ref[h * HEAD : (h + 1) * HEAD, :]

        def step(j, carry, last):
            top, total, acc = carry
            slot = slot_of(j, ctx, n_ctx)
            k = kv_ref[slot, 0]
            v = kv_ref[slot, 1]
            s = softmax_block(q, k, last, j * keys, first_row, length)
            new_top = jnp.maximum(top, jnp.max(s, axis=0, keepdims=True))
            p = jnp.exp(s - new_top)
            fade = jnp.exp(top - new_top)
            total = total * fade + jnp.sum(p, axis=0, keepdims=True)
            acc = acc * fade + jnp.dot(v, p.astype(BF), preferred_element_type=F32)
            return new_top, total, acc

        carry = (
            jnp.full((1, rows), NEG, F32),
            jnp.zeros((1, rows), F32),
            jnp.zeros((HEAD, rows), F32),
        )
        carry = lax.fori_loop(0, count - 1, functools.partial(step, last=False), carry)
        top, total, acc = step(count - 1, carry, True)
        o_ref[h * HEAD : (h + 1) * HEAD, :] = (acc / total).astype(BF)
        lse_ref[0, h : h + 1, :] = top + jnp.log(total)


def attend(q, kv, info, group, start, heads):
    rows = q.shape[1]
    n_ctx, _, depth, keys = kv.shape
    return pl.pallas_call(
        functools.partial(attend_kernel, group),
        name="attend",
        grid_spec=pltpu.PrefetchScalarGridSpec(
            num_scalar_prefetch=1,
            grid=(heads,),
            in_specs=[
                pl.BlockSpec((group * HEAD, rows), lambda g, i: (start + g, 0)),
                pl.BlockSpec((n_ctx, 2, HEAD, keys), lambda g, i: (0, 0, start + g, 0)),
            ],
            out_specs=[
                pl.BlockSpec((group * HEAD, rows), lambda g, i: (g, 0)),
                pl.BlockSpec((1, 8, rows), lambda g, i: (g, 0, 0)),
            ],
        ),
        out_shape=[
            jax.ShapeDtypeStruct((heads * group * HEAD, rows), BF),
            jax.ShapeDtypeStruct((heads, 8, rows), F32),
        ],
        compiler_params=pltpu.CompilerParams(vmem_limit_bytes=48 << 20),
        cost_estimate=pl.CostEstimate(
            flops=4 * heads * group * HEAD * rows * n_ctx * keys,
            transcendentals=heads * group * rows * n_ctx * keys,
            bytes_accessed=2 * q.size + kv.size,
        ),
    )(info, q, kv)


def attend_back_kernel(group, info_ref, q_ref, kv_ref, o_ref, do_ref, lse_ref, dq_ref, dkv_ref):
    count, first_row, length, ctx = info_ref[0], info_ref[1], info_ref[2], info_ref[3]
    n_ctx = kv_ref.shape[0]
    keys = kv_ref.shape[3]
    delta = []
    for h in range(group):
        part = slice(h * HEAD, (h + 1) * HEAD)
        delta.append(
            jnp.sum(do_ref[part, :].astype(F32) * o_ref[part, :].astype(F32), axis=0, keepdims=True)
        )
    dq_ref[...] = jnp.zeros_like(dq_ref)

    def step(j, last):
        slot = slot_of(j, ctx, n_ctx)
        k = kv_ref[slot, 0]
        v = kv_ref[slot, 1]
        dk = jnp.zeros((keys, HEAD), F32)
        dv = jnp.zeros((keys, HEAD), F32)
        for h in range(group):
            part = slice(h * HEAD, (h + 1) * HEAD)
            q = q_ref[part, :]
            do = do_ref[part, :]
            s = softmax_block(q, k, last, j * keys, first_row, length)
            p = jnp.exp(s - lse_ref[0, h : h + 1, :])
            dp = lax.dot_general(v, do, (((0,), (0,)), ((), ())), preferred_element_type=F32)
            ds = (p * (dp - delta[h])).astype(BF)
            pb = p.astype(BF)
            dv += lax.dot_general(pb, do, (((1,), (1,)), ((), ())), preferred_element_type=F32)
            dk += lax.dot_general(ds, q, (((1,), (1,)), ((), ())), preferred_element_type=F32)
            dq_ref[part, :] += jnp.dot(k, ds, preferred_element_type=F32)
        dkv_ref[slot, 0] = dk.T.astype(BF)
        dkv_ref[slot, 1] = dv.T.astype(BF)

    @pl.loop(0, count - 1)
    def _(j):
        step(j, False)

    step(count - 1, True)

    @pl.loop(count, n_ctx)
    def _(j):
        dkv_ref[slot_of(j, ctx, n_ctx)] = jnp.zeros(dkv_ref.shape[1:], BF)


def attend_back(q, kv, o, do, lse, info, group):
    rows = q.shape[1]
    n_ctx, _, depth, keys = kv.shape
    heads = depth // HEAD
    wide = pl.BlockSpec((group * HEAD, rows), lambda g, i: (g, 0))
    blocks = pl.BlockSpec((n_ctx, 2, HEAD, keys), lambda g, i: (0, 0, g, 0))
    return pl.pallas_call(
        functools.partial(attend_back_kernel, group),
        name="attend_back",
        grid_spec=pltpu.PrefetchScalarGridSpec(
            num_scalar_prefetch=1,
            grid=(heads,),
            in_specs=[
                wide,
                blocks,
                wide,
                wide,
                pl.BlockSpec((1, 8, rows), lambda g, i: (g, 0, 0)),
            ],
            out_specs=[wide, blocks],
        ),
        out_shape=[
            jax.ShapeDtypeStruct(q.shape, F32),
            jax.ShapeDtypeStruct(kv.shape, BF),
        ],
        compiler_params=pltpu.CompilerParams(vmem_limit_bytes=48 << 20),
        cost_estimate=pl.CostEstimate(
            flops=10 * q.shape[0] * rows * n_ctx * keys,
            transcendentals=q.shape[0] // HEAD * rows * n_ctx * keys,
            bytes_accessed=10 * q.size + 4 * kv.size,
        ),
    )(info, q, kv, o, do, lse)


def expert_kernel(info_ref, near_in, far_in, near_do, far_do, gate_ref, up_ref, down_ref, *refs):
    near_out, far_out, mix_out, act_out, dg_out, du_out = refs[:6]
    rows_x, rows_do, shares_in, mix_sum, back_sum, shares_out = refs[6:]
    e = pl.program_id(0)
    half, width = near_do.shape[2:]
    rows = 2 * half

    @pl.when(e == 0)
    def _():
        rows_x[:half, :] = near_in[:, :width]
        rows_x[half:, :] = far_in[:, :width]
        rows_do[:half, :] = near_do[0, 0]
        rows_do[half:, :] = far_do[0, 0]
        shares_in[:half, :] = near_in[:, width:].astype(F32)
        shares_in[half:, :] = far_in[:, width:].astype(F32)

    lanes = lax.broadcasted_iota(jnp.int32, (rows, 128), 1)
    x = rows_x[...]
    do = rows_do[...]
    per, _, hidden = gate_ref.shape
    mix = back = share = None
    for i in range(per):
        chosen = info_ref[0] + e * per + i
        gate, up, down = gate_ref[i], up_ref[i], down_ref[i]
        weight = jnp.sum(
            jnp.where((lanes == chosen) | (lanes == chosen + E), shares_in[...], 0.0),
            axis=1,
            keepdims=True,
        )
        g = jnp.dot(x, gate, preferred_element_type=F32)
        u = jnp.dot(x, up, preferred_element_type=F32)
        dact = dot(do, down, 1, 1)
        sig = jax.nn.sigmoid(g)
        silu = g * sig
        act = silu * u
        share_i = jnp.where(lanes == chosen, jnp.sum(act * dact, axis=1, keepdims=True), 0.0)
        dhid = dact * weight
        part = slice(i * hidden, (i + 1) * hidden)
        act_out[:, part] = (act * weight).astype(BF)
        dg_out[:, part] = (dhid * u * (sig * (1.0 + g * (1.0 - sig)))).astype(BF)
        du_out[:, part] = (dhid * silu).astype(BF)
        mix_i = jnp.dot(act_out[:, part], down, preferred_element_type=F32)
        back_i = dot(dg_out[:, part], gate, 1, 1) + dot(du_out[:, part], up, 1, 1)
        mix = mix_i if mix is None else mix + mix_i
        back = back_i if back is None else back + back_i
        share = share_i if share is None else share + share_i

    @pl.when(e == 0)
    def _():
        mix_sum[...] = mix
        back_sum[...] = back
        shares_out[...] = share

    @pl.when(e > 0)
    def _():
        mix_sum[...] += mix
        back_sum[...] += back
        shares_out[...] += share

    @pl.when(e == pl.num_programs(0) - 1)
    def _():
        near_out[:, :width] = back_sum[:half, :].astype(BF)
        near_out[:, width:] = shares_out[:half, :].astype(BF)
        far_out[:, :width] = back_sum[half:, :].astype(BF)
        far_out[:, width:] = shares_out[half:, :].astype(BF)
        mix_out[...] = mix_sum[...].astype(BF)


def experts(info, near, far, do_near, do_far, gate, up, down, weight):
    half, wide = near.shape
    width = do_near.shape[3]
    held, _, hidden = gate.shape
    rows = 2 * half
    whole = lambda shape: pl.BlockSpec(shape, lambda e, i: (0, 0))
    per = 1
    each = lambda shape: pl.BlockSpec((per,) + shape, lambda e, i: (e, 0, 0))
    column = pl.BlockSpec((rows, per * hidden), lambda e, i: (0, e))
    mid = jax.ShapeDtypeStruct((rows, held * hidden), BF)
    message = jax.ShapeDtypeStruct((half, wide), BF)
    return pl.pallas_call(
        expert_kernel,
        name="experts",
        grid_spec=pltpu.PrefetchScalarGridSpec(
            num_scalar_prefetch=1,
            grid=(held // per,),
            in_specs=[
                whole((half, wide)),
                whole((half, wide)),
                pl.BlockSpec((1, 1, half, width), lambda e, i: (i[3], i[4], 0, 0)),
                pl.BlockSpec((1, 1, half, width), lambda e, i: (i[5], i[4], 0, 0)),
                each((width, hidden)),
                each((width, hidden)),
                each((hidden, width)),
            ],
            out_specs=[
                whole((half, wide)),
                whole((half, wide)),
                whole((rows, width)),
                column,
                column,
                column,
            ],
            scratch_shapes=[
                pltpu.VMEM((rows, width), BF),
                pltpu.VMEM((rows, width), BF),
                pltpu.VMEM((rows, 128), F32),
                pltpu.VMEM((rows, width), F32),
                pltpu.VMEM((rows, width), F32),
                pltpu.VMEM((rows, 128), F32),
            ],
        ),
        out_shape=[
            message,
            message,
            jax.ShapeDtypeStruct((rows, width), BF),
            mid,
            mid,
            mid,
        ],
        compiler_params=pltpu.CompilerParams(vmem_limit_bytes=56 << 20),
        cost_estimate=pl.CostEstimate(
            flops=12 * weight * rows * width * held * hidden,
            transcendentals=rows * held * hidden,
            bytes_accessed=6 * held * hidden * width + 16 * rows * width,
        ),
    )(info, near, far, do_near, do_far, gate, up, down)


def expert_grad_kernel(count, info_ref, *refs):
    rows_x, rows_do = refs[: 2 * count], refs[2 * count : 4 * count]
    acts, dgs, dus = (refs[(4 + k) * count : (5 + k) * count] for k in range(3))
    out = refs[-1]
    width = rows_do[0].shape[-1]
    hidden = acts[0].shape[1]
    down = both = None
    for s in range(count):
        do = jnp.concatenate([rows_do[2 * s][0, 0], rows_do[2 * s + 1][0, 0]], axis=0)
        x = jnp.concatenate([rows_x[2 * s][:, :width], rows_x[2 * s + 1][:, :width]], axis=0)
        dgu = jnp.concatenate([dgs[s][...], dus[s][...]], axis=1)
        first, second = dot(acts[s][...], do, 0, 0), dot(dgu, x, 0, 0)
        down = first if down is None else down + first
        both = second if both is None else both + second
    out[0, 0] = down.astype(BF)
    out[0, 1] = both[:hidden].astype(BF)
    out[0, 2] = both[hidden:].astype(BF)


def expert_grads(info, chunks, do_all, acts, dgs, dus, held, start, count):
    n_z = len(acts)
    if n_z > 4:
        total = 0.0
        for b in range(0, n_z, 4):
            part = slice(b, b + 4)
            here = jnp.concatenate([info[:1], info[1 + b : 5 + b], info[1 + n_z :]])
            total = total + expert_grads(
                here,
                chunks[2 * b : 2 * b + 8],
                do_all,
                acts[part],
                dgs[part],
                dus[part],
                held,
                start,
                count,
            ).astype(F32)
        return total.astype(BF)
    size, width = do_all.shape[2:]
    wide = chunks[0].shape[1]
    rows, mid = acts[0].shape
    hidden = mid // held
    at = 1 + n_z + start
    chunk = pl.BlockSpec((size, wide), lambda e, i: (0, 0), pipeline_mode=pl.Buffered(1))
    do_chunk = lambda other, s: pl.BlockSpec(
        (1, 1, size, width),
        lambda e, i: ((1 - i[0]) if other else i[0], i[1 + s], 0, 0),
        pipeline_mode=pl.Buffered(1),
    )
    column = pl.BlockSpec((rows, hidden), lambda e, i: (0, i[at + e]))
    return pl.pallas_call(
        functools.partial(expert_grad_kernel, n_z),
        name="expert_grads",
        grid_spec=pltpu.PrefetchScalarGridSpec(
            num_scalar_prefetch=1,
            grid=(count,),
            in_specs=[chunk for _ in chunks]
            + [do_chunk(other, s) for s in range(n_z) for other in (False, True)]
            + [column] * (3 * n_z),
            out_specs=pl.BlockSpec((1, 3, hidden, width), lambda e, i: (e, 0, 0, 0)),
        ),
        out_shape=jax.ShapeDtypeStruct((count, 3, hidden, width), BF),
        compiler_params=pltpu.CompilerParams(vmem_limit_bytes=58 << 20),
        cost_estimate=pl.CostEstimate(
            flops=60 * n_z * rows * width * hidden * count,
            transcendentals=0,
            bytes_accessed=4 * n_z * rows * (width + hidden * count),
        ),
    )(info, *chunks, *([do_all] * (2 * n_z)), *acts, *dgs, *dus)


def place_kernel(count, info_ref, *refs):
    down, gate, up = refs[count:]
    for i, ref in enumerate(refs[:count]):

        @pl.when(pl.program_id(0) == i)
        def _():
            down[0] = ref[0, 0].astype(F32)
            gate[0] = ref[0, 1].astype(F32).T
            up[0] = ref[0, 2].astype(F32).T


def place(info, parts):
    hidden, width = parts[0][0].shape[2:]
    count = len(parts)
    out = lambda *shape: pl.BlockSpec((1,) + shape, lambda e, i: (i[e], 0, 0))
    return pl.pallas_call(
        functools.partial(place_kernel, count),
        name="place",
        grid_spec=pltpu.PrefetchScalarGridSpec(
            num_scalar_prefetch=1,
            grid=(count,),
            in_specs=[
                pl.BlockSpec((1, 3, hidden, width), lambda e, i, k=k: (k, 0, 0, 0)) for _, k in parts
            ],
            out_specs=[out(hidden, width), out(width, hidden), out(width, hidden)],
        ),
        out_shape=[
            jax.ShapeDtypeStruct((count, hidden, width), F32),
            jax.ShapeDtypeStruct((count, width, hidden), F32),
            jax.ShapeDtypeStruct((count, width, hidden), F32),
        ],
        compiler_params=pltpu.CompilerParams(vmem_limit_bytes=48 << 20),
        cost_estimate=pl.CostEstimate(
            flops=0, transcendentals=0, bytes_accessed=18 * count * hidden * width
        ),
    )(info, *[array for array, _ in parts])


def local(
    sizes,
    tokens,
    lengths,
    routes,
    visit_order,
    cotangent,
    first_gain,
    query_weight,
    key_matrix,
    value_matrix,
    output_weight,
    second_gain,
    router_weight,
    gate_weight,
    up_weight,
    down_weight,
):
    n_z, n_cx = sizes
    n_ctx = 2 * n_cx
    z = lax.axis_index("fsdp")
    cx = lax.axis_index("cx")
    core = lax.axis_index("core")
    tp = lax.axis_index("tp")
    ctx = cx * 2 + core
    rows, width = tokens.shape[1:]
    half = rows // 2
    shard = query_weight.shape[0]
    q_width = query_weight.shape[1]
    kv_width = key_matrix.shape[1]
    group = q_width // kv_width
    held = gate_weight.shape[0]
    hidden = gate_weight.shape[2]
    first_row = ctx * rows
    length = lengths[0]
    positions = first_row + jnp.arange(rows, dtype=jnp.int32)
    live = positions < length
    valid = live.astype(F32)[:, None]

    wide_split = n_cx == 2 and (shard // 4) % 16 == 0

    def bring(own, over_chips):
        piece = pick(own, ctx, n_ctx, 0) if over_chips else pick(own, core, 2, 0)
        return own, [shift(piece, "fsdp", n_z, s) for s in range(1, n_z)]

    def spread(own, got, over_chips):
        got = jnp.stack(got)[None]
        if over_chips:
            got = jnp.concatenate([got, swap(got, "cx")], axis=0)
        return own, got, swap(got, "core")

    kv_own, kv_got = bring(jnp.concatenate([key_matrix, value_matrix], axis=1), False)

    small = jnp.concatenate([first_gain[None], second_gain[None], router_weight.T], axis=0)
    small_full = lax.all_to_all(jnp.broadcast_to(small[None], (n_z, 2 + E, shard)), "fsdp", 0, 0)
    small_full = jnp.transpose(small_full, (1, 0, 2)).reshape(2 + E, width)
    gain_first = small_full[0:1].astype(F32)
    gain_second = small_full[1:2].astype(F32)
    router = small_full[2:]

    grad_half = (pick(cotangent[0], tp, 2, 0).astype(F32) * pick(valid, tp, 2, 0)).astype(BF)
    grad_other = swap(grad_half, "tp")

    kv_pieces = spread(kv_own, kv_got, False)
    q_own, q_got = bring(after(query_weight, *kv_got), wide_split)
    started = anchor(*kv_got)
    kv_pieces = (kv_own, kv_pieces[1], after(kv_pieces[2], started))
    here = jnp.stack([z, core, cx]).astype(jnp.int32)

    routed, kept = keep_plan(routes[0], visit_order[0, 0], live)

    inputs = tokens[0].astype(F32)
    inverse_one, normed_one = normalize(inputs)
    hidden_one = after((normed_one * gain_first).astype(BF), grad_other)
    frequency = jnp.exp(
        jnp.arange(HEAD // 2, dtype=F32) * (-2.0 * math.log(10000.0) / HEAD)
    )
    angles = frequency[:, None] * positions.astype(F32)[None, :]
    cos, sin = jnp.cos(angles), jnp.sin(angles)
    scale = HEAD**-0.5
    kv_mine, w_kv = project(here, *kv_pieces, hidden_one, cos, sin, kv_width, 1.0)
    kv_mine = kv_mine.reshape(1, 2, kv_width, rows)
    near_kv = [kv_mine]
    for s in range(1, n_cx):
        near_kv.append(shift(near_kv[-1], "cx", n_cx))
    near_kv = jnp.concatenate([near_kv[0]] + [after(v, anchor(kv_mine)) for v in near_kv[1:]], axis=0)
    started = anchor(kv_mine)
    q_got = [after(v, started) for v in q_got]
    q_pieces = spread(q_own, q_got, wide_split)
    o_own, o_got = bring(after(output_weight.T, *q_got), wide_split)
    grad_all = lax.all_gather(after(grad_half, *q_got), ("tp", "fsdp"))
    grad_all = grad_all.reshape(2, n_z, half, width)
    query, w_q = project(here, *q_pieces, hidden_one, cos, sin, q_width, scale)
    kv = jnp.concatenate([near_kv, swap(near_kv, "core")], axis=0)
    count = jnp.minimum(ctx + 1, (length + rows - 1) // rows)
    info = jnp.stack([count, first_row, length, ctx])
    kv_heads = kv_width // HEAD
    split = [(0, kv_heads // 2), (kv_heads // 2, kv_heads - kv_heads // 2)]
    early, early_lse = attend(after(query, grad_other), kv, info, group, *split[0])
    o_pieces = spread(o_own, [after(v, early) for v in o_got], wide_split)
    later, later_lse = attend(after(query, early), kv, info, group, *split[1])
    attended = jnp.concatenate([early, later], axis=0)
    lse = jnp.concatenate([early_lse, later_lse], axis=0)
    o_full = assembled(here, *[after(v, later) for v in o_pieces])

    far = dot(pick(attended, 1 - tp, 2, 1), o_full, 0, 1).astype(BF)
    near = dot(pick(attended, tp, 2, 1), o_full, 0, 1)
    residual = pick(tokens[0], tp, 2, 0).astype(F32) + near + swap(far, "tp").astype(F32)
    inverse_two, normed_two = normalize(residual)
    hidden_two = (normed_two * gain_second).astype(BF)
    logits = dot(hidden_two, router, 1, 1)
    routed_half = pick(routed, tp, 2, 0)
    kept_half = pick(kept, tp, 2, 0).astype(F32)
    masked = jnp.where(routed_half, logits, NEG)
    raised = jnp.where(
        routed_half, jnp.exp(masked - jnp.max(masked, axis=1, keepdims=True)), 0.0
    )
    gates = raised / jnp.sum(raised, axis=1, keepdims=True)
    weights = gates * kept_half

    high = weights.astype(BF)
    low = (weights - high.astype(F32)).astype(BF)
    message = jnp.concatenate(
        [hidden_two, high, low, jnp.zeros((half, 128 - 2 * E), BF)], axis=1
    )
    blocks = [(z + n_z - s) % n_z for s in range(n_z)]
    near = [message]
    far = [swap(message, "tp")]
    coming = shift(message, "fsdp", n_z)
    done, moving, joined = [], None, ()
    for s in range(n_z):
        first = near[s]
        if s + 1 < n_z:
            near.append(after(coming, *[d[0] for d in done[-1:]]))
            far.append(swap(near[-1], "tp"))
            first = after(first, near[-1])
            if s + 2 < n_z:
                coming = shift(near[-1], "fsdp", n_z)
        first = after(first, *joined)
        if s:
            info_s = [z * held, tp, blocks[s], tp, blocks[s], 1 - tp]
            rows_do = (grad_all, grad_all)
        else:
            info_s = [z * held, tp, blocks[s], 0, 0, 0]
            rows_do = (grad_half[None, None], grad_other[None, None])
        done.append(
            experts(
                jnp.stack([jnp.asarray(v, jnp.int32) for v in info_s]),
                first,
                far[s],
                *rows_do,
                gate_weight,
                up_weight,
                down_weight,
                10 if s else 1,
            )
        )
        if s > 1:
            part = done[s - 1][0].astype(F32) + swap(done[s - 1][1], "tp").astype(F32)
            if s > 2:
                part = shift(moving, "fsdp", n_z).astype(F32) + part
            moving = part.astype(BF)
            joined = (moving,)
    last = swap(done[-1][1], "tp")
    by_core = held % 2 == 0
    first_slot = held // 2 if by_core else 0
    slots = [((1 - core) * first_slot + k) % held for k in range(first_slot)]
    slots += [core * first_slot + k for k in range(held - first_slot)]
    order = jnp.stack([jnp.asarray(v, jnp.int32) for v in [tp] + blocks + slots])
    grad_args = (
        [v for s in range(n_z) for v in (near[s], far[s])],
        grad_all,
        [done[s][3] for s in range(n_z)],
        [done[s][4] for s in range(n_z)],
        [done[s][5] for s in range(n_z)],
        held,
    )
    theirs = expert_grads(after(order, moving), *grad_args, 0, first_slot) if by_core else None
    mix_moving = shift(done[1][2], "fsdp", n_z)
    part = done[-1][0].astype(F32) + after(last, theirs if by_core else moving).astype(F32)
    moving = (shift(moving, "fsdp", n_z).astype(F32) + part).astype(BF)
    own = done[0][0].astype(F32) + swap(after(done[0][1], last), "tp").astype(F32)
    mine = expert_grads(after(order, moving), *grad_args, first_slot, held - first_slot)
    back = shift(moving, "fsdp", n_z)

    if by_core:
        expert_half = mine.astype(F32) + after(swap(theirs, "core"), mine).astype(F32)
        expert_half = expert_half.astype(BF)
        expert_sum = lax.psum(expert_half, "cx")
        back, own = after(back, expert_half), after(own, expert_half)
    else:
        expert_sum = lax.psum(mine, ("cx", "core"))
    back = back.astype(F32) + own
    hidden_grad = back[:, :width]
    gate_grad = back[:, width : width + E] * kept_half

    logit_grad = (
        gates * (gate_grad - jnp.sum(gates * gate_grad, axis=1, keepdims=True))
    ).astype(BF)
    hidden_grad = hidden_grad + dot(logit_grad, router, 1, 0)
    grad_router = dot(logit_grad, hidden_two, 0, 0)
    grad_second = jnp.sum(hidden_grad * normed_two, axis=0, keepdims=True)
    branch_half = (
        grad_half.astype(F32) + norm_backward(hidden_grad, gain_second, inverse_two, normed_two)
    ).astype(BF)
    lead = tp == 0
    branch_other = swap(branch_half, "tp")
    branch = jnp.concatenate(
        [jnp.where(lead, branch_half, branch_other), jnp.where(lead, branch_other, branch_half)],
        axis=0,
    )

    attended_grad = dot(o_full, branch, 0, 1).astype(BF)
    grad_output = dot(branch, attended, 0, 1).astype(BF)
    attended_grad = after(attended_grad, grad_output)

    grad_query_rot, grad_kv = attend_back(
        query, kv, attended, attended_grad, lse, info, group
    )
    def mix_step(arrived, s, *others):
        return (after(arrived, *others).astype(F32) + done[s][2].astype(F32)).astype(BF)

    for s in range(2, n_z):
        mix_moving = mix_step(mix_moving, s, *((theirs,) if s == 2 and by_core else (grad_kv,)))
        mix_moving = shift(mix_moving, "fsdp", n_z)
    kv_sum = grad_kv[:n_cx].astype(F32) + swap(grad_kv[n_cx:], "core").astype(F32)
    kv_moving = kv_sum[1].astype(BF)
    for s in range(2, n_cx):
        kv_moving = (shift(kv_moving, "cx", n_cx).astype(F32) + kv_sum[s]).astype(BF)
    kv_far = shift(kv_moving, "cx", n_cx)
    query_grad = (rotate(grad_query_rot, cos, sin, True) * scale).astype(BF)

    def by_core_halves(v):
        blocks = v.reshape(n_z, v.shape[0] // n_z, v.shape[1])
        theirs = pick(blocks, 1 - core, 2, 1)
        return pick(blocks, core, 2, 1).astype(F32), theirs, swap(theirs, "core")

    def by_fsdp(mine, came, *others):
        half = (mine + after(came, *others).astype(F32)).astype(BF)
        return half, lax.all_to_all(half, "fsdp", 0, 0)

    def by_chip(came, *others):
        total = jnp.sum(after(came, *others).astype(F32), axis=0).astype(BF)
        return total, ring_gather(total[None], "cx", n_cx, 0)

    def whole_of(came, *others):
        total = jnp.sum(after(came, *others).astype(F32), axis=0).astype(BF)
        return core_join(total, 0).astype(F32)

    grad_q = dot(hidden_one, query_grad, 0, 1).astype(BF)
    o_mine, o_theirs, o_came = by_core_halves(grad_output)
    q_mine, q_theirs, q_came = by_core_halves(grad_q)
    started = anchor(kv_moving, o_theirs, q_theirs)
    o_half, o_came = by_fsdp(o_mine, o_came, started)
    q_half = (q_mine + after(q_came, started).astype(F32)).astype(BF)
    started = anchor(started, o_half, q_half)

    kv_grad = after(kv_far, started).astype(F32) + kv_sum[0]
    key_grad = rotate(kv_grad[0], cos, sin, True).astype(BF)
    value_grad = kv_grad[1].astype(BF)
    grad_both = jnp.concatenate([key_grad, value_grad], axis=0)
    first_part = dot(query_grad, w_q, 0, 1) + dot(grad_both, w_kv, 0, 1)
    grad_first = jnp.sum(first_part * normed_one, axis=0, keepdims=True)
    first_low = first_part.astype(BF)
    first_other = swap(first_low, "tp")
    small_grad = jnp.concatenate([grad_first, grad_second, grad_router], axis=0)
    small_other = swap(small_grad, "tp")
    grad_kv_w = dot(hidden_one, grad_both, 0, 1).astype(BF)
    kv_mine, kv_theirs, kv_came = by_core_halves(grad_kv_w)
    started = anchor(first_low, small_grad, kv_theirs)
    kv_half = (kv_mine + after(kv_came, started).astype(F32)).astype(BF)
    kv_half = jnp.concatenate([q_half, kv_half], axis=2)
    kv_came = lax.all_to_all(kv_half, "fsdp", 0, 0)
    small_grad = small_grad + after(small_other, started)
    small_other = swap(small_grad, "core")
    started = anchor(kv_half, small_grad)

    mixed = mix_step(mix_moving, 0, started)
    mix_other = swap(mixed[half:], "tp")
    o_total, o_came = by_chip(o_came, started)
    small_grad = small_grad + after(small_other, started)
    everyone = ring_gather(small_grad[None], "cx", n_cx, 0)
    started = anchor(mixed, o_total, small_grad)

    first_grad = first_low.astype(F32) + after(first_other, started).astype(F32)
    grad_inputs = branch.astype(F32) + norm_backward(
        first_grad, gain_first, inverse_one, normed_one
    )
    mixture = mixed[:half].astype(F32) + after(mix_other, first_grad).astype(F32)
    out_half = (pick(valid, tp, 2, 0) * (residual + mixture)).astype(BF)
    out_other = swap(out_half, "tp")
    kv_total, kv_came = by_chip(kv_came, started)
    total = jnp.sum(after(everyone, started), axis=0)
    small_mine = pick(total, z, n_z, 1)
    for s in range(1, n_z):
        small_mine = small_mine + shift(pick(total, (z + s) % n_z, n_z, 1), "fsdp", n_z, s)
    parts = [(expert_sum, k) for k in range(held - first_slot)]
    if by_core:
        others = swap(after(expert_sum, started), "core")
        parts = [(others, k) for k in range(first_slot)] + parts
    grad_output = whole_of(o_came, started).T
    started = anchor(out_half, kv_total)
    grad_down, grad_gate, grad_up = place(order[1 + n_z :], parts)
    grad_kv_w = whole_of(kv_came, started, grad_down)
    grad_q, grad_kv_w = grad_kv_w[:, :q_width], grad_kv_w[:, q_width:]
    out_other = after(out_other, started)
    layer_out = jnp.concatenate(
        [jnp.where(lead, out_half, out_other), jnp.where(lead, out_other, out_half)], axis=0
    )

    return (
        layer_out[None],
        grad_inputs[None],
        small_mine[0],
        grad_q,
        grad_kv_w[:, :kv_width],
        grad_kv_w[:, kv_width:],
        grad_output,
        small_mine[1],
        small_mine[2:].T,
        grad_gate,
        grad_up,
        grad_down,
    )


def solution(mesh):
    n_z, n_ctx, n_tp = mesh.shape["fsdp"], mesh.shape["ctx"], mesh.shape["tp"]
    named = Mesh(
        mesh.devices.reshape(n_z, n_ctx // 2, 2, n_tp), ("fsdp", "cx", "core", "tp")
    )
    ctx = ("cx", "core")
    placed = (
        P("fsdp", ctx, None),
        P("fsdp"),
        P("fsdp", ctx, None),
        P("fsdp", ctx, None),
        P("fsdp", ctx, None),
        P("fsdp"),
        P("fsdp", "tp"),
        P("fsdp", "tp"),
        P("fsdp", "tp"),
        P("tp", "fsdp"),
        P("fsdp"),
        P("fsdp", None),
        P("fsdp", None, "tp"),
        P("fsdp", None, "tp"),
        P("fsdp", "tp", None),
    )
    return jax.shard_map(
        functools.partial(local, (n_z, n_ctx // 2)),
        mesh=named,
        in_specs=placed,
        out_specs=(
            P("fsdp", ctx, None),
            P("fsdp", ctx, None),
            P("fsdp"),
            P("fsdp", "tp"),
            P("fsdp", "tp"),
            P("fsdp", "tp"),
            P("tp", "fsdp"),
            P("fsdp"),
            P("fsdp", None),
            P("fsdp", None, "tp"),
            P("fsdp", None, "tp"),
            P("fsdp", "tp", None),
        ),
        check_vma=False,
    )
```
